32 devices in a mesh: seq: 4 (over z), dp: 8 (over y, x, core).
Axes of the slice: x: 2, y: 2, z: 4, core: 2. Of those that a mesh axis runs over, the one named last changes fastest.
Arguments:
- tokens: bfloat16 [16, 512, 1536], P('dp', 'seq'), may hold values from -6 to 6
- positions: int32 [16, 512], P('dp', 'seq'), may hold values from 0 to 511, as said below
- out_grad: bfloat16 [16, 512, 1536], P('dp', 'seq'), may hold values from -6 to 6
- w_query: bfloat16 [1536, 1536], P(('seq', 'dp')), may hold values from -0.15625 to 0.15625
- w_key: bfloat16 [1536, 768], P(('seq', 'dp')), may hold values from -0.15625 to 0.15625
- w_value: bfloat16 [1536, 768], P(('seq', 'dp')), may hold values from -0.15625 to 0.15625
- w_output: bfloat16 [1536, 1536], P(('seq', 'dp')), may hold values from -2.5 to 2.5
- gain_attn: bfloat16 [1536], P(('seq', 'dp')), may hold values from 0.25 to 1.75
- gain_ffn: bfloat16 [1536], P(('seq', 'dp')), may hold values from 0.25 to 1.75
- w_gate: bfloat16 [4096, 1536], P(('seq', 'dp')), may hold values from -0.15625 to 0.15625
- w_up: bfloat16 [4096, 1536], P(('seq', 'dp')), may hold values from -0.15625 to 0.15625
- w_down: bfloat16 [4096, 1536], P(('seq', 'dp')), may hold values from -0.09375 to 0.09375
Outputs:
- layer_out: bfloat16 [16, 512, 1536], P('dp', 'seq')
- in_grad: bfloat16 [16, 512, 1536], P('dp', 'seq')
- grad_query: float32 [1536, 1536], P(('seq', 'dp'))
- grad_key: float32 [1536, 768], P(('seq', 'dp'))
- grad_value: float32 [1536, 768], P(('seq', 'dp'))
- grad_output: float32 [1536, 1536], P(('seq', 'dp'))
- grad_gain_attn: float32 [1536], P(('seq', 'dp'))
- grad_gain_ffn: float32 [1536], P(('seq', 'dp'))
- grad_gate: float32 [4096, 1536], P(('seq', 'dp'))
- grad_up: float32 [4096, 1536], P(('seq', 'dp'))
- grad_down: float32 [4096, 1536], P(('seq', 'dp'))
The draws below stay inside these ranges and needn't reach their ends.
Inputs may be any that keep to these rules, and one draw needn't show every extreme that they name: Within a sequence the positions rise by one from token to token and return to 0 where a new document begins; every sequence's first token has position 0.
All inputs are finite; a program needn't handle non-finite values.
Results may differ from the reference program's by a relative error of at most 0.014.
Values may be sent and summed in bfloat16 or wider, within the bound.
No kernel may reach another device: no remote copies, remote signals or barrier semaphores. Data moves between devices by JAX's collectives and lax.ppermute only.
A program may use at most 256 MiB of HBM per device.

```python
import jax
import jax.numpy as jnp
from jax import lax

D = 1536
HEADS = 16
KV_HEADS = 8
HEAD = 96
FF = 4096
LEN = 512
SEQS = 16


def draw_positions(key, part):
    places = jnp.arange(LEN, dtype=jnp.int32)[None, :]
    series = jnp.arange(SEQS, dtype=jnp.int32)[:, None]
    marks = jax.random.randint(key, (SEQS, LEN), 0, max(LEN // 4, 2)) == 0
    marks = marks & (series > 0) | (places == 0)
    starts = jnp.where(marks, places, 0)
    return places - lax.cummax(starts, axis=1)


def shard_levels(stream_key, dims, cuts, low, top_value):
    loudness, own = 1.0, jax.random.fold_in(stream_key, 6)
    for dim, shards_of in cuts:
        steps = jnp.exp(jax.random.uniform(jax.random.fold_in(own, dim), (shards_of,), jnp.float32, low / len(cuts), top_value / len(cuts)))
        loudness = loudness * jnp.repeat(steps, dims[dim] // shards_of).reshape([-1 if axis == dim else 1 for axis in range(len(dims))])
    return loudness


def noise(rng, extent, deviation, limit, split=(), kind=jnp.bfloat16):
    values = jax.random.normal(rng, extent, jnp.float32) * deviation
    if len(split) > 0:
        values = shard_levels(rng, extent, split, -0.22, 0.18) * values
    return jnp.clip(values, min=-limit, max=limit).astype(kind)


def setup_inputs(seed: int = 0) -> dict:
    key_of = jax.random.split(jax.random.key(seed), 13)
    return {
        "tokens": noise(key_of[0], (SEQS, LEN, D), 1.0, 6.0, ((0, 8), (1, 4))),
        "positions": draw_positions(jax.random.fold_in(key_of[12], 71), 0),
        "out_grad": noise(key_of[2], (SEQS, LEN, D), 1.0, 6.0, ((0, 8), (1, 4))),
        "w_query": noise(key_of[3], (D, HEADS * HEAD), D ** -0.5, 0.15625, ((0, 32),)),
        "w_key": noise(key_of[4], (D, KV_HEADS * HEAD), D ** -0.5, 0.15625, ((0, 32),)),
        "w_value": noise(key_of[5], (D, KV_HEADS * HEAD), D ** -0.5, 0.15625, ((0, 32),)),
        "w_output": noise(key_of[6], (HEADS * HEAD, D), (max(D // 256, 1)) ** -0.5, 2.5, ((0, 32),)),
        "gain_attn": jnp.clip(1.0 + 0.15 * jax.random.normal(key_of[7], (D,), jnp.float32), 0.25, 1.75).astype(jnp.bfloat16),
        "gain_ffn": jnp.clip(1.0 + 0.15 * jax.random.normal(key_of[8], (D,), jnp.float32), 0.25, 1.75).astype(jnp.bfloat16),
        "w_gate": noise(key_of[9], (FF, D), D ** -0.5, 0.15625, ((0, 32),)),
        "w_up": noise(key_of[10], (FF, D), D ** -0.5, 0.15625, ((0, 32),)),
        "w_down": noise(key_of[11], (FF, D), FF ** -0.5, 0.09375, ((0, 32),)),
    }


EPS = 1e-05
THETA = 100000.0
NEG = -1e+30
HIGH = lax.Precision.HIGHEST

@jax.custom_vjp
def low(v):
    return lax.optimization_barrier(v.astype(jnp.bfloat16)).astype(jnp.float32)

@jax.custom_vjp
def low_back(v):
    return v

def low_keep(v):
    return (low(v), None)

def low_pass(kept, grad):
    return (grad,)

def back_keep(v):
    return (v, None)

def back_low(kept, grad):
    return (low(grad),)
low.defvjp(low_keep, low_pass)
low_back.defvjp(back_keep, back_low)

def norm_rows(values, gain):
    return values * lax.rsqrt(lax.optimization_barrier(jnp.mean(values * values, axis=-1, keepdims=True)) + EPS) * gain

def rotate(values, cosine, sine):
    half = values.shape[-1] // 2
    turned = jnp.concatenate([-values[..., half:], values[..., :half]], axis=-1)
    return values * cosine[:, None, :] + turned * sine[:, None, :]

def angle_tables(places):
    offsets = jnp.arange(0, HEAD, 2, dtype=jnp.float32)
    inverse = THETA ** (-offsets / HEAD)
    angles = places.astype(jnp.float32)[:, None] * inverse[None, :]
    angles = jnp.concatenate([angles, angles], axis=-1)
    return (jnp.cos(angles), jnp.sin(angles))

def attend_head(queries, keys_head, values_head):
    width = keys_head.shape[0]
    scores = jnp.einsum('gqd,kd->gqk', queries, keys_head, precision=HIGH) * HEAD ** (-0.5)
    scores = low_back(scores)
    allowed = jnp.arange(width)[None, :] <= jnp.arange(width)[:, None]
    scores = jnp.where(allowed[None], scores, NEG)
    probs = jax.nn.softmax(scores, axis=-1)
    return jnp.einsum('gqk,kd->gqd', low(probs), values_head, precision=HIGH)

def layer(inputs, cosine, sine, w_query, w_key, w_value, w_output, gain_attn, gain_ffn, w_gate, w_up, w_down):
    length = inputs.shape[0]
    group = HEADS // KV_HEADS
    normed = low(norm_rows(inputs, gain_attn))
    query_raw = low_back(jnp.dot(normed, w_query, precision=HIGH))
    key_raw = low_back(jnp.dot(normed, w_key, precision=HIGH))
    values = low(low_back(jnp.dot(normed, w_value, precision=HIGH)))
    queries = low(rotate(query_raw.reshape(length, HEADS, HEAD), cosine, sine))
    keys = low(rotate(key_raw.reshape(length, KV_HEADS, HEAD), cosine, sine))
    query_heads = queries.reshape(length, KV_HEADS, group, HEAD).transpose(1, 2, 0, 3)
    key_heads = keys.transpose(1, 0, 2)
    value_heads = values.reshape(length, KV_HEADS, HEAD).transpose(1, 0, 2)
    block = jax.checkpoint(attend_head)
    mixed = lax.map(lambda item: block(item[0], item[1], item[2]), (query_heads, key_heads, value_heads))
    mixed = mixed.transpose(2, 0, 1, 3).reshape(length, HEADS * HEAD)
    mixed = low(low_back(mixed))
    first_sum = inputs + low_back(jnp.dot(mixed, w_output, precision=HIGH))
    second = low(norm_rows(first_sum, gain_ffn))
    gate_value = low_back(jnp.dot(second, w_gate.T, precision=HIGH))
    up_value = low_back(jnp.dot(second, w_up.T, precision=HIGH))
    hidden = low(jax.nn.silu(gate_value) * up_value)
    return first_sum + jnp.dot(hidden, w_down, precision=HIGH)

def reference(tokens, positions, out_grad, w_query, w_key, w_value, w_output, gain_attn, gain_ffn, w_gate, w_up, w_down):
    weights = tuple((matrix.astype(jnp.float32) for matrix in (w_query, w_key, w_value, w_output, gain_attn, gain_ffn, w_gate, w_up, w_down)))

    def one_sequence(sums, item):
        inputs, places, grad = item
        cosine, sine = angle_tables(places)

        def forward(values, *params):
            return layer(values, cosine, sine, *params)
        result, pull = jax.vjp(forward, inputs.astype(jnp.float32), *weights)
        grads = pull(grad.astype(jnp.float32))
        sums = tuple((total + extra for total, extra in zip(sums, grads[1:])))
        return (sums, (result.astype(jnp.bfloat16), grads[0].astype(jnp.bfloat16)))
    start = tuple((jnp.zeros_like(matrix) for matrix in weights))
    sums, outputs = lax.scan(one_sequence, start, (tokens, positions, out_grad))
    return (outputs[0], outputs[1], sums[0], sums[1], sums[2], sums[3], sums[4], sums[5], sums[6], sums[7], sums[8])
```

```python
import jax
import jax.numpy as jnp
from jax import lax
from jax.sharding import PartitionSpec as P

HEADS = 16
KV_HEADS = 8
HEAD = 96
GROUP = HEADS // KV_HEADS

EPS = 1e-05
THETA = 100000.0
NEG = -1e30
BF = jnp.bfloat16
F32 = jnp.float32


def inverse_rms(values):
    return lax.rsqrt(jnp.mean(values * values, axis=-1, keepdims=True) + EPS)


def rotate(values, cosine, sine):
    half = values.shape[-1] // 2
    turned = jnp.concatenate([-values[..., half:], values[..., :half]], axis=-1)
    return values * cosine[:, None, :] + turned * sine[:, None, :]


def angle_tables(places):
    offsets = jnp.arange(0, HEAD, 2, dtype=F32)
    inverse = THETA ** (-offsets / HEAD)
    angles = places.astype(F32)[:, None] * inverse[None, :]
    angles = jnp.concatenate([angles, angles], axis=-1)
    return (jnp.cos(angles), jnp.sin(angles))


def mm(left, right):
    return jnp.dot(left, right, preferred_element_type=F32)


def mm_t(left, right):
    return lax.dot_general(left, right, (((1,), (1,)), ((), ())), preferred_element_type=F32)


def t_mm(left, right):
    return lax.dot_general(left, right, (((0,), (0,)), ((), ())), preferred_element_type=F32)


class Moves:
    def __init__(self):
        self.Z = lax.axis_size("seq")
        self.DP = lax.axis_size("dp")
        self.Q = self.DP // 4
        self.zi = lax.axis_index("seq")
        place = lax.axis_index("dp")
        self.qi = place // 4
        self.xi = (place // 2) % 2
        self.ci = place % 2
        self.index = {"z": self.zi, "q": self.qi, "x": self.xi, "c": self.ci}
        self.size = {"z": self.Z, "q": self.Q, "x": 2, "c": 2}

    def step(self, axis, value):
        if axis == "c":
            return lax.ppermute(value, "dp", [(i, i ^ 1) for i in range(self.DP)])
        if axis == "x":
            return lax.ppermute(value, "dp", [(i, i ^ 2) for i in range(self.DP)])
        if axis == "q":
            return lax.ppermute(
                value, "dp", [(i, i % 4 + 4 * ((i // 4 + 1) % self.Q)) for i in range(self.DP)]
            )
        return lax.ppermute(value, "seq", [(i, (i + 1) % self.Z) for i in range(self.Z)])

    def up(self, value):
        return lax.ppermute(value, "seq", [(i, i + 1) for i in range(self.Z - 1)])

    def down(self, value):
        return lax.ppermute(value, "seq", [(i + 1, i) for i in range(self.Z - 1)])

    def gather(self, value, name, position, step=None):
        size, index = self.size[name], self.index[name]
        step = step or (lambda v: self.step(name, v))
        blocks = [value]
        for _ in range(size - 1):
            blocks.append(step(blocks[-1]))
        if size == 2:
            return jnp.where(
                index == 0, jnp.stack(blocks, axis=position), jnp.stack(blocks[::-1], axis=position)
            )
        out = jnp.zeros(value.shape[:position] + (size,) + value.shape[position:], value.dtype)
        for k, block in enumerate(blocks):
            out = lax.dynamic_update_slice_in_dim(
                out, jnp.expand_dims(block, position), (index - k) % size, axis=position
            )
        return out

    def scatter(self, value, name, position, step=None, sign=1):
        size, index = self.size[name], self.index[name]
        step = step or (lambda v: self.step(name, v))

        def take(k):
            return lax.dynamic_index_in_dim(
                value, (index - sign * k) % size, axis=position, keepdims=False
            )

        received = None
        for k in range(1, size):
            part = take(k)
            if received is not None:
                part = part + received
            received = step(part.astype(BF)).astype(F32)
        return take(0) + received


def head_layout(values, seqs, rows):
    return (
        values.reshape(seqs, rows, KV_HEADS, GROUP, HEAD)
        .transpose(2, 0, 3, 1, 4)
        .reshape(KV_HEADS, seqs, GROUP * rows, HEAD)
    )


def flat_layout(values, seqs, rows):
    return (
        values.reshape(KV_HEADS, seqs, GROUP, rows, HEAD)
        .transpose(1, 3, 0, 2, 4)
        .reshape(seqs * rows, HEADS * HEAD)
    )


def key_layout(values, seqs, wide):
    return values.reshape(seqs, wide, KV_HEADS, HEAD).transpose(2, 0, 1, 3)


def key_flat(values, seqs, wide):
    return values.transpose(1, 2, 0, 3).reshape(seqs * wide, KV_HEADS * HEAD)


def allowed_mask(rows, width, first):
    query_place = first + jnp.arange(GROUP * rows, dtype=jnp.int32) % rows
    key_place = jnp.arange(width, dtype=jnp.int32)
    return key_place[None, :] <= query_place[:, None]


def attend_forward(query_heads, key_heads, value_heads, allowed):
    def one(item):
        queries, keys, values = item
        raw = jnp.einsum("sqd,skd->sqk", queries, keys, preferred_element_type=F32) * HEAD ** (-0.5)
        scores = jnp.where(allowed, raw, NEG)
        top = jnp.max(scores, axis=-1, keepdims=True)
        weights = jnp.exp(scores - top)
        total = jnp.sum(weights, axis=-1, keepdims=True)
        probs = (weights / total).astype(BF)
        mixed = jnp.einsum("sqk,skd->sqd", probs, values, preferred_element_type=F32)
        return (mixed.astype(BF), top[..., 0] + jnp.log(total[..., 0]))

    return lax.map(one, (query_heads, key_heads, value_heads))


def attend_backward(query_heads, key_heads, value_heads, mixed_grads, log_totals, allowed):
    scale = HEAD ** (-0.5)

    def one(item):
        queries, keys, values, mixed_grad, norm_log = item
        raw = jnp.einsum("sqd,skd->sqk", queries, keys, preferred_element_type=F32) * scale
        scores = jnp.where(allowed, raw, NEG)
        probs = jnp.exp(scores - norm_log[..., None])
        prob_grad = jnp.einsum("sqd,skd->sqk", mixed_grad, values, preferred_element_type=F32)
        centre = jnp.sum(probs * prob_grad, axis=-1, keepdims=True)
        score_grad = (probs * (prob_grad - centre)).astype(BF)
        query_grad = jnp.einsum("sqk,skd->sqd", score_grad, keys, preferred_element_type=F32) * scale
        key_grad = jnp.einsum("sqk,sqd->skd", score_grad, queries, preferred_element_type=F32) * scale
        value_grad = jnp.einsum(
            "sqk,sqd->skd", probs.astype(BF), mixed_grad, preferred_element_type=F32
        )
        return (query_grad, key_grad, value_grad)

    return lax.map(one, (query_heads, key_heads, value_heads, mixed_grads, log_totals))


def per_device(
    tokens,
    positions,
    out_grad,
    w_query,
    w_key,
    w_value,
    w_output,
    gain_attn,
    gain_ffn,
    w_gate,
    w_up,
    w_down,
):
    move = Moves()
    Z, Q = move.Z, move.Q
    seqs, rows, width = tokens.shape
    wide = rows * Z
    own_rows = seqs * rows
    query_width = HEADS * HEAD
    pair_width = KV_HEADS * HEAD
    share = w_query.shape[0]
    units = w_gate.shape[0]
    allowed = allowed_mask(rows, wide, move.zi * rows)

    gains = jnp.pad(jnp.stack([gain_attn, gain_ffn]), ((0, 0), (0, 128 - share)))
    for position, name in enumerate("zqxc"):
        gains = move.gather(gains, name, position)
    gains = gains[..., :share].transpose(4, 0, 1, 2, 3, 5).reshape(2, width).astype(F32)
    attn_scale, ffn_scale = gains[0:1], gains[1:2]

    places_all = move.gather(positions, "z", 1, move.up).reshape(seqs * wide)
    tokens_all = move.gather(tokens, "z", 1, move.up).reshape(seqs * wide, width)

    def gather_rows(shard, order):
        dims = []
        for name in order:
            position = sum(1 for d in dims if "zqxc".index(d) < "zqxc".index(name))
            shard = move.gather(shard, name, position)
            dims.append(name)
        return shard.reshape((-1,) + shard.shape[-1:])

    pair_full = gather_rows(jnp.concatenate([w_key, w_value], axis=1), "zqxc")
    query_full = gather_rows(w_query, "zxqc")
    output_full = gather_rows(w_output, "zqxc")

    block = jnp.concatenate([w_gate, w_up, w_down], axis=0)
    ffn_blocks = []
    for k in range(Z):
        if k:
            block = move.step("z", block)
        line = [block]
        for _ in range(Q - 1):
            line.append(move.step("q", line[-1]))
        ffn_blocks.append(line)

    def spread(value):
        value = jnp.concatenate([value, move.step("x", value)], axis=0)
        return jnp.concatenate([value, move.step("c", value)], axis=0)

    def collect(value):
        value = value[: 2 * own_rows] + move.step("c", value[2 * own_rows :])
        return value[:own_rows] + move.step("x", value[own_rows:].astype(BF)).astype(F32)

    grad_out = out_grad.reshape(own_rows, width)
    grad_spread = spread(grad_out)

    inputs = tokens.reshape(own_rows, width).astype(F32)
    inverse1 = inverse_rms(inputs)
    normed = (inputs * inverse1 * attn_scale).astype(BF)
    inputs_all = tokens_all.astype(F32)
    normed_all = (inputs_all * inverse_rms(inputs_all) * attn_scale).astype(BF)
    cosine, sine = angle_tables(positions.reshape(own_rows))
    cosine_all, sine_all = angle_tables(places_all)
    query_raw = mm(normed, query_full)
    pair_raw = mm(normed_all, pair_full)
    queries = rotate(query_raw.reshape(own_rows, HEADS, HEAD), cosine, sine).astype(BF)
    keys = rotate(
        pair_raw[:, :pair_width].reshape(seqs * wide, KV_HEADS, HEAD), cosine_all, sine_all
    ).astype(BF)
    values = pair_raw[:, pair_width:].astype(BF)
    query_heads = head_layout(queries, seqs, rows)
    key_heads = key_layout(keys, seqs, wide)
    value_heads = key_layout(values, seqs, wide)
    mixed_heads, log_totals = attend_forward(query_heads, key_heads, value_heads, allowed)
    mixed = flat_layout(mixed_heads, seqs, rows)
    first_sum = inputs + mm(mixed, output_full)

    inverse2 = inverse_rms(first_sum)
    second = (first_sum * inverse2 * ffn_scale).astype(BF)
    second_spread = spread(second)
    out_part = 0.0
    second_grad_part = 0.0
    ffn_sums = []
    for k in range(Z):
        line = ffn_blocks[k]
        gate_w = jnp.concatenate([b[:units] for b in line], axis=0)
        up_w = jnp.concatenate([b[units : 2 * units] for b in line], axis=0)
        down_w = jnp.concatenate([b[2 * units :] for b in line], axis=0)
        gate = mm_t(second_spread, gate_w)
        up = mm_t(second_spread, up_w)
        sigma = jax.nn.sigmoid(gate)
        hidden = (gate * sigma * up).astype(BF)
        out_part = out_part + mm(hidden, down_w)
        hidden_grad = mm_t(grad_spread, down_w)
        gate_grad = (hidden_grad * up * sigma * (1.0 + gate * (1.0 - sigma))).astype(BF)
        up_grad = (hidden_grad * gate * sigma).astype(BF)
        second_grad_part = second_grad_part + mm(gate_grad, gate_w) + mm(up_grad, up_w)
        gate_sum = t_mm(gate_grad, second_spread)
        up_sum = t_mm(up_grad, second_spread)
        down_sum = t_mm(hidden, grad_spread)
        received = None
        for j in list(range(1, Q)) + [0]:
            cut = slice(j * units, (j + 1) * units)
            part = jnp.concatenate([gate_sum[cut], up_sum[cut], down_sum[cut]], axis=0)
            if received is not None:
                part = part + received
            if j:
                received = move.step("q", part.astype(BF)).astype(F32)
        ffn_sums.append(part)
    received = None
    for k in list(range(1, Z)) + [0]:
        part = ffn_sums[k]
        if received is not None:
            part = part + received
        if k:
            received = move.step("z", part.astype(BF)).astype(F32)
    grad_gate, grad_up, grad_down = part[:units], part[units : 2 * units], part[2 * units :]

    layer_out = (first_sum + collect(out_part)).astype(BF)
    second_grad = collect(second_grad_part)
    scaled2 = second_grad * ffn_scale
    ffn_gain_part = jnp.sum(second_grad * first_sum * inverse2, axis=0)
    first_grad = (
        grad_out.astype(F32)
        + inverse2 * scaled2
        - first_sum * inverse2**3 * jnp.mean(scaled2 * first_sum, axis=-1, keepdims=True)
    )

    attn_out_grad = first_grad.astype(BF)
    mixed_grad = mm_t(attn_out_grad, output_full).astype(BF)
    query_grad_heads, key_grad_heads, value_grad_heads = attend_backward(
        query_heads, key_heads, value_heads, head_layout(mixed_grad, seqs, rows), log_totals, allowed
    )
    query_grad = flat_layout(query_grad_heads, seqs, rows)
    query_back = (
        rotate(query_grad.reshape(own_rows, HEADS, HEAD), cosine, -sine)
        .reshape(own_rows, query_width)
        .astype(BF)
    )
    key_back = (
        rotate(
            key_flat(key_grad_heads, seqs, wide).reshape(seqs * wide, KV_HEADS, HEAD),
            cosine_all,
            -sine_all,
        )
        .reshape(seqs * wide, pair_width)
        .astype(BF)
    )
    pair_back = jnp.concatenate(
        [key_back, key_flat(value_grad_heads, seqs, wide).astype(BF)], axis=1
    )

    def scatter_rows(value, order):
        value = value.reshape(Z, Q, 2, 2, share, value.shape[-1])
        dims = list("zqxc")
        for name in order:
            value = move.scatter(value, name, dims.index(name))
            dims.remove(name)
        return value

    output_sum = t_mm(mixed, attn_out_grad)
    output_sum = jnp.concatenate(
        [output_sum, jnp.broadcast_to(ffn_gain_part[:, None], (width, 128))], axis=1
    )
    output_sum = scatter_rows(output_sum, "cxqz")
    grad_output, grad_gain_ffn = output_sum[:, :width], output_sum[:, width]
    grad_query = scatter_rows(t_mm(normed, query_back), "cqxz")
    grad_pair = scatter_rows(t_mm(normed_all, pair_back), "cxqz")
    grad_key, grad_value = grad_pair[:, :pair_width], grad_pair[:, pair_width:]
    grad_gain_attn = (
        jnp.sum(grad_query * w_query.astype(F32), axis=1)
        + jnp.sum(grad_key * w_key.astype(F32), axis=1)
        + jnp.sum(grad_value * w_value.astype(F32), axis=1)
    ) / gain_attn.astype(F32)

    pair_grad = mm_t(pair_back, pair_full).reshape(seqs, Z, rows, width)
    pair_grad = move.scatter(pair_grad, "z", 1, move.down, -1).reshape(own_rows, width)
    normed_grad = mm_t(query_back, query_full) + pair_grad
    scaled1 = normed_grad * attn_scale
    in_grad = (
        first_grad
        + inverse1 * scaled1
        - inputs * inverse1**3 * jnp.mean(scaled1 * inputs, axis=-1, keepdims=True)
    ).astype(BF)
    return (
        layer_out.reshape(seqs, rows, width),
        in_grad.reshape(seqs, rows, width),
        grad_query,
        grad_key,
        grad_value,
        grad_output,
        grad_gain_attn,
        grad_gain_ffn,
        grad_gate,
        grad_up,
        grad_down,
    )


def solution(mesh):
    rows = P(("seq", "dp"), None)
    vector = P(("seq", "dp"))
    act = P("dp", "seq", None)
    return jax.shard_map(
        per_device,
        mesh=mesh,
        in_specs=(act, P("dp", "seq"), act, rows, rows, rows, rows, vector, vector, rows, rows, rows),
        out_specs=(act, act, rows, rows, rows, rows, vector, vector, rows, rows, rows),
        check_vma=False,
    )
```

```python
import functools

import jax
import jax.numpy as jnp
from jax import lax
from jax.experimental import pallas as pl
from jax.experimental.pallas import tpu as pltpu
from jax.sharding import PartitionSpec as P

HEADS = 16
KV_HEADS = 8
HEAD = 96
GROUP = HEADS // KV_HEADS

EPS = 1e-05
THETA = 100000.0
NEG = -1e30
BF = jnp.bfloat16
F32 = jnp.float32


def inverse_rms(values):
    return lax.rsqrt(jnp.mean(values * values, axis=-1, keepdims=True) + EPS)


def angle_tables(places):
    offsets = jnp.arange(0, HEAD, 2, dtype=F32)
    angles = (THETA ** (-offsets / HEAD))[:, None] * places.astype(F32)[None, :]
    return (jnp.cos(angles), jnp.sin(angles))


def mm(left, right):
    return jnp.dot(left, right, preferred_element_type=F32)


def mm_t(left, right):
    return lax.dot_general(left, right, (((1,), (1,)), ((), ())), preferred_element_type=F32)


def t_mm(left, right):
    return lax.dot_general(left, right, (((0,), (0,)), ((), ())), preferred_element_type=F32)


class Moves:
    def __init__(self):
        self.Z = lax.axis_size("seq")
        self.DP = lax.axis_size("dp")
        self.Q = self.DP // 4
        self.zi = lax.axis_index("seq")
        place = lax.axis_index("dp")
        self.qi = place // 4
        self.xi = (place // 2) % 2
        self.ci = place % 2
        self.index = {"z": self.zi, "q": self.qi, "x": self.xi, "c": self.ci}
        self.size = {"z": self.Z, "q": self.Q, "x": 2, "c": 2}

    def step(self, axis, value):
        if axis == "c":
            return lax.ppermute(value, "dp", [(i, i ^ 1) for i in range(self.DP)])
        if axis == "x":
            return lax.ppermute(value, "dp", [(i, i ^ 2) for i in range(self.DP)])
        if axis == "q":
            return lax.ppermute(
                value, "dp", [(i, i % 4 + 4 * ((i // 4 + 1) % self.Q)) for i in range(self.DP)]
            )
        return lax.ppermute(value, "seq", [(i, (i + 1) % self.Z) for i in range(self.Z)])

    def up(self, value):
        return lax.ppermute(value, "seq", [(i, i + 1) for i in range(self.Z - 1)])

    def down(self, value):
        return lax.ppermute(value, "seq", [(i + 1, i) for i in range(self.Z - 1)])

    def gather(self, value, name, position, step=None):
        size, index = self.size[name], self.index[name]
        step = step or (lambda v: self.step(name, v))
        blocks = [value]
        for _ in range(size - 1):
            blocks.append(step(blocks[-1]))
        if size == 2:
            return jnp.where(
                index == 0, jnp.stack(blocks, axis=position), jnp.stack(blocks[::-1], axis=position)
            )
        out = jnp.zeros(value.shape[:position] + (size,) + value.shape[position:], value.dtype)
        for k, block in enumerate(blocks):
            out = lax.dynamic_update_slice_in_dim(
                out, jnp.expand_dims(block, position), (index - k) % size, axis=position
            )
        return out

    def scatter(self, value, name, position, step=None, sign=1):
        size, index = self.size[name], self.index[name]
        step = step or (lambda v: self.step(name, v))

        def take(k):
            return lax.dynamic_index_in_dim(
                value, (index - sign * k) % size, axis=position, keepdims=False
            )

        received = None
        for k in range(1, size):
            part = take(k)
            if received is not None:
                part = part + received
            received = step(part.astype(BF)).astype(F32)
        return take(0) + received


VMEM = pl.BlockSpec(memory_space=pltpu.VMEM)
ANY = pl.BlockSpec(memory_space=pl.ANY)
SMEM = pl.BlockSpec(memory_space=pltpu.SMEM)
SCALE = HEAD ** (-0.5)
HALF = HEAD // 2


def kernel_call(body, out_shape, in_specs, out_specs, scratch, flops, moved, args):
    return pl.pallas_call(
        body,
        out_shape=out_shape,
        in_specs=in_specs,
        out_specs=out_specs,
        scratch_shapes=scratch,
        compiler_params=pltpu.CompilerParams(vmem_limit_bytes=60 << 20),
        cost_estimate=pl.CostEstimate(flops=flops, bytes_accessed=moved, transcendentals=0),
    )(*args)


def turned_store(ref, row, lanes, block, cosine, sine):
    upper, lower = block[:HALF], block[HALF:]
    ref[pl.ds(row, HALF), lanes] = (upper * cosine - lower * sine).astype(ref.dtype)
    ref[pl.ds(row + HALF, HALF), lanes] = (lower * cosine + upper * sine).astype(ref.dtype)


def head_scores(queries, keys, place, wide):
    scores = mm(keys, queries) * SCALE
    rows = scores.shape[1] // GROUP
    key_place = lax.broadcasted_iota(jnp.int32, scores.shape, 0)
    query_place = place * rows + lax.rem(lax.broadcasted_iota(jnp.int32, scores.shape, 1), rows)
    return jnp.where(key_place <= query_place, scores, NEG)


def group_of(ref, g, lanes):
    return jnp.concatenate(
        [ref[pl.ds(pl.multiple_of((g * GROUP + j) * HEAD, 16), HEAD), lanes] for j in range(GROUP)],
        axis=1,
    )


def flip(value):
    return value.astype(F32).T.astype(value.dtype)


def attend_forward_body(
    seqs, wide, meta, tokens, gain, cosine, sine, pair_w, query_w,
    mixed, mixed_t, logs, query_t, pair_t, normed_t,
    pair_v, query_v, normed, own, sems,
):
    place = meta[0]
    rows = own.shape[0] // seqs
    pair_width = KV_HEADS * HEAD
    copies = [
        pltpu.make_async_copy(pair_w, pair_v, sems.at[0]),
        pltpu.make_async_copy(query_w, query_v, sems.at[1]),
    ]
    for copy in copies:
        copy.start()
    step = 256
    for b in range(seqs * wide // step):
        cut = slice(b * step, (b + 1) * step)
        values = tokens[cut, :].astype(F32)
        block = (values * inverse_rms(values) * gain[...]).astype(BF)
        normed[cut, :] = block
        normed_t[:, cut] = flip(block)
    for s in range(seqs):
        own[s * rows : (s + 1) * rows, :] = normed[
            pl.ds(pl.multiple_of(s * wide + place * rows, 128), rows), :
        ]
    copies[0].wait()
    width = 4 * HEAD
    for n in range(2 * pair_width // width):
        for s in range(seqs):
            lanes = slice(s * wide, (s + 1) * wide)
            block = mm(normed[lanes, :], pair_v[:, n * width : (n + 1) * width]).T
            if (n + 1) * width <= pair_width:
                for h in range(4):
                    turned_store(
                        pair_t, n * width + h * HEAD, lanes, block[h * HEAD : (h + 1) * HEAD],
                        cosine[:, lanes], sine[:, lanes],
                    )
            else:
                pair_t[n * width : (n + 1) * width, lanes] = block.astype(BF)
    copies[1].wait()
    for n in range(HEADS * HEAD // width):
        block = mm(own[...], query_v[:, n * width : (n + 1) * width]).T
        for s in range(seqs):
            lanes = slice(s * rows, (s + 1) * rows)
            here = pl.ds(pl.multiple_of(s * wide + place * rows, 128), rows)
            for h in range(4):
                turned_store(
                    query_t, n * width + h * HEAD, lanes, block[h * HEAD : (h + 1) * HEAD, lanes],
                    cosine[:, here], sine[:, here],
                )

    def one(g, _):
        row = pl.multiple_of(g * HEAD, 16)
        for s in range(seqs):
            lanes = slice(s * wide, (s + 1) * wide)
            mine = slice(s * rows, (s + 1) * rows)
            scores = head_scores(
                group_of(query_t, g, mine), flip(pair_t[pl.ds(row, HEAD), lanes]), place, wide
            )
            top = jnp.max(scores, axis=0, keepdims=True)
            weights = jnp.exp(scores - top)
            total = jnp.sum(weights, axis=0, keepdims=True)
            probs = (weights * (1.0 / total)).astype(BF)
            out = mm(pair_t[pl.ds(row + pair_width, HEAD), lanes], probs).astype(BF)
            for j in range(GROUP):
                mixed_t[pl.ds(pl.multiple_of((g * GROUP + j) * HEAD, 16), HEAD), mine] = out[
                    :, j * rows : (j + 1) * rows
                ]
            logs[g, s] = top + jnp.log(total)
        return 0

    lax.fori_loop(0, KV_HEADS, one, 0)
    mixed[...] = flip(mixed_t[...])


def attend_forward(meta, tokens, gain, cosine, sine, pair_w, query_w, seqs, rows):
    count, width = tokens.shape
    wide = count // seqs
    own = seqs * rows
    q, kv = query_w.shape[1], pair_w.shape[1]
    sds = jax.ShapeDtypeStruct
    return kernel_call(
        functools.partial(attend_forward_body, seqs, wide),
        (
            sds((own, q), BF), sds((q, own), BF), sds((KV_HEADS, seqs, 1, GROUP * rows), F32),
            sds((q, own), BF), sds((kv, count), BF), sds((width, count), BF),
        ),
        [SMEM, VMEM, VMEM, VMEM, VMEM, ANY, ANY],
        (VMEM,) * 6,
        [
            pltpu.VMEM(pair_w.shape, BF), pltpu.VMEM(query_w.shape, BF), pltpu.VMEM((count, width), BF),
            pltpu.VMEM((own, width), BF), pltpu.SemaphoreType.DMA((2,)),
        ],
        2 * count * width * kv + 2 * own * width * q + 4 * own * wide * q,
        20 << 20,
        (meta, tokens, gain, cosine, sine, pair_w, query_w),
    )


def attend_backward_body(
    seqs, wide, meta, query_t, pair_t, grad_t, logs, cosine, sine, query_back, pair_back
):
    place = meta[0]
    rows = query_t.shape[1] // seqs
    pair_width = KV_HEADS * HEAD

    def one(g, _):
        row = pl.multiple_of(g * HEAD, 16)
        for s in range(seqs):
            lanes = slice(s * wide, (s + 1) * wide)
            mine = slice(s * rows, (s + 1) * rows)
            here = pl.ds(pl.multiple_of(s * wide + place * rows, 128), rows)
            queries = group_of(query_t, g, mine)
            grads = group_of(grad_t, g, mine)
            keys_t = pair_t[pl.ds(row, HEAD), lanes]
            values_t = pair_t[pl.ds(row + pair_width, HEAD), lanes]
            probs = jnp.exp(head_scores(queries, flip(keys_t), place, wide) - logs[g, s])
            prob_grad = mm(flip(values_t), grads)
            centre = jnp.sum(probs * prob_grad, axis=0, keepdims=True)
            score_grad = (probs * (prob_grad - centre)).astype(BF)
            query_grad = mm(keys_t, score_grad) * SCALE
            for j in range(GROUP):
                turned_store(
                    query_back, pl.multiple_of((g * GROUP + j) * HEAD, 16), mine,
                    query_grad[:, j * rows : (j + 1) * rows], cosine[:, here], -sine[:, here],
                )
            turned_store(
                pair_back, row, lanes, mm_t(queries, score_grad) * SCALE,
                cosine[:, lanes], -sine[:, lanes],
            )
            pair_back[pl.ds(row + pair_width, HEAD), lanes] = mm_t(
                grads, probs.astype(BF)
            ).astype(BF)
        return 0

    lax.fori_loop(0, KV_HEADS, one, 0)


def attend_backward(meta, query_t, pair_t, grad_t, logs, cosine, sine, seqs):
    wide = pair_t.shape[1] // seqs
    return kernel_call(
        functools.partial(attend_backward_body, seqs, wide),
        (jax.ShapeDtypeStruct(query_t.shape, BF), jax.ShapeDtypeStruct(pair_t.shape, BF)),
        [SMEM] + [VMEM] * 6,
        (VMEM, VMEM),
        [],
        10 * query_t.size * wide,
        12 << 20,
        (meta, query_t, pair_t, grad_t, logs, cosine, sine),
    )


def output_body(tokens, mixed, gain, weights, total, second, weights_v, sem):
    copy = pltpu.make_async_copy(weights, weights_v, sem)
    copy.start()
    copy.wait()
    value = tokens[...].astype(F32) + mm(mixed[...], weights_v[...])
    total[...] = value
    second[...] = (value * inverse_rms(value) * gain[...]).astype(BF)


def output_forward(tokens, mixed, gain, weights):
    return kernel_call(
        output_body,
        (jax.ShapeDtypeStruct(tokens.shape, F32), jax.ShapeDtypeStruct(tokens.shape, BF)),
        [VMEM, VMEM, VMEM, ANY],
        (VMEM, VMEM),
        [pltpu.VMEM(weights.shape, BF), pltpu.SemaphoreType.DMA],
        2 * tokens.shape[0] * weights.size,
        10 << 20,
        (tokens, mixed, gain, weights),
    )


def output_back_body(
    grad, total, second_grad, gain, mixed_t, weights, first_grad, mixed_grad_t, sums, weights_v, da, sem
):
    copy = pltpu.make_async_copy(weights, weights_v, sem)
    copy.start()
    value = total[...]
    inverse = inverse_rms(value)
    back = second_grad[...]
    scaled = back * gain[...]
    first = (
        grad[...].astype(F32)
        + inverse * scaled
        - value * inverse**3 * jnp.mean(scaled * value, axis=-1, keepdims=True)
    )
    first_grad[...] = first
    da[...] = first.astype(BF)
    width = value.shape[1]
    gain_part = jnp.sum((back * value * inverse).T, axis=1, keepdims=True)
    sums[:, width:] = jnp.broadcast_to(gain_part, (width, 128))
    step = 512
    for n in range(width // step):
        cut = slice(n * step, (n + 1) * step)
        sums[:, cut] = mm(mixed_t[...], da[:, cut])
    copy.wait()
    for n in range(width // step):
        cut = slice(n * step, (n + 1) * step)
        mixed_grad_t[cut, :] = mm_t(weights_v[cut, :], da[...]).astype(BF)


def output_backward(grad, total, second_grad, gain, mixed_t, weights):
    own, width = grad.shape
    return kernel_call(
        output_back_body,
        (
            jax.ShapeDtypeStruct((own, width), F32),
            jax.ShapeDtypeStruct(mixed_t.shape, BF),
            jax.ShapeDtypeStruct((width, width + 128), F32),
        ),
        [VMEM] * 5 + [ANY],
        (VMEM,) * 3,
        [pltpu.VMEM(weights.shape, BF), pltpu.VMEM((own, width), BF), pltpu.SemaphoreType.DMA],
        4 * own * weights.size,
        22 << 20,
        (grad, total, second_grad, gain, mixed_t, weights),
    )


def ffn_body(blocks, units, *refs):
    second, grads = refs[:4], refs[4:8]
    shards = refs[8 : 8 + blocks]
    (out, back, hidden_t, gate_t, up_t) = refs[8 + blocks : 13 + blocks]
    second_v, grads_v, weights, hidden, gate_g, up_g, sems = refs[13 + blocks :]
    rows = second[0].shape[0]
    first = []
    for i in range(4):
        cut = pl.ds(i * rows, rows)
        first.append(pltpu.make_async_copy(second[i], second_v.at[cut], sems.at[0, i]))
        first.append(pltpu.make_async_copy(grads[i], grads_v.at[cut], sems.at[1, i]))
    copies = [
        [
            pltpu.make_async_copy(
                shards[b].at[pl.ds(p * units, units)],
                weights.at[p, pl.ds(b * units, units)],
                sems.at[2 + p, b],
            )
            for p in range(3)
        ]
        for b in range(blocks)
    ]
    for copy in first:
        copy.start()
    for line in copies:
        for copy in line:
            copy.start()
    for copy in first:
        copy.wait()
    step = 256
    count = 4 * rows
    per = step // units
    for n in range(blocks // per):
        for line in copies[n * per : (n + 1) * per]:
            for copy in line:
                copy.wait()
        cut = slice(n * step, (n + 1) * step)
        gate_w, up_w, down_w = weights[0, cut], weights[1, cut], weights[2, cut]

        def one(m, _):
            here = pl.ds(pl.multiple_of(m * step, step), step)
            gate = mm_t(second_v[here, :], gate_w)
            up = mm_t(second_v[here, :], up_w)
            hidden_grad = mm_t(grads_v[here, :], down_w)
            sigma = jax.nn.sigmoid(gate)
            mixed = gate * sigma * up
            hidden[here, cut] = mixed.astype(BF)
            hidden_t[cut, here] = mixed.T.astype(BF)
            gate_grad = hidden_grad * up * sigma * (1.0 + gate * (1.0 - sigma))
            gate_g[here, cut] = gate_grad.astype(BF)
            gate_t[cut, here] = gate_grad.T.astype(BF)
            up_grad = hidden_grad * (gate * sigma)
            up_g[here, cut] = up_grad.astype(BF)
            up_t[cut, here] = up_grad.T.astype(BF)
            return 0

        lax.fori_loop(0, count // step, one, 0)

    def two(m, _):
        here = pl.ds(pl.multiple_of(m * step, step), step)
        back[here, :] = (mm(gate_g[here, :], weights[0]) + mm(up_g[here, :], weights[1])).astype(back.dtype)
        out[here, :] = mm(hidden[here, :], weights[2]).astype(out.dtype)
        return 0

    lax.fori_loop(0, count // step, two, 0)


def ffn(second, grads, shards, units):
    blocks = len(shards)
    rows, width = second[0].shape
    count, total = 4 * rows, blocks * units
    sds = jax.ShapeDtypeStruct
    return kernel_call(
        functools.partial(ffn_body, blocks, units),
        (
            sds((count, width), BF), sds((count, width), BF),
            sds((total, count), BF), sds((total, count), BF), sds((total, count), BF),
        ),
        [ANY] * (8 + blocks),
        (VMEM,) * 5,
        [
            pltpu.VMEM((count, width), BF), pltpu.VMEM((count, width), BF),
            pltpu.VMEM((3, total, width), BF),
            pltpu.VMEM((count, total), BF), pltpu.VMEM((count, total), BF), pltpu.VMEM((count, total), BF),
            pltpu.SemaphoreType.DMA((5, max(blocks, 4))),
        ],
        12 * count * total * width,
        34 << 20,
        (*second, *grads, *shards),
    )


def ffn_sums_body(units, lines, hidden_t, gate_t, up_t, *refs):
    second, grads = refs[:4], refs[4:8]
    outs = refs[8 : 8 + lines]
    rows = second[0].shape[0]
    for p, left, right in ((0, gate_t, second), (1, up_t, second), (2, hidden_t, grads)):
        total = mm(left[:, :rows], right[0][...])
        for i in range(1, 4):
            total += mm(left[:, i * rows : (i + 1) * rows], right[i][...])
        for j in range(lines):
            outs[j][p * units : (p + 1) * units, :] = total[j * units : (j + 1) * units].astype(
                outs[j].dtype
            )


def ffn_sums(k, hidden_t, gate_t, up_t, second, grads, units, lines):
    rows, width = second[0].shape
    here = pl.BlockSpec((lines * units, 4 * rows), lambda i: (k, 0))
    whole = pl.BlockSpec((rows, width), lambda i: (0, 0))
    full = pl.BlockSpec((3 * units, width), lambda i: (0, 0))
    return pl.pallas_call(
        functools.partial(ffn_sums_body, units, lines),
        out_shape=tuple(
            jax.ShapeDtypeStruct((3 * units, width), BF if j else F32) for j in range(lines)
        ),
        grid=(1,),
        in_specs=[here] * 3 + [whole] * 8,
        out_specs=(full,) * lines,
        compiler_params=pltpu.CompilerParams(vmem_limit_bytes=60 << 20),
        cost_estimate=pl.CostEstimate(
            flops=24 * lines * units * rows * width, bytes_accessed=14 << 20, transcendentals=0
        ),
    )(hidden_t, gate_t, up_t, *second, *grads)


def project_sums_body(seqs, meta, normed_t, query_back, pair_back, query_sums, pair_sums):
    place = meta[0]
    wide = normed_t.shape[1] // seqs
    rows = query_back.shape[1] // seqs
    own = jnp.concatenate(
        [normed_t[:, pl.ds(pl.multiple_of(s * wide + place * rows, 128), rows)] for s in range(seqs)],
        axis=1,
    )
    step = 512
    for n in range(query_back.shape[0] // step):
        cut = slice(n * step, (n + 1) * step)
        query_sums[:, cut] = mm_t(own, query_back[cut, :])
    for n in range(pair_back.shape[0] // step):
        cut = slice(n * step, (n + 1) * step)
        pair_sums[:, cut] = mm_t(normed_t[...], pair_back[cut, :])


def project_sums(meta, normed_t, query_back, pair_back, seqs):
    width = normed_t.shape[0]
    return kernel_call(
        functools.partial(project_sums_body, seqs),
        (
            jax.ShapeDtypeStruct((width, query_back.shape[0]), F32),
            jax.ShapeDtypeStruct((width, pair_back.shape[0]), F32),
        ),
        [SMEM, VMEM, VMEM, VMEM],
        (VMEM, VMEM),
        [],
        2 * width * (query_back.size + pair_back.size),
        26 << 20,
        (meta, normed_t, query_back, pair_back),
    )


def project_back_body(seqs, query_back, pair_back, query_w, pair_w, query_grad, pair_grad, pair_v, query_v, sems):
    copies = [
        pltpu.make_async_copy(pair_w, pair_v, sems.at[0]),
        pltpu.make_async_copy(query_w, query_v, sems.at[1]),
    ]
    for copy in copies:
        copy.start()
    blocks, _, own = pair_grad.shape
    rows = own // seqs
    wide = pair_back.shape[1] // seqs
    step = 512
    copies[0].wait()
    for n in range(pair_w.shape[0] // step):
        cut = slice(n * step, (n + 1) * step)
        for s in range(seqs):
            part = mm(pair_v[cut, :], pair_back[:, s * wide : (s + 1) * wide])
            for z in range(blocks):
                pair_grad[z, cut, s * rows : (s + 1) * rows] = part[:, z * rows : (z + 1) * rows].astype(BF)
    copies[1].wait()
    for n in range(query_w.shape[0] // step):
        cut = slice(n * step, (n + 1) * step)
        query_grad[cut, :] = mm(query_v[cut, :], query_back[...])


def project_back(query_back, pair_back, query_w, pair_w, seqs, blocks):
    width = query_w.shape[0]
    own = query_back.shape[1]
    return kernel_call(
        functools.partial(project_back_body, seqs),
        (
            jax.ShapeDtypeStruct((width, own), F32),
            jax.ShapeDtypeStruct((blocks, width, own), BF),
        ),
        [VMEM, VMEM, ANY, ANY],
        (VMEM, VMEM),
        [pltpu.VMEM(pair_w.shape, BF), pltpu.VMEM(query_w.shape, BF), pltpu.SemaphoreType.DMA((2,))],
        2 * width * (query_back.size + pair_back.size),
        20 << 20,
        (query_back, pair_back, query_w, pair_w),
    )


def input_grad_body(tokens, gain, first_grad, query_grad, pair_grad, received, out):
    back = (query_grad[...] + pair_grad[...].astype(F32) + received[...].astype(F32)).T
    value = tokens[...].astype(F32)
    inverse = inverse_rms(value)
    scaled = back * gain[...]
    out[...] = (
        first_grad[...]
        + inverse * scaled
        - value * inverse**3 * jnp.mean(scaled * value, axis=-1, keepdims=True)
    ).astype(BF)


def input_grad(tokens, gain, first_grad, query_grad, pair_grad, received):
    return kernel_call(
        input_grad_body,
        jax.ShapeDtypeStruct(tokens.shape, BF),
        [VMEM] * 6,
        VMEM,
        [],
        tokens.size * 20,
        8 << 20,
        (tokens, gain, first_grad, query_grad, pair_grad, received),
    )


def per_device(
    tokens,
    positions,
    out_grad,
    w_query,
    w_key,
    w_value,
    w_output,
    gain_attn,
    gain_ffn,
    w_gate,
    w_up,
    w_down,
):
    move = Moves()
    Z, Q = move.Z, move.Q
    seqs, rows, width = tokens.shape
    wide = rows * Z
    own_rows = seqs * rows
    pair_width = KV_HEADS * HEAD
    share = w_query.shape[0]
    units = w_gate.shape[0]
    meta = move.zi.astype(jnp.int32).reshape(1)

    gains = jnp.pad(jnp.stack([gain_attn, gain_ffn]), ((0, 0), (0, 128 - share)))
    for position, name in enumerate("zqxc"):
        gains = move.gather(gains, name, position)
    gains = gains[..., :share].transpose(4, 0, 1, 2, 3, 5).reshape(2, width).astype(F32)
    attn_scale, ffn_scale = gains[0:1], gains[1:2]

    places_all = move.gather(positions, "z", 1, move.up).reshape(seqs * wide)
    tokens_all = move.gather(tokens, "z", 1, move.up).reshape(seqs * wide, width)

    def gather_rows(shard, order):
        dims = []
        for name in order:
            position = sum(1 for d in dims if "zqxc".index(d) < "zqxc".index(name))
            shard = move.gather(shard, name, position)
            dims.append(name)
        return shard.reshape((-1,) + shard.shape[-1:])

    pair_full = gather_rows(jnp.concatenate([w_key, w_value], axis=1), "zqxc")
    query_full = gather_rows(w_query, "zxqc")
    output_full = gather_rows(w_output, "zqxc")

    block = jnp.concatenate([w_gate, w_up, w_down], axis=0)
    ffn_blocks = []
    for k in range(Z):
        if k:
            block = move.step("z", block)
        line = [block]
        for _ in range(Q - 1):
            line.append(move.step("q", line[-1]))
        ffn_blocks.append(line)

    def spread(value):
        near = move.step("x", value)
        return (value, near, move.step("c", value), move.step("c", near))

    def collect(value):
        half = 2 * own_rows
        value = value[:half].astype(F32) + move.step("c", value[half:]).astype(F32)
        return value[:own_rows] + move.step("x", value[own_rows:].astype(BF)).astype(F32)

    grad_out = out_grad.reshape(own_rows, width)
    grad_spread = spread(grad_out)
    inputs = tokens.reshape(own_rows, width)

    cosine, sine = angle_tables(places_all)
    mixed, mixed_t, logs, query_t, pair_t, normed_t = attend_forward(
        meta, tokens_all, attn_scale, cosine, sine, pair_full, query_full, seqs, rows
    )
    first_sum, second = output_forward(inputs, mixed, ffn_scale, output_full)

    second_spread = spread(second)
    shards = [b for line in ffn_blocks for b in line]
    out_part, second_part, hidden_t, gate_t, up_t = ffn(second_spread, grad_spread, shards, units)
    second_grad = collect(second_part)
    received = None
    for k in list(range(1, Z)) + [0]:
        own, *others = ffn_sums(k, hidden_t, gate_t, up_t, second_spread, grad_spread, units, Q)
        passing = None
        for part in others:
            passing = move.step("q", part if passing is None else (part.astype(F32) + passing).astype(BF))
            passing = passing.astype(F32)
        own = own + passing
        if received is not None:
            own = own + received
        if k:
            received = move.step("z", own.astype(BF)).astype(F32)
    grad_gate, grad_up, grad_down = own[:units], own[units : 2 * units], own[2 * units :]
    layer_out = (first_sum + collect(out_part)).astype(BF)

    def scatter_rows(value, order):
        value = value.reshape(Z, Q, 2, 2, share, value.shape[-1])
        dims = list("zqxc")
        for name in order:
            value = move.scatter(value, name, dims.index(name))
            dims.remove(name)
        return value

    first_grad, mixed_grad_t, output_sum = output_backward(
        grad_out, first_sum, second_grad, ffn_scale, mixed_t, output_full
    )
    output_sum = scatter_rows(output_sum, "cxqz")
    grad_output, grad_gain_ffn = output_sum[:, :width], output_sum[:, width]
    query_back, pair_back = attend_backward(
        meta, query_t, pair_t, mixed_grad_t, logs, cosine, sine, seqs
    )
    query_sum, pair_sum = project_sums(meta, normed_t, query_back, pair_back, seqs)
    grad_query = scatter_rows(query_sum, "cqxz")
    grad_pair = scatter_rows(pair_sum, "cxqz")
    grad_key, grad_value = grad_pair[:, :pair_width], grad_pair[:, pair_width:]
    grad_gain_attn = (
        jnp.sum(grad_query * w_query.astype(F32), axis=1)
        + jnp.sum(grad_key * w_key.astype(F32), axis=1)
        + jnp.sum(grad_value * w_value.astype(F32), axis=1)
    ) / gain_attn.astype(F32)

    query_grad, pair_grad = project_back(query_back, pair_back, query_full, pair_full, seqs, Z)
    received = None
    for k in range(1, Z):
        part = lax.dynamic_index_in_dim(pair_grad, (move.zi + k) % Z, axis=0, keepdims=False)
        if received is not None:
            part = (part.astype(F32) + received.astype(F32)).astype(BF)
        received = move.down(part)
    mine = lax.dynamic_index_in_dim(pair_grad, move.zi, axis=0, keepdims=False)
    in_grad = input_grad(inputs, attn_scale, first_grad, query_grad, mine, received)
    return (
        layer_out.reshape(seqs, rows, width),
        in_grad.reshape(seqs, rows, width),
        grad_query,
        grad_key,
        grad_value,
        grad_output,
        grad_gain_attn,
        grad_gain_ffn,
        grad_gate,
        grad_up,
        grad_down,
    )


def solution(mesh):
    rows = P(("seq", "dp"), None)
    vector = P(("seq", "dp"))
    act = P("dp", "seq", None)
    return jax.shard_map(
        per_device,
        mesh=mesh,
        in_specs=(act, P("dp", "seq"), act, rows, rows, rows, rows, vector, vector, rows, rows, rows),
        out_specs=(act, act, rows, rows, rows, rows, vector, vector, rows, rows, rows),
        check_vma=False,
    )
```

```python
import functools

import jax
import jax.numpy as jnp
from jax import lax
from jax.experimental import pallas as pl
from jax.experimental.pallas import tpu as pltpu
from jax.sharding import PartitionSpec as P

HEADS = 16
KV_HEADS = 8
HEAD = 96
GROUP = HEADS // KV_HEADS

EPS = 1e-05
THETA = 100000.0
NEG = -1e30
BF = jnp.bfloat16
F32 = jnp.float32


def inverse_rms(values):
    return lax.rsqrt(jnp.mean(values * values, axis=-1, keepdims=True) + EPS)


def angle_tables(places):
    offsets = jnp.arange(0, HEAD, 2, dtype=F32)
    angles = (THETA ** (-offsets / HEAD))[:, None] * places.astype(F32)[None, :]
    return (jnp.cos(angles), jnp.sin(angles))


def mm(left, right):
    return jnp.dot(left, right, preferred_element_type=F32)


def mm_t(left, right):
    return lax.dot_general(left, right, (((1,), (1,)), ((), ())), preferred_element_type=F32)


def t_mm(left, right):
    return lax.dot_general(left, right, (((0,), (0,)), ((), ())), preferred_element_type=F32)


def in_f32(value):
    return value.astype(F32)


def after(value, *others):
    return lax.optimization_barrier((value, *others))[0]


class Moves:
    def __init__(self):
        self.Z = lax.axis_size("seq")
        self.DP = lax.axis_size("dp")
        self.Q = self.DP // 4
        self.zi = lax.axis_index("seq")
        place = lax.axis_index("dp")
        self.qi = place // 4
        self.xi = (place // 2) % 2
        self.ci = place % 2

    def step(self, offset, value):
        if offset == "c":
            return lax.ppermute(value, "dp", [(n, n ^ 1) for n in range(self.DP)])
        j, i = offset
        return lax.ppermute(
            value, "dp", [(n, (n % 4) ^ (2 * i) | 4 * ((n // 4 + j) % self.Q)) for n in range(self.DP)]
        )


VMEM = pl.BlockSpec(memory_space=pltpu.VMEM)
ANY = pl.BlockSpec(memory_space=pl.ANY)
SMEM = pl.BlockSpec(memory_space=pltpu.SMEM)
SCALE = HEAD ** (-0.5)
HALF = HEAD // 2
QUERY = HEADS * HEAD
PAIR = 2 * KV_HEADS * HEAD


def kernel_call(body, out_shape, in_specs, out_specs, scratch, flops, moved, args):
    return pl.pallas_call(
        body,
        out_shape=out_shape,
        in_specs=in_specs,
        out_specs=out_specs,
        scratch_shapes=scratch,
        compiler_params=pltpu.CompilerParams(vmem_limit_bytes=60 << 20),
        cost_estimate=pl.CostEstimate(flops=flops, bytes_accessed=moved, transcendentals=0),
    )(*args)


def load_rows(meta, places, lines, refs, target, sems, columns):
    copies = []
    if len(refs) == 1:
        copies.append(pltpu.make_async_copy(refs[0].at[:, columns], target, sems.at[0]))
    else:
        qi, xi, ci = meta[1], meta[2], meta[3]
        for ref, (j, i, l, first) in zip(refs, places):
            blocks, share, _ = ref.shape
            q = lax.rem(qi + (lines - j), lines)
            x = lax.rem(xi + i, 2)
            c = lax.rem(ci + l, 2)
            for k in range(blocks):
                row = pl.multiple_of(((((first + k) * lines + q) * 2 + x) * 2 + c) * share, share)
                copies.append(
                    pltpu.make_async_copy(
                        ref.at[k, :, columns], target.at[pl.ds(row, share), :], sems.at[len(copies)]
                    )
                )
    for copy in copies:
        copy.start()
    return copies


def arrays_of(pieces):
    return [piece[0] for piece in pieces]


def places_of(pieces):
    return tuple(piece[1:] for piece in pieces)


def copies_of(pieces):
    count = 1 if len(pieces) == 1 else sum(piece[0].shape[0] for piece in pieces)
    return pltpu.SemaphoreType.DMA((count,))


def store_rows(meta, split, block, first, send, keep, columns):
    if not split:
        keep[pl.ds(first, block.shape[0]), columns] = block.astype(keep.dtype)
        return
    lines, share = keep.shape[0] // 2, keep.shape[2]
    qi, xi, ci = meta[1], meta[2], meta[3]
    for n in range(block.shape[0] // (2 * share)):
        chip = first // (2 * share) + n
        z, q, x = chip // (2 * lines), chip // 2 % lines, chip % 2
        j = lax.rem(qi + (lines - q), lines)
        i = lax.rem(xi + x, 2)
        even = block[2 * n * share : (2 * n + 1) * share]
        odd = block[(2 * n + 1) * share : (2 * n + 2) * share]
        keep[2 * j + i, z, :, columns] = jnp.where(ci == 0, even, odd).astype(keep.dtype)
        send[2 * j + i, z, :, columns] = jnp.where(ci == 0, odd, even).astype(send.dtype)


def sums_shapes(split, parts, rows, width):
    if not split:
        return (jax.ShapeDtypeStruct((8, 128), BF), jax.ShapeDtypeStruct((rows, width), BF))
    shape = (parts[1] * 2, parts[0], rows // (parts[0] * parts[1] * 4), width)
    return (jax.ShapeDtypeStruct(shape, BF), jax.ShapeDtypeStruct(shape, BF))


def turned_store(ref, row, lanes, block, cosine, sine):
    upper, lower = block[:HALF], block[HALF:]
    ref[pl.ds(row, HALF), lanes] = (upper * cosine - lower * sine).astype(ref.dtype)
    ref[pl.ds(row + HALF, HALF), lanes] = (lower * cosine + upper * sine).astype(ref.dtype)


def head_scores(queries, keys, place, wide):
    scores = mm(keys, queries) * SCALE
    rows = scores.shape[1] // GROUP
    key_place = lax.broadcasted_iota(jnp.int32, scores.shape, 0)
    query_place = place * rows + lax.rem(lax.broadcasted_iota(jnp.int32, scores.shape, 1), rows)
    return jnp.where(key_place <= query_place, scores, NEG)


def group_of(ref, g, lanes):
    return jnp.concatenate(
        [ref[pl.ds(pl.multiple_of((g * GROUP + j) * HEAD, 16), HEAD), lanes] for j in range(GROUP)],
        axis=1,
    )


def flip(value):
    return value.astype(F32).T.astype(value.dtype)


def project_forward_body(seqs, wide, places, lines, meta, tokens, cosine, sine, *refs):
    count = len(places)
    pieces, refs = refs[:count], refs[count:]
    (
        query_t, pair_t, normed_t, gains,
        pair_v, query_v, normed, own, pair_sems, query_sems,
    ) = refs
    place = meta[0]
    rows = own.shape[0] // seqs
    pair_width = KV_HEADS * HEAD
    pair_copies = load_rows(meta, places, lines, pieces, pair_v, pair_sems, pl.ds(0, PAIR + 128))
    query_copies = load_rows(meta, places, lines, pieces, query_v, query_sems, pl.ds(PAIR + 128, QUERY))
    for copy in pair_copies:
        copy.wait()
    gains[...] = pair_v[:, PAIR:].astype(F32).T[:8]
    gain = gains[0:1]
    step = 256
    for b in range(seqs * wide // step):
        cut = slice(b * step, (b + 1) * step)
        values = tokens[cut, : normed.shape[1]].astype(F32)
        block = (values * inverse_rms(values) * gain).astype(BF)
        normed[cut, :] = block
        normed_t[:, cut] = flip(block)
    for s in range(seqs):
        own[s * rows : (s + 1) * rows, :] = normed[
            pl.ds(pl.multiple_of(s * wide + place * rows, 128), rows), :
        ]
    width = 4 * HEAD
    for n in range(2 * pair_width // width):
        for s in range(seqs):
            lanes = slice(s * wide, (s + 1) * wide)
            block = mm(normed[lanes, :], pair_v[:, n * width : (n + 1) * width]).T
            if (n + 1) * width <= pair_width:
                for h in range(4):
                    turned_store(
                        pair_t, n * width + h * HEAD, lanes, block[h * HEAD : (h + 1) * HEAD],
                        cosine[:, lanes], sine[:, lanes],
                    )
            else:
                pair_t[n * width : (n + 1) * width, lanes] = block.astype(BF)
    for copy in query_copies:
        copy.wait()
    for n in range(HEADS * HEAD // width):
        block = mm(own[...], query_v[:, n * width : (n + 1) * width]).T
        for s in range(seqs):
            lanes = slice(s * rows, (s + 1) * rows)
            here = pl.ds(pl.multiple_of(s * wide + place * rows, 128), rows)
            for h in range(4):
                turned_store(
                    query_t, n * width + h * HEAD, lanes, block[h * HEAD : (h + 1) * HEAD, lanes],
                    cosine[:, here], sine[:, here],
                )


def attend_forward_body(seqs, wide, meta, query_t, pair_t, mixed, mixed_t, logs):
    place = meta[0]
    rows = query_t.shape[1] // seqs
    pair_width = KV_HEADS * HEAD

    def one(g, _):
        row = pl.multiple_of(g * HEAD, 16)
        for s in range(seqs):
            lanes = slice(s * wide, (s + 1) * wide)
            mine = slice(s * rows, (s + 1) * rows)
            scores = head_scores(
                group_of(query_t, g, mine), flip(pair_t[pl.ds(row, HEAD), lanes]), place, wide
            )
            top = jnp.max(scores, axis=0, keepdims=True)
            weights = jnp.exp(scores - top)
            total = jnp.sum(weights, axis=0, keepdims=True)
            probs = (weights * (1.0 / total)).astype(BF)
            out = mm(pair_t[pl.ds(row + pair_width, HEAD), lanes], probs).astype(BF)
            for j in range(GROUP):
                mixed_t[pl.ds(pl.multiple_of((g * GROUP + j) * HEAD, 16), HEAD), mine] = out[
                    :, j * rows : (j + 1) * rows
                ]
            logs[g, s] = top + jnp.log(total)
        return 0

    lax.fori_loop(0, KV_HEADS, one, 0)
    mixed[...] = flip(mixed_t[...])


def project_forward(meta, tokens, cosine, sine, pieces, lines, width, seqs, rows):
    count = tokens.shape[0]
    wide = count // seqs
    own = seqs * rows
    sds = jax.ShapeDtypeStruct
    return kernel_call(
        functools.partial(project_forward_body, seqs, wide, places_of(pieces), lines),
        (sds((QUERY, own), BF), sds((PAIR, count), BF), sds((width, count), BF), sds((8, width), F32)),
        [SMEM, VMEM, VMEM, VMEM] + [ANY] * len(pieces),
        (VMEM,) * 4,
        [
            pltpu.VMEM((width, PAIR + 128), BF), pltpu.VMEM((width, QUERY), BF),
            pltpu.VMEM((count, width), BF), pltpu.VMEM((own, width), BF), copies_of(pieces), copies_of(pieces),
        ],
        2 * count * width * PAIR + 2 * own * width * QUERY,
        20 << 20,
        (meta, tokens, cosine, sine, *arrays_of(pieces)),
    )


def attend_forward(meta, query_t, pair_t, seqs):
    own = query_t.shape[1]
    wide = pair_t.shape[1] // seqs
    sds = jax.ShapeDtypeStruct
    return kernel_call(
        functools.partial(attend_forward_body, seqs, wide),
        (
            sds((own, QUERY), BF), sds((QUERY, own), BF),
            sds((KV_HEADS, seqs, 1, GROUP * own // seqs), F32),
        ),
        [SMEM, VMEM, VMEM],
        (VMEM,) * 3,
        [],
        4 * own * wide * QUERY,
        6 << 20,
        (meta, query_t, pair_t),
    )


def attend_backward_body(
    seqs, wide, meta, query_t, pair_t, grad_t, logs, cosine, sine, query_back, pair_back
):
    place = meta[0]
    rows = query_t.shape[1] // seqs
    pair_width = KV_HEADS * HEAD

    def one(g, _):
        row = pl.multiple_of(g * HEAD, 16)
        for s in range(seqs):
            lanes = slice(s * wide, (s + 1) * wide)
            mine = slice(s * rows, (s + 1) * rows)
            here = pl.ds(pl.multiple_of(s * wide + place * rows, 128), rows)
            queries = group_of(query_t, g, mine)
            grads = group_of(grad_t, g, mine)
            keys_t = pair_t[pl.ds(row, HEAD), lanes]
            values_t = pair_t[pl.ds(row + pair_width, HEAD), lanes]
            probs = jnp.exp(head_scores(queries, flip(keys_t), place, wide) - logs[g, s])
            prob_grad = mm(flip(values_t), grads)
            centre = jnp.sum(probs * prob_grad, axis=0, keepdims=True)
            score_grad = (probs * (prob_grad - centre)).astype(BF)
            query_grad = mm(keys_t, score_grad) * SCALE
            for j in range(GROUP):
                turned_store(
                    query_back, pl.multiple_of((g * GROUP + j) * HEAD, 16), mine,
                    query_grad[:, j * rows : (j + 1) * rows], cosine[:, here], -sine[:, here],
                )
            turned_store(
                pair_back, row, lanes, mm_t(queries, score_grad) * SCALE,
                cosine[:, lanes], -sine[:, lanes],
            )
            pair_back[pl.ds(row + pair_width, HEAD), lanes] = mm_t(
                grads, probs.astype(BF)
            ).astype(BF)
        return 0

    lax.fori_loop(0, KV_HEADS, one, 0)


def attend_backward(meta, query_t, pair_t, grad_t, logs, cosine, sine, seqs):
    wide = pair_t.shape[1] // seqs
    return kernel_call(
        functools.partial(attend_backward_body, seqs, wide),
        (jax.ShapeDtypeStruct(query_t.shape, BF), jax.ShapeDtypeStruct(pair_t.shape, BF)),
        [SMEM] + [VMEM] * 6,
        (VMEM, VMEM),
        [],
        10 * query_t.size * wide,
        12 << 20,
        (meta, query_t, pair_t, grad_t, logs, cosine, sine),
    )


def output_body(places, lines, meta, tokens, mixed, gain, *refs):
    pieces, (total, second, weights_v, sems) = refs[:-4], refs[-4:]
    for copy in load_rows(meta, places, lines, pieces, weights_v, sems, pl.ds(PAIR + 128 + QUERY, weights_v.shape[1])):
        copy.wait()
    value = tokens[...].astype(F32) + mm(mixed[...], weights_v[...])
    total[...] = value
    second[...] = (value * inverse_rms(value) * gain[1:2]).astype(BF)


def output_forward(meta, tokens, mixed, gain, pieces, lines):
    return kernel_call(
        functools.partial(output_body, places_of(pieces), lines),
        (jax.ShapeDtypeStruct(tokens.shape, F32), jax.ShapeDtypeStruct(tokens.shape, BF)),
        [SMEM, VMEM, VMEM, VMEM] + [ANY] * len(pieces),
        (VMEM, VMEM),
        [pltpu.VMEM((QUERY, tokens.shape[1]), BF), copies_of(pieces)],
        2 * tokens.size * QUERY,
        10 << 20,
        (meta, tokens, mixed, gain, *arrays_of(pieces)),
    )


def output_back_body(places, lines, split, meta, grad, total, second_grad, gain, mixed_t, *refs):
    pieces, (first_grad, mixed_grad_t, send, keep, weights_v, da, sems) = refs[:-7], refs[-7:]
    copies = load_rows(meta, places, lines, pieces, weights_v, sems, pl.ds(PAIR + 128 + QUERY, weights_v.shape[1]))
    value = total[...]
    inverse = inverse_rms(value)
    back = second_grad[...]
    scaled = back * gain[1:2]
    first = (
        grad[...].astype(F32)
        + inverse * scaled
        - value * inverse**3 * jnp.mean(scaled * value, axis=-1, keepdims=True)
    )
    first_grad[...] = first
    da[...] = first.astype(BF)
    width = value.shape[1]
    gain_part = jnp.broadcast_to(
        jnp.sum((back * value * inverse).T, axis=1, keepdims=True), (width, 128)
    )
    store_rows(meta, split, gain_part, 0, send, keep, pl.ds(width, 128))
    step = 384
    for n in range(width // step):
        cut = slice(n * step, (n + 1) * step)
        store_rows(meta, split, mm(mixed_t[cut, :], da[...]), n * step, send, keep, pl.ds(0, width))
    for copy in copies:
        copy.wait()
    for n in range(width // step):
        cut = slice(n * step, (n + 1) * step)
        mixed_grad_t[cut, :] = mm_t(weights_v[cut, :], da[...]).astype(BF)


def output_backward(meta, grad, total, second_grad, gain, mixed_t, pieces, parts, split):
    own, width = grad.shape
    return kernel_call(
        functools.partial(output_back_body, places_of(pieces), parts[1], split),
        (
            jax.ShapeDtypeStruct((own, width), F32),
            jax.ShapeDtypeStruct(mixed_t.shape, BF),
            *sums_shapes(split, parts, QUERY, width + 128),
        ),
        [SMEM] + [VMEM] * 5 + [ANY] * len(pieces),
        (VMEM,) * 4,
        [pltpu.VMEM((QUERY, width), BF), pltpu.VMEM((own, width), BF), copies_of(pieces)],
        4 * own * width * QUERY,
        22 << 20,
        (meta, grad, total, second_grad, gain, mixed_t, *arrays_of(pieces)),
    )


def ffn_body(count, *refs):
    second, grads, shards = refs[:count], refs[count : 2 * count], refs[2 * count]
    out_a, out_b, back_a, back_b, hidden_t, gate_t, up_t = refs[2 * count + 1 : 2 * count + 8]
    second_v, grads_v, weights, hidden, gate_g, up_g, sems = refs[2 * count + 8 :]
    rows = second[0].shape[0]
    blocks, units = shards.shape[0], shards.shape[1] // 3
    copies = [
        pltpu.make_async_copy(
            shards.at[b, pl.ds(p * units, units)], weights.at[p, pl.ds(b * units, units)], sems.at[p, b]
        )
        for b in range(blocks)
        for p in range(3)
    ]
    for i in range(count):
        cut = pl.ds(i * rows, rows)
        copies.append(pltpu.make_async_copy(second[i], second_v.at[cut], sems.at[3, i]))
        copies.append(pltpu.make_async_copy(grads[i], grads_v.at[cut], sems.at[4, i]))
    for copy in copies:
        copy.start()
    for copy in copies:
        copy.wait()
    step = 256
    total = blocks * units
    for n in range(total // step):
        cut = slice(n * step, (n + 1) * step)
        gate_w, up_w, down_w = weights[0, cut], weights[1, cut], weights[2, cut]

        def one(m, _):
            here = pl.ds(pl.multiple_of(m * step, step), step)
            gate = mm_t(second_v[here, :], gate_w)
            up = mm_t(second_v[here, :], up_w)
            hidden_grad = mm_t(grads_v[here, :], down_w)
            sigma = jax.nn.sigmoid(gate)
            mixed = gate * sigma * up
            hidden[here, cut] = mixed.astype(BF)
            hidden_t[cut, here] = mixed.T.astype(BF)
            gate_grad = hidden_grad * up * sigma * (1.0 + gate * (1.0 - sigma))
            gate_g[here, cut] = gate_grad.astype(BF)
            gate_t[cut, here] = gate_grad.T.astype(BF)
            up_grad = hidden_grad * (gate * sigma)
            up_g[here, cut] = up_grad.astype(BF)
            up_t[cut, here] = up_grad.T.astype(BF)
            return 0

        lax.fori_loop(0, count * rows // step, one, 0)

    half = count * rows // 2
    for first, out, back in ((0, out_a, back_a), (half, out_b, back_b)):

        def two(m, _):
            to = pl.ds(pl.multiple_of(m * step, step), step)
            here = pl.ds(pl.multiple_of(first + m * step, step), step)
            back[to, :] = (mm(gate_g[here, :], weights[0]) + mm(up_g[here, :], weights[1])).astype(back.dtype)
            out[to, :] = mm(hidden[here, :], weights[2]).astype(out.dtype)
            return 0

        lax.fori_loop(0, half // step, two, 0)


def ffn(tokens_of, weights):
    pieces = len(tokens_of) // 2
    rows, width = tokens_of[0].shape
    count, total = pieces * rows, weights.shape[0] * weights.shape[1] // 3
    sds = jax.ShapeDtypeStruct
    return kernel_call(
        functools.partial(ffn_body, pieces),
        (sds((count // 2, width), BF),) * 4 + (sds((total, count), BF),) * 3,
        [ANY] * (2 * pieces + 1),
        (VMEM,) * 7,
        [
            pltpu.VMEM((count, width), BF), pltpu.VMEM((count, width), BF),
            pltpu.VMEM((3, total, width), BF),
            pltpu.VMEM((count, total), BF), pltpu.VMEM((count, total), BF), pltpu.VMEM((count, total), BF),
            pltpu.SemaphoreType.DMA((5, max(weights.shape[0], pieces))),
        ],
        12 * count * total * width,
        34 << 20,
        (*tokens_of, weights),
    )


def ffn_sums_body(count, units, *refs):
    tokens_of, lefts, out = refs[: 2 * count], refs[2 * count : 2 * count + 3], refs[2 * count + 3]
    second_v, grads_v, sems = refs[2 * count + 4 :]
    rows = tokens_of[0].shape[0]
    copies = []
    for i in range(count):
        cut = pl.ds(i * rows, rows)
        copies.append(pltpu.make_async_copy(tokens_of[i], second_v.at[cut], sems.at[0, i]))
        copies.append(pltpu.make_async_copy(tokens_of[count + i], grads_v.at[cut], sems.at[1, i]))
    for copy in copies:
        copy.start()
    for copy in copies:
        copy.wait()
    for p, right in ((0, second_v), (1, second_v), (2, grads_v)):

        def one(b, _):
            here = pl.ds(pl.multiple_of(b * units, units), units)
            out[b, p * units : (p + 1) * units, :] = mm(lefts[p][here, :], right[...]).astype(BF)
            return 0

        lax.fori_loop(0, out.shape[0], one, 0)


def ffn_sums(hidden_t, gate_t, up_t, tokens_of, units):
    pieces = len(tokens_of) // 2
    rows, width = tokens_of[0].shape
    total = hidden_t.shape[0]
    return kernel_call(
        functools.partial(ffn_sums_body, pieces, units),
        jax.ShapeDtypeStruct((total // units, 3 * units, width), BF),
        [ANY] * (2 * pieces) + [VMEM] * 3,
        VMEM,
        [
            pltpu.VMEM((pieces * rows, width), BF), pltpu.VMEM((pieces * rows, width), BF),
            pltpu.SemaphoreType.DMA((2, pieces)),
        ],
        6 * total * pieces * rows * width,
        22 << 20,
        (*tokens_of, gate_t, up_t, hidden_t),
    )


def project_sums_body(seqs, split, meta, normed_t, query_back, pair_back, send, keep):
    place = meta[0]
    wide = normed_t.shape[1] // seqs
    rows = query_back.shape[1] // seqs
    step = 384
    for n in range(normed_t.shape[0] // step):
        cut = slice(n * step, (n + 1) * step)
        own = jnp.concatenate(
            [normed_t[cut, pl.ds(pl.multiple_of(s * wide + place * rows, 128), rows)] for s in range(seqs)],
            axis=1,
        )
        store_rows(
            meta, split, mm_t(own, query_back[...]), n * step, send, keep, pl.ds(PAIR, QUERY)
        )
        store_rows(
            meta, split, mm_t(normed_t[cut, :], pair_back[...]), n * step, send, keep, pl.ds(0, PAIR)
        )


def project_sums(meta, normed_t, query_back, pair_back, seqs, parts, split):
    width = normed_t.shape[0]
    return kernel_call(
        functools.partial(project_sums_body, seqs, split),
        sums_shapes(split, parts, width, PAIR + QUERY),
        [SMEM, VMEM, VMEM, VMEM],
        (VMEM,) * 2,
        [],
        2 * width * (query_back.size + pair_back.size),
        26 << 20,
        (meta, normed_t, query_back, pair_back),
    )


def project_back_body(seqs, places, lines, meta, query_back, pair_back, *refs):
    count = len(places)
    pieces, refs = refs[:count], refs[count:]
    query_grad, pair_grad, pair_v, query_v, pair_sems, query_sems = refs
    pair_copies = load_rows(meta, places, lines, pieces, pair_v, pair_sems, pl.ds(0, PAIR))
    query_copies = load_rows(meta, places, lines, pieces, query_v, query_sems, pl.ds(PAIR + 128, QUERY))
    blocks, _, own = pair_grad.shape
    rows = own // seqs
    wide = pair_back.shape[1] // seqs
    step = 512
    for copy in pair_copies:
        copy.wait()
    for n in range(pair_v.shape[0] // step):
        cut = slice(n * step, (n + 1) * step)
        for s in range(seqs):
            part = mm(pair_v[cut, :], pair_back[:, s * wide : (s + 1) * wide])
            for z in range(blocks):
                pair_grad[z, cut, s * rows : (s + 1) * rows] = part[:, z * rows : (z + 1) * rows].astype(BF)
    for copy in query_copies:
        copy.wait()
    for n in range(query_v.shape[0] // step):
        cut = slice(n * step, (n + 1) * step)
        query_grad[cut, :] = mm(query_v[cut, :], query_back[...])


def project_back(meta, query_back, pair_back, pieces, lines, width, seqs, blocks):
    own = query_back.shape[1]
    return kernel_call(
        functools.partial(project_back_body, seqs, places_of(pieces), lines),
        (
            jax.ShapeDtypeStruct((width, own), F32),
            jax.ShapeDtypeStruct((blocks, width, own), BF),
        ),
        [SMEM, VMEM, VMEM] + [ANY] * len(pieces),
        (VMEM, VMEM),
        [pltpu.VMEM((width, PAIR), BF), pltpu.VMEM((width, QUERY), BF), copies_of(pieces), copies_of(pieces)],
        2 * width * (query_back.size + pair_back.size),
        20 << 20,
        (meta, query_back, pair_back, *arrays_of(pieces)),
    )


def input_grad_body(tokens, gain, first_grad, query_grad, pair_grad, out):
    back = (query_grad[...] + pair_grad[...].astype(F32)).T
    value = tokens[...].astype(F32)
    inverse = inverse_rms(value)
    scaled = back * gain[0:1]
    out[...] = (
        first_grad[...]
        + inverse * scaled
        - value * inverse**3 * jnp.mean(scaled * value, axis=-1, keepdims=True)
    ).astype(BF)


def input_grad(tokens, gain, first_grad, query_grad, pair_grad):
    return kernel_call(
        input_grad_body,
        jax.ShapeDtypeStruct(tokens.shape, BF),
        [VMEM] * 5,
        VMEM,
        [],
        tokens.size * 20,
        8 << 20,
        (tokens, gain, first_grad, query_grad, pair_grad),
    )


def per_device(
    tokens,
    positions,
    out_grad,
    w_query,
    w_key,
    w_value,
    w_output,
    gain_attn,
    gain_ffn,
    w_gate,
    w_up,
    w_down,
):
    move = Moves()
    Z, Q, step = move.Z, move.Q, move.step
    seqs, rows, width = tokens.shape
    wide = rows * Z
    own_rows = seqs * rows
    pair_width = KV_HEADS * HEAD
    share, units = w_query.shape[0], w_gate.shape[0]
    split = share % 16 == 0
    meta = jnp.stack([move.zi, move.qi, move.xi, move.ci]).astype(jnp.int32)
    near = [(j, i) for j in range(Q) for i in range(2)]
    grad_out = out_grad.reshape(own_rows, width)
    inputs = tokens.reshape(own_rows, width)

    def over_z(value):
        return lax.all_gather(value, "seq", axis=0, tiled=False)

    def sum_z(value):
        return lax.psum_scatter(value, "seq", scatter_dimension=0, tiled=False)

    gains_in = jnp.pad(jnp.stack([gain_attn, gain_ffn], axis=1), ((0, 0), (0, 126)))
    pack = over_z(jnp.concatenate([w_key, w_value, gains_in, w_query, w_output], axis=1))
    places = jnp.stack([positions // 256, positions % 256], axis=-1).astype(BF)
    carried = jnp.concatenate([tokens, jnp.pad(places, ((0, 0), (0, 0), (0, 126)))], axis=-1)
    tokens_all = over_z(carried).transpose(1, 0, 2, 3).reshape(seqs * wide, width + 128)
    places_all = in_f32(tokens_all[:, width]) * 256 + in_f32(tokens_all[:, width + 1])
    cosine, sine = angle_tables(places_all)
    ffn_w = over_z(jnp.concatenate([w_gate, w_up, w_down], axis=0))

    def spread(value):
        pieces = [step((j, i), value) if j or i else value for j, i in near]
        return tuple(pieces) + tuple(step("c", piece) for piece in pieces)

    def blocks_to(value, *held):
        return [after(step((-j % Q, i), value[n].astype(BF)), *held) for n, (j, i) in enumerate(near) if n]

    def total(first, parts):
        for part in parts:
            first = first + in_f32(part)
        return first

    grad_spread = spread(grad_out)
    pack = after(pack, *grad_spread)

    if Q == 2:
        at_x, at_q = step((0, 1), pack), step((1, 0), pack)
        middle = Z // 2
        chips = [
            (pack, 0, 0, 0), (at_x, 0, 1, 0), (at_q, 1, 0, 0),
            (step((0, 1), at_q[:middle]), 1, 1, 0), (step((1, 0), at_x[middle:]), 1, 1, middle),
        ]
    else:
        chips = [(step((j, i), pack) if j or i else pack, j, i, 0) for j, i in near]
    pieces = []
    for array, j, i, z in chips:
        pieces += [(array, j, i, 0, z), (step("c", array), j, i, 1, z)]
    if not split:
        whole = jnp.zeros((Z, Q, 2, 2) + pack.shape[1:], BF)
        for array, j, i, l, z in pieces:
            block = array[:, None, None, None]
            at = (z, (move.qi - j) % Q, (move.xi + i) % 2, (move.ci + l) % 2, 0, 0)
            whole = lax.dynamic_update_slice(whole, block, at)
        pieces = [(whole.reshape(-1, pack.shape[-1]), 0, 0, 0, 0)]

    query_t, pair_t, normed_t, gains = project_forward(
        meta, tokens_all, cosine, sine, pieces, Q, width, seqs, rows
    )
    mixed, mixed_t, logs = attend_forward(meta, query_t, pair_t, seqs)
    first_sum, second = output_forward(meta, inputs, mixed, gains, pieces, Q)

    second_spread = spread(second)
    half = len(near)
    chunks, outs, backs = [], [], []
    for n in range(0, 2 * half, 8):
        tokens_of = second_spread[n : n + 8] + grad_spread[n : n + 8]
        *parts, hidden_t, gate_t, up_t = ffn(tokens_of, ffn_w)
        chunks.append((tokens_of, (hidden_t, gate_t, up_t)))
        outs += parts[:2]
        backs += parts[2:]
    if len(outs) > 2:
        outs = (jnp.concatenate(outs[: len(outs) // 2]), jnp.concatenate(outs[len(outs) // 2 :]))
        backs = (jnp.concatenate(backs[: len(backs) // 2]), jnp.concatenate(backs[len(backs) // 2 :]))

    def own_core(parts):
        other = step("c", parts[1])
        return (in_f32(parts[0]) + in_f32(other)).reshape(half, own_rows, width), other

    back, other = own_core(backs)
    ffn_sum = None
    for tokens_of, made in chunks:
        part = ffn_sums(after(made[0], other), made[1], made[2], tokens_of, units)
        ffn_sum = part if ffn_sum is None else in_f32(ffn_sum) + in_f32(part)
    ffn_sum = ffn_sum.astype(BF)
    grad_ffn = in_f32(sum_z(ffn_sum))
    grad_gate, grad_up, grad_down = grad_ffn[:units], grad_ffn[units : 2 * units], grad_ffn[2 * units :]
    second_grad = total(back[0], blocks_to(back, ffn_sum))

    def pieces_for(send, keep):
        if split:
            return send, keep
        value = keep.reshape(Z, Q, 2, 2, share, keep.shape[-1])

        def cut(c):
            return jnp.stack(
                [
                    lax.dynamic_slice(
                        value,
                        (0, (move.qi - j) % Q, (move.xi + i) % 2, c, 0, 0),
                        (Z, 1, 1, 1, share, keep.shape[-1]),
                    )[:, 0, 0, 0]
                    for j, i in near
                ]
            )

        return cut(1 - move.ci), cut(move.ci)

    first_grad, mixed_grad_t, out_send, out_keep = output_backward(
        meta, grad_out, first_sum, second_grad, gains, mixed_t, pieces, (Z, Q), split
    )
    out_send, out_keep = pieces_for(out_send, out_keep)
    query_back, pair_back = attend_backward(meta, query_t, pair_t, mixed_grad_t, logs, cosine, sine, seqs)
    out_keep = in_f32(out_keep) + in_f32(after(step("c", out_send), query_back))
    send, keep = project_sums(meta, normed_t, query_back, pair_back, seqs, (Z, Q), split)
    send, keep = pieces_for(send, keep)
    query_grad, pair_grad = project_back(
        after(meta, keep), query_back, pair_back, pieces, Q, width, seqs, Z
    )
    out_rows = total(out_keep[0], blocks_to(out_keep, query_grad)).astype(BF)
    keep = in_f32(keep) + in_f32(after(step("c", send), query_grad))
    pair_grad = sum_z(after(pair_grad, grad_gate))
    rows_of = jnp.concatenate([total(keep[0], blocks_to(keep)).astype(BF), out_rows], axis=-1)
    sums = in_f32(sum_z(after(rows_of, pair_grad)))
    in_grad = input_grad(inputs, gains, first_grad, query_grad, pair_grad)
    layer, _ = own_core((outs[0], after(outs[1], keep)))
    layer_out = total(first_sum + layer[0], blocks_to(layer)).astype(BF)

    grad_key, grad_value = sums[:, :pair_width], sums[:, pair_width : 2 * pair_width]
    grad_query = sums[:, 2 * pair_width : 2 * pair_width + QUERY]
    output_sum = sums[:, 2 * pair_width + QUERY :]
    grad_output, grad_gain_ffn = output_sum[:, :width], output_sum[:, width]
    grad_gain_attn = (
        jnp.sum(grad_query * in_f32(w_query), axis=1)
        + jnp.sum(grad_key * in_f32(w_key), axis=1)
        + jnp.sum(grad_value * in_f32(w_value), axis=1)
    ) / in_f32(gain_attn)
    return (
        layer_out.reshape(seqs, rows, width),
        in_grad.reshape(seqs, rows, width),
        grad_query,
        grad_key,
        grad_value,
        grad_output,
        grad_gain_attn,
        grad_gain_ffn,
        grad_gate,
        grad_up,
        grad_down,
    )


def solution(mesh):
    rows = P(("seq", "dp"), None)
    vector = P(("seq", "dp"))
    act = P("dp", "seq", None)
    return jax.shard_map(
        per_device,
        mesh=mesh,
        in_specs=(act, P("dp", "seq"), act, rows, rows, rows, rows, vector, vector, rows, rows, rows),
        out_specs=(act, act, rows, rows, rows, rows, vector, vector, rows, rows, rows),
        check_vma=False,
    )
```

```python
import functools

import jax
import jax.numpy as jnp
from jax import lax
from jax.experimental import pallas as pl
from jax.experimental.pallas import tpu as pltpu
from jax.sharding import PartitionSpec as P

HEADS = 16
KV_HEADS = 8
HEAD = 96
GROUP = HEADS // KV_HEADS

EPS = 1e-05
THETA = 100000.0
NEG = -1e30
BF = jnp.bfloat16
F32 = jnp.float32


def inverse_rms(values):
    return lax.rsqrt(jnp.mean(values * values, axis=-1, keepdims=True) + EPS)


def angle_tables(places):
    offsets = jnp.arange(0, HEAD, 2, dtype=F32)
    angles = (THETA ** (-offsets / HEAD))[:, None] * places.astype(F32)[None, :]
    return (jnp.cos(angles), jnp.sin(angles))


def mm(left, right):
    return jnp.dot(left, right, preferred_element_type=F32)


def mm_t(left, right):
    return lax.dot_general(left, right, (((1,), (1,)), ((), ())), preferred_element_type=F32)


def t_mm(left, right):
    return lax.dot_general(left, right, (((0,), (0,)), ((), ())), preferred_element_type=F32)


def in_f32(value):
    return value.astype(F32)


def after(value, *others):
    return lax.optimization_barrier((value, *others))[0]


class Moves:
    def __init__(self):
        self.Z = lax.axis_size("seq")
        self.DP = lax.axis_size("dp")
        self.Q = self.DP // 4
        self.zi = lax.axis_index("seq")
        place = lax.axis_index("dp")
        self.qi = place // 4
        self.xi = (place // 2) % 2
        self.ci = place % 2

    def around(self, hop, value):
        return lax.ppermute(value, "seq", [(n, (n + hop) % self.Z) for n in range(self.Z)])

    def step(self, offset, value):
        if offset == "c":
            return lax.ppermute(value, "dp", [(n, n ^ 1) for n in range(self.DP)])
        j, i = offset
        return lax.ppermute(
            value, "dp", [(n, (n % 4) ^ (2 * i) | 4 * ((n // 4 + j) % self.Q)) for n in range(self.DP)]
        )


VMEM = pl.BlockSpec(memory_space=pltpu.VMEM)
ANY = pl.BlockSpec(memory_space=pl.ANY)
SMEM = pl.BlockSpec(memory_space=pltpu.SMEM)
SCALE = HEAD ** (-0.5)
HALF = HEAD // 2
QUERY = HEADS * HEAD
PAIR = 2 * KV_HEADS * HEAD


def kernel_call(body, out_shape, in_specs, out_specs, scratch, flops, moved, args):
    return pl.pallas_call(
        body,
        out_shape=out_shape,
        in_specs=in_specs,
        out_specs=out_specs,
        scratch_shapes=scratch,
        compiler_params=pltpu.CompilerParams(vmem_limit_bytes=60 << 20),
        cost_estimate=pl.CostEstimate(flops=flops, bytes_accessed=moved, transcendentals=0),
    )(*args)


def load_rows(meta, places, lines, refs, target, sems, columns):
    copies = []
    if len(refs) == 1:
        copies.append(pltpu.make_async_copy(refs[0].at[:, columns], target, sems.at[0]))
    else:
        zi, qi, xi, ci, count = meta[0], meta[1], meta[2], meta[3], target.shape[0] // (4 * lines * refs[0].shape[1])
        for ref, (j, i, l, first) in zip(refs, places):
            blocks, share, _ = ref.shape
            q = lax.rem(qi + (lines - j), lines)
            x = lax.rem(xi + i, 2)
            c = lax.rem(ci + l, 2)
            for k in range(blocks):
                z = lax.rem(zi + (count - first - k), count) if len(refs) == 10 else first + k
                row = pl.multiple_of((((z * lines + q) * 2 + x) * 2 + c) * share, share)
                copies.append(
                    pltpu.make_async_copy(
                        ref.at[k, :, columns], target.at[pl.ds(row, share), :], sems.at[len(copies)]
                    )
                )
    for copy in copies:
        copy.start()
    return copies


def arrays_of(pieces):
    return [piece[0] for piece in pieces]


def places_of(pieces):
    return tuple(piece[1:] for piece in pieces)


def copies_of(pieces):
    count = 1 if len(pieces) == 1 else sum(piece[0].shape[0] for piece in pieces)
    return pltpu.SemaphoreType.DMA((count,))


def store_rows(meta, split, block, first, send, keep, columns):
    if not split:
        keep[pl.ds(first, block.shape[0]), columns] = block.astype(keep.dtype)
        return
    lines, share = keep.shape[0] // 2, keep.shape[2]
    qi, xi, ci = meta[1], meta[2], meta[3]
    for n in range(block.shape[0] // (2 * share)):
        chip = first // (2 * share) + n
        z, q, x = chip // (2 * lines), chip // 2 % lines, chip % 2
        j = lax.rem(qi + (lines - q), lines)
        i = lax.rem(xi + x, 2)
        even = block[2 * n * share : (2 * n + 1) * share]
        odd = block[(2 * n + 1) * share : (2 * n + 2) * share]
        keep[2 * j + i, z, :, columns] = jnp.where(ci == 0, even, odd).astype(keep.dtype)
        send[2 * j + i, z, :, columns] = jnp.where(ci == 0, odd, even).astype(send.dtype)


def sums_shapes(split, parts, rows, width):
    if not split:
        return (jax.ShapeDtypeStruct((8, 128), BF), jax.ShapeDtypeStruct((rows, width), BF))
    shape = (parts[1] * 2, parts[0], rows // (parts[0] * parts[1] * 4), width)
    return (jax.ShapeDtypeStruct(shape, BF), jax.ShapeDtypeStruct(shape, BF))


def turned_store(ref, row, lanes, block, cosine, sine):
    upper, lower = block[:HALF], block[HALF:]
    ref[pl.ds(row, HALF), lanes] = (upper * cosine - lower * sine).astype(ref.dtype)
    ref[pl.ds(row + HALF, HALF), lanes] = (lower * cosine + upper * sine).astype(ref.dtype)


def head_scores(queries, keys, place, wide):
    scores = mm(keys, queries) * SCALE
    rows = scores.shape[1] // GROUP
    key_place = lax.broadcasted_iota(jnp.int32, scores.shape, 0)
    query_place = place * rows + lax.rem(lax.broadcasted_iota(jnp.int32, scores.shape, 1), rows)
    return jnp.where(key_place <= query_place, scores, NEG)


def group_of(ref, g, lanes):
    return jnp.concatenate(
        [ref[pl.ds(pl.multiple_of((g * GROUP + j) * HEAD, 16), HEAD), lanes] for j in range(GROUP)],
        axis=1,
    )


def flip(value):
    return value.astype(F32).T.astype(value.dtype)


def project_forward_body(seqs, wide, places, lines, meta, tokens, cosine, sine, *refs):
    count = len(places)
    pieces, refs = refs[:count], refs[count:]
    (
        query_t, pair_t, normed_t, gains,
        pair_v, query_v, normed, own, pair_sems, query_sems,
    ) = refs
    place = meta[0]
    rows = own.shape[0] // seqs
    pair_width = KV_HEADS * HEAD
    pair_copies = load_rows(meta, places, lines, pieces, pair_v, pair_sems, pl.ds(0, PAIR + 128))
    query_copies = load_rows(meta, places, lines, pieces, query_v, query_sems, pl.ds(PAIR + 128, QUERY))
    for copy in pair_copies:
        copy.wait()
    gains[...] = pair_v[:, PAIR:].astype(F32).T[:8]
    gain = gains[0:1]
    for s in range(seqs):
        for z in range(wide // rows):
            cut = slice(s * wide + z * rows, s * wide + (z + 1) * rows)
            values = tokens[z, s, :, : normed.shape[1]].astype(F32)
            block = (values * inverse_rms(values) * gain).astype(BF)
            normed[cut, :] = block
            normed_t[:, cut] = flip(block)
    for s in range(seqs):
        own[s * rows : (s + 1) * rows, :] = normed[
            pl.ds(pl.multiple_of(s * wide + place * rows, 128), rows), :
        ]
    width = 4 * HEAD
    for n in range(2 * pair_width // width):
        for s in range(seqs):
            lanes = slice(s * wide, (s + 1) * wide)
            block = mm(normed[lanes, :], pair_v[:, n * width : (n + 1) * width]).T
            if (n + 1) * width <= pair_width:
                for h in range(4):
                    turned_store(
                        pair_t, n * width + h * HEAD, lanes, block[h * HEAD : (h + 1) * HEAD],
                        cosine[:, lanes], sine[:, lanes],
                    )
            else:
                pair_t[n * width : (n + 1) * width, lanes] = block.astype(BF)
    for copy in query_copies:
        copy.wait()
    for n in range(HEADS * HEAD // width):
        block = mm(own[...], query_v[:, n * width : (n + 1) * width]).T
        for s in range(seqs):
            lanes = slice(s * rows, (s + 1) * rows)
            here = pl.ds(pl.multiple_of(s * wide + place * rows, 128), rows)
            for h in range(4):
                turned_store(
                    query_t, n * width + h * HEAD, lanes, block[h * HEAD : (h + 1) * HEAD, lanes],
                    cosine[:, here], sine[:, here],
                )


def attend_forward_body(seqs, wide, meta, query_t, pair_t, mixed, mixed_t, logs):
    place = meta[0]
    rows = query_t.shape[1] // seqs
    pair_width = KV_HEADS * HEAD

    def one(g, _):
        row = pl.multiple_of(g * HEAD, 16)
        for s in range(seqs):
            lanes = slice(s * wide, (s + 1) * wide)
            mine = slice(s * rows, (s + 1) * rows)
            scores = head_scores(
                group_of(query_t, g, mine), flip(pair_t[pl.ds(row, HEAD), lanes]), place, wide
            )
            top = jnp.max(scores, axis=0, keepdims=True)
            weights = jnp.exp(scores - top)
            total = jnp.sum(weights, axis=0, keepdims=True)
            probs = (weights * (1.0 / total)).astype(BF)
            out = mm(pair_t[pl.ds(row + pair_width, HEAD), lanes], probs).astype(BF)
            for j in range(GROUP):
                mixed_t[pl.ds(pl.multiple_of((g * GROUP + j) * HEAD, 16), HEAD), mine] = out[
                    :, j * rows : (j + 1) * rows
                ]
            logs[g, s] = top + jnp.log(total)
        return 0

    lax.fori_loop(0, KV_HEADS, one, 0)
    mixed[...] = flip(mixed_t[...])


def project_forward(meta, tokens, cosine, sine, pieces, lines, width, seqs, rows):
    wide = tokens.shape[0] * rows
    count, own = seqs * wide, seqs * rows
    sds = jax.ShapeDtypeStruct
    return kernel_call(
        functools.partial(project_forward_body, seqs, wide, places_of(pieces), lines),
        (sds((QUERY, own), BF), sds((PAIR, count), BF), sds((width, count), BF), sds((8, width), F32)),
        [SMEM, VMEM, VMEM, VMEM] + [ANY] * len(pieces),
        (VMEM,) * 4,
        [
            pltpu.VMEM((width, PAIR + 128), BF), pltpu.VMEM((width, QUERY), BF),
            pltpu.VMEM((count, width), BF), pltpu.VMEM((own, width), BF), copies_of(pieces), copies_of(pieces),
        ],
        2 * count * width * PAIR + 2 * own * width * QUERY,
        20 << 20,
        (meta, tokens, cosine, sine, *arrays_of(pieces)),
    )


def attend_forward(meta, query_t, pair_t, seqs):
    own = query_t.shape[1]
    wide = pair_t.shape[1] // seqs
    sds = jax.ShapeDtypeStruct
    return kernel_call(
        functools.partial(attend_forward_body, seqs, wide),
        (
            sds((own, QUERY), BF), sds((QUERY, own), BF),
            sds((KV_HEADS, seqs, 1, GROUP * own // seqs), F32),
        ),
        [SMEM, VMEM, VMEM],
        (VMEM,) * 3,
        [],
        4 * own * wide * QUERY,
        6 << 20,
        (meta, query_t, pair_t),
    )


def attend_backward_body(
    seqs, wide, meta, query_t, pair_t, grad_t, logs, cosine, sine, query_back, pair_back
):
    place = meta[0]
    rows = query_t.shape[1] // seqs
    pair_width = KV_HEADS * HEAD

    def one(g, _):
        row = pl.multiple_of(g * HEAD, 16)
        for s in range(seqs):
            lanes = slice(s * wide, (s + 1) * wide)
            mine = slice(s * rows, (s + 1) * rows)
            here = pl.ds(pl.multiple_of(s * wide + place * rows, 128), rows)
            queries = group_of(query_t, g, mine)
            grads = group_of(grad_t, g, mine)
            keys_t = pair_t[pl.ds(row, HEAD), lanes]
            values_t = pair_t[pl.ds(row + pair_width, HEAD), lanes]
            probs = jnp.exp(head_scores(queries, flip(keys_t), place, wide) - logs[g, s])
            prob_grad = mm(flip(values_t), grads)
            centre = jnp.sum(probs * prob_grad, axis=0, keepdims=True)
            score_grad = (probs * (prob_grad - centre)).astype(BF)
            query_grad = mm(keys_t, score_grad) * SCALE
            for j in range(GROUP):
                turned_store(
                    query_back, pl.multiple_of((g * GROUP + j) * HEAD, 16), mine,
                    query_grad[:, j * rows : (j + 1) * rows], cosine[:, here], -sine[:, here],
                )
            turned_store(
                pair_back, row, lanes, mm_t(queries, score_grad) * SCALE,
                cosine[:, lanes], -sine[:, lanes],
            )
            pair_back[pl.ds(row + pair_width, HEAD), lanes] = mm_t(
                grads, probs.astype(BF)
            ).astype(BF)
        return 0

    lax.fori_loop(0, KV_HEADS, one, 0)


def attend_backward(meta, query_t, pair_t, grad_t, logs, cosine, sine, seqs):
    wide = pair_t.shape[1] // seqs
    return kernel_call(
        functools.partial(attend_backward_body, seqs, wide),
        (jax.ShapeDtypeStruct(query_t.shape, BF), jax.ShapeDtypeStruct(pair_t.shape, BF)),
        [SMEM] + [VMEM] * 6,
        (VMEM, VMEM),
        [],
        10**12,
        12 << 20,
        (meta, query_t, pair_t, grad_t, logs, cosine, sine),
    )


def output_body(places, lines, meta, tokens, mixed, gain, *refs):
    pieces, (total, second, weights_v, sems) = refs[:-4], refs[-4:]
    for copy in load_rows(meta, places, lines, pieces, weights_v, sems, pl.ds(0, weights_v.shape[1])):
        copy.wait()
    value = tokens[...].astype(F32) + mm(mixed[...], weights_v[...])
    total[...] = value
    second[...] = (value * inverse_rms(value) * gain[1:2]).astype(BF)


def output_forward(meta, tokens, mixed, gain, pieces, lines):
    return kernel_call(
        functools.partial(output_body, places_of(pieces), lines),
        (jax.ShapeDtypeStruct(tokens.shape, F32), jax.ShapeDtypeStruct(tokens.shape, BF)),
        [SMEM, VMEM, VMEM, VMEM] + [ANY] * len(pieces),
        (VMEM, VMEM),
        [pltpu.VMEM((QUERY, tokens.shape[1]), BF), copies_of(pieces)],
        2 * tokens.size * QUERY,
        10 << 20,
        (meta, tokens, mixed, gain, *arrays_of(pieces)),
    )


def output_back_body(places, lines, split, meta, grad, total, second_grad, gain, mixed_t, *refs):
    pieces, (first_grad, mixed_grad_t, send, keep, weights_v, da, sems) = refs[:-7], refs[-7:]
    copies = load_rows(meta, places, lines, pieces, weights_v, sems, pl.ds(0, weights_v.shape[1]))
    value = total[...]
    inverse = inverse_rms(value)
    back = second_grad[...]
    scaled = back * gain[1:2]
    first = (
        grad[...].astype(F32)
        + inverse * scaled
        - value * inverse**3 * jnp.mean(scaled * value, axis=-1, keepdims=True)
    )
    first_grad[...] = first
    da[...] = first.astype(BF)
    width = value.shape[1]
    gain_part = jnp.broadcast_to(
        jnp.sum((back * value * inverse).T, axis=1, keepdims=True), (width, 128)
    )
    store_rows(meta, split, gain_part, 0, send, keep, pl.ds(width, 128))
    step = 384
    for n in range(width // step):
        cut = slice(n * step, (n + 1) * step)
        store_rows(meta, split, mm(mixed_t[cut, :], da[...]), n * step, send, keep, pl.ds(0, width))
    for copy in copies:
        copy.wait()
    for n in range(width // step):
        cut = slice(n * step, (n + 1) * step)
        mixed_grad_t[cut, :] = mm_t(weights_v[cut, :], da[...]).astype(BF)


def output_backward(meta, grad, total, second_grad, gain, mixed_t, pieces, parts, split):
    own, width = grad.shape
    return kernel_call(
        functools.partial(output_back_body, places_of(pieces), parts[1], split),
        (
            jax.ShapeDtypeStruct((own, width), F32),
            jax.ShapeDtypeStruct(mixed_t.shape, BF),
            *sums_shapes(split, parts, QUERY, width + 128),
        ),
        [SMEM] + [VMEM] * 5 + [ANY] * len(pieces),
        (VMEM,) * 4,
        [pltpu.VMEM((QUERY, width), BF), pltpu.VMEM((own, width), BF), copies_of(pieces)],
        4 * own * width * QUERY,
        22 << 20,
        (meta, grad, total, second_grad, gain, mixed_t, *arrays_of(pieces)),
    )


def ffn_body(count, *refs):
    second, grads, shards = refs[:count], refs[count : 2 * count], refs[2 * count]
    out_a, out_b, back_a, back_b, hidden_t, gate_t, up_t = refs[2 * count + 1 : 2 * count + 8]
    second_v, grads_v, weights, hidden, gate_g, up_g, sems = refs[2 * count + 8 :]
    rows = second[0].shape[0]
    blocks, units = shards.shape[0], shards.shape[1] // 3
    copies = [
        pltpu.make_async_copy(
            shards.at[b, pl.ds(p * units, units)], weights.at[p, pl.ds(b * units, units)], sems.at[p, b]
        )
        for b in range(blocks)
        for p in range(3)
    ]
    for i in range(count):
        cut = pl.ds(i * rows, rows)
        copies.append(pltpu.make_async_copy(second[i], second_v.at[cut], sems.at[3, i]))
        copies.append(pltpu.make_async_copy(grads[i], grads_v.at[cut], sems.at[4, i]))
    for copy in copies:
        copy.start()
    for copy in copies:
        copy.wait()
    step = 256
    total = blocks * units
    for n in range(total // step):
        cut = slice(n * step, (n + 1) * step)
        gate_w, up_w, down_w = weights[0, cut], weights[1, cut], weights[2, cut]

        def one(m, _):
            here = pl.ds(pl.multiple_of(m * step, step), step)
            gate = mm_t(second_v[here, :], gate_w)
            up = mm_t(second_v[here, :], up_w)
            hidden_grad = mm_t(grads_v[here, :], down_w)
            sigma = jax.nn.sigmoid(gate)
            mixed = gate * sigma * up
            hidden[here, cut] = mixed.astype(BF)
            hidden_t[cut, here] = mixed.T.astype(BF)
            gate_grad = hidden_grad * up * sigma * (1.0 + gate * (1.0 - sigma))
            gate_g[here, cut] = gate_grad.astype(BF)
            gate_t[cut, here] = gate_grad.T.astype(BF)
            up_grad = hidden_grad * (gate * sigma)
            up_g[here, cut] = up_grad.astype(BF)
            up_t[cut, here] = up_grad.T.astype(BF)
            return 0

        lax.fori_loop(0, count * rows // step, one, 0)

    half = count * rows // 2
    for first, out, back in ((0, out_a, back_a), (half, out_b, back_b)):

        def two(m, _):
            to = pl.ds(pl.multiple_of(m * step, step), step)
            here = pl.ds(pl.multiple_of(first + m * step, step), step)
            back[to, :] = (mm(gate_g[here, :], weights[0]) + mm(up_g[here, :], weights[1])).astype(back.dtype)
            out[to, :] = mm(hidden[here, :], weights[2]).astype(out.dtype)
            return 0

        lax.fori_loop(0, half // step, two, 0)


def ffn(tokens_of, weights):
    pieces = len(tokens_of) // 2
    rows, width = tokens_of[0].shape
    count, total = pieces * rows, weights.shape[0] * weights.shape[1] // 3
    sds = jax.ShapeDtypeStruct
    return kernel_call(
        functools.partial(ffn_body, pieces),
        (sds((count // 2, width), BF),) * 4 + (sds((total, count), BF),) * 3,
        [ANY] * (2 * pieces + 1),
        (VMEM,) * 7,
        [
            pltpu.VMEM((count, width), BF), pltpu.VMEM((count, width), BF),
            pltpu.VMEM((3, total, width), BF),
            pltpu.VMEM((count, total), BF), pltpu.VMEM((count, total), BF), pltpu.VMEM((count, total), BF),
            pltpu.SemaphoreType.DMA((5, max(weights.shape[0], pieces))),
        ],
        12 * count * total * width,
        34 << 20,
        (*tokens_of, weights),
    )


def ffn_sums_body(count, units, parts, *refs):
    tokens_of, lefts = refs[:count], refs[count : count + len(parts)]
    out, tokens_v, sems = refs[count + len(parts) :]
    rows = tokens_of[0].shape[0]
    copies = [
        pltpu.make_async_copy(tokens_of[i], tokens_v.at[pl.ds(i * rows, rows)], sems.at[i])
        for i in range(count)
    ]
    for copy in copies:
        copy.start()
    for copy in copies:
        copy.wait()
    for n, left in enumerate(lefts):

        def one(b, _):
            here = pl.ds(pl.multiple_of(b * units, units), units)
            out[b, n * units : (n + 1) * units, :] = mm(left[here, :], tokens_v[...]).astype(BF)
            return 0

        lax.fori_loop(0, out.shape[0], one, 0)


def ffn_sums(parts, hidden_t, gate_t, up_t, tokens_of, units, cost):
    pieces = len(tokens_of) // 2
    rows, width = tokens_of[0].shape
    total = hidden_t.shape[0]
    return kernel_call(
        functools.partial(ffn_sums_body, pieces, units, parts),
        jax.ShapeDtypeStruct((total // units, len(parts) * units, width), BF),
        [ANY] * pieces + [VMEM] * len(parts),
        VMEM,
        [pltpu.VMEM((pieces * rows, width), BF), pltpu.SemaphoreType.DMA((pieces,))],
        cost,
        16 << 20,
        (*tokens_of[pieces if parts == (2,) else 0 :][:pieces], *[(gate_t, up_t, hidden_t)[p] for p in parts]),
    )


def project_sums_body(seqs, split, meta, normed_t, query_back, pair_back, send, keep):
    place = meta[0]
    wide = normed_t.shape[1] // seqs
    rows = query_back.shape[1] // seqs
    step = 384
    for n in range(normed_t.shape[0] // step):
        cut = slice(n * step, (n + 1) * step)
        own = jnp.concatenate(
            [normed_t[cut, pl.ds(pl.multiple_of(s * wide + place * rows, 128), rows)] for s in range(seqs)],
            axis=1,
        )
        store_rows(
            meta, split, mm_t(own, query_back[...]), n * step, send, keep, pl.ds(PAIR, QUERY)
        )
        store_rows(
            meta, split, mm_t(normed_t[cut, :], pair_back[...]), n * step, send, keep, pl.ds(0, PAIR)
        )


def project_sums(meta, normed_t, query_back, pair_back, seqs, parts, split):
    width = normed_t.shape[0]
    return kernel_call(
        functools.partial(project_sums_body, seqs, split),
        sums_shapes(split, parts, width, PAIR + QUERY),
        [SMEM, VMEM, VMEM, VMEM],
        (VMEM,) * 2,
        [],
        2 * width * (query_back.size + pair_back.size),
        26 << 20,
        (meta, normed_t, query_back, pair_back),
    )


def project_back_body(seqs, places, lines, meta, query_back, pair_back, *refs):
    count = len(places)
    pieces, refs = refs[:count], refs[count:]
    query_grad, pair_grad, pair_v, query_v, pair_sems, query_sems = refs
    pair_copies = load_rows(meta, places, lines, pieces, pair_v, pair_sems, pl.ds(0, PAIR))
    query_copies = load_rows(meta, places, lines, pieces, query_v, query_sems, pl.ds(PAIR + 128, QUERY))
    blocks, _, own = pair_grad.shape
    rows = own // seqs
    wide = pair_back.shape[1] // seqs
    step = 512
    for copy in pair_copies:
        copy.wait()
    for n in range(pair_v.shape[0] // step):
        cut = slice(n * step, (n + 1) * step)
        for s in range(seqs):
            part = mm(pair_v[cut, :], pair_back[:, s * wide : (s + 1) * wide])
            for z in range(blocks):
                pair_grad[z, cut, s * rows : (s + 1) * rows] = part[:, z * rows : (z + 1) * rows].astype(BF)
    for copy in query_copies:
        copy.wait()
    for n in range(query_v.shape[0] // step):
        cut = slice(n * step, (n + 1) * step)
        query_grad[cut, :] = mm(query_v[cut, :], query_back[...])


def project_back(meta, query_back, pair_back, pieces, lines, width, seqs, blocks):
    own = query_back.shape[1]
    return kernel_call(
        functools.partial(project_back_body, seqs, places_of(pieces), lines),
        (
            jax.ShapeDtypeStruct((width, own), F32),
            jax.ShapeDtypeStruct((blocks, width, own), BF),
        ),
        [SMEM, VMEM, VMEM] + [ANY] * len(pieces),
        (VMEM, VMEM),
        [pltpu.VMEM((width, PAIR), BF), pltpu.VMEM((width, QUERY), BF), copies_of(pieces), copies_of(pieces)],
        1,
        20 << 20,
        (meta, query_back, pair_back, *arrays_of(pieces)),
    )


def input_grad_body(tokens, gain, first_grad, query_grad, pair_grad, out):
    back = (query_grad[...] + pair_grad[...].astype(F32)).T
    value = tokens[...].astype(F32)
    inverse = inverse_rms(value)
    scaled = back * gain[0:1]
    out[...] = (
        first_grad[...]
        + inverse * scaled
        - value * inverse**3 * jnp.mean(scaled * value, axis=-1, keepdims=True)
    ).astype(BF)


def input_grad(tokens, gain, first_grad, query_grad, pair_grad):
    return kernel_call(
        input_grad_body,
        jax.ShapeDtypeStruct(tokens.shape, BF),
        [VMEM] * 5,
        VMEM,
        [],
        tokens.size * 20,
        8 << 20,
        (tokens, gain, first_grad, query_grad, pair_grad),
    )


def per_device(
    tokens,
    positions,
    out_grad,
    w_query,
    w_key,
    w_value,
    w_output,
    gain_attn,
    gain_ffn,
    w_gate,
    w_up,
    w_down,
):
    move = Moves()
    Z, Q, step = move.Z, move.Q, move.step
    seqs, rows, width = tokens.shape
    wide = rows * Z
    own_rows = seqs * rows
    pair_width = KV_HEADS * HEAD
    share, units = w_query.shape[0], w_gate.shape[0]
    split = share % 16 == 0
    meta = jnp.stack([move.zi, move.qi, move.xi, move.ci]).astype(jnp.int32)
    near = [(j, i) for j in range(Q) for i in range(2)]
    rounds = (Z, Q) == (4, 2)
    grad_out = out_grad.reshape(own_rows, width)
    inputs = tokens.reshape(own_rows, width)

    always = lax.optimization_barrier(jnp.ones((), jnp.bool_))

    def window(body, *operands):
        shapes = jax.eval_shape(body, *operands)
        return lax.cond(
            always,
            body,
            lambda *_: jax.tree.map(lambda s: jnp.zeros(s.shape, s.dtype), shapes),
            *operands,
        )

    def over_z(value):
        return lax.all_gather(value, "seq", axis=0, tiled=False)

    def sum_z(value):
        return lax.psum_scatter(value, "seq", scatter_dimension=0, tiled=False)

    gains_in = jnp.pad(jnp.stack([gain_attn, gain_ffn], axis=1), ((0, 0), (0, 126)))
    pack0 = jnp.concatenate([w_key, w_value, gains_in, w_query], axis=1)
    places = jnp.stack([positions // 256, positions % 256], axis=-1).astype(BF)
    carried = jnp.concatenate([tokens, jnp.pad(places, ((0, 0), (0, 0), (0, 126)))], axis=-1)
    ffn_in = jnp.concatenate([w_gate, w_up, w_down], axis=0)
    half = len(near)

    def spread(value):
        return tuple(step((j, i), value) if j or i else value for j, i in near)

    def cores(pieces):
        return tuple(pieces) + tuple(step("c", piece) for piece in pieces)

    def added(own, other):
        sums = [in_f32(own[n]) + in_f32(other[n]) for n in range(len(near))]
        return sums[0], [part.astype(BF) for part in sums[1:]]

    def blocks_to(blocks, *held):
        return [after(step((-j % Q, i), block), *held) for block, (j, i) in zip(blocks, near[1:])]

    def total(first, parts):
        for part in parts:
            first = first + in_f32(part)
        return first

    def chips_of(rows):
        return [(step((j, i), rows) if j or i else rows, j, i, 0) for j, i in near]

    def everywhere(chips):
        found = []
        for array, j, i, z in chips:
            found += [(array, j, i, 0, z), (step("c", array), j, i, 1, z)]
        if split:
            return found
        rows = found[0][0]
        whole = jnp.zeros((Z, Q, 2, 2) + rows.shape[1:], BF)
        for array, j, i, l, z in found:
            for k in range(array.shape[0]):
                at = (z + k, (move.qi - j) % Q, (move.xi + i) % 2, (move.ci + l) % 2, 0, 0)
                whole = lax.dynamic_update_slice(whole, array[k][None, None, None, None], at)
        return [(whole.reshape(-1, rows.shape[-1]), 0, 0, 0, 0)]

    tokens_all = over_z(carried)
    if rounds:
        up, down = move.around(1, pack0), move.around(-1, pack0)
        grad_spread = spread(grad_out)
        ffn_w = over_z(after(ffn_in, up))
        pack = jnp.stack([pack0, up, move.around(1, up), down])
        pack, *grad_spread = lax.optimization_barrier((pack, *grad_spread))

        def round2(pack, output0):
            return (
                step((0, 1), pack), step((1, 0), pack), step("c", pack),
                move.around(1, output0), move.around(-1, output0),
            )

        at_x, at_q, pack_c, output1, output3 = window(round2, pack, w_output)

        def round3(at_x, at_q, output0, output1, output3):
            corner = step((0, 1), at_q[:2]), step((1, 0), at_x[2:])
            cores_of = step("c", at_x), step("c", at_q)
            output2 = move.around(1, output1)
            return corner + cores_of + (jnp.stack([output0, output1, output2, output3]),)

        corner_a, corner_b, at_xc, at_qc, out_pack = window(
            round3, at_x, at_q, w_output, output1, output3
        )
        pieces = [
            (pack, 0, 0, 0, 0), (pack_c, 0, 0, 1, 0), (at_x, 0, 1, 0, 0), (at_xc, 0, 1, 1, 0),
            (at_q, 1, 0, 0, 0), (at_qc, 1, 0, 1, 0),
            (corner_a, 1, 1, 0, 0), (step("c", corner_a), 1, 1, 1, 0),
            (corner_b, 1, 1, 0, 2), (step("c", corner_b), 1, 1, 1, 2),
        ]
    else:
        pack = over_z(pack0)
        grad_spread = spread(grad_out)
        ffn_w = over_z(ffn_in)
        out_pack = over_z(w_output)
        pieces = everywhere(chips_of(pack))

    placed = in_f32(tokens_all[..., width]) * 256 + in_f32(tokens_all[..., width + 1])
    cosine, sine = angle_tables(placed.transpose(1, 0, 2).reshape(seqs * wide))

    if rounds:

        def round4(meta, cosine, sine, out_pack, tokens_all, arrays):
            moved = step((0, 1), out_pack), step((1, 0), out_pack)
            found = [(array,) + piece[1:] for array, piece in zip(arrays, pieces)]
            return moved + tuple(
                project_forward(meta, tokens_all, cosine, sine, found, Q, width, seqs, rows)
            )

        out_x, out_q, query_t, pair_t, normed_t, gains = window(
            round4, meta, cosine, sine, out_pack, tokens_all, arrays_of(pieces)
        )

        def round5(meta, query_t, pair_t, out_pack, out_x, out_q):
            corner = step((0, 1), out_q[:2]), step((1, 0), out_x[2:])
            cores_of = step("c", out_pack), step("c", out_x), step("c", out_q)
            return corner + cores_of + tuple(attend_forward(meta, query_t, pair_t, seqs))

        corner_a, corner_b, out_packc, out_xc, out_qc, mixed, mixed_t, logs = window(
            round5, meta, query_t, pair_t, out_pack, out_x, out_q
        )
        out_pieces = [
            (out_pack, 0, 0, 0, 0), (out_packc, 0, 0, 1, 0), (out_x, 0, 1, 0, 0), (out_xc, 0, 1, 1, 0),
            (out_q, 1, 0, 0, 0), (out_qc, 1, 0, 1, 0),
            (corner_a, 1, 1, 0, 0), (step("c", corner_a), 1, 1, 1, 0),
            (corner_b, 1, 1, 0, 2), (step("c", corner_b), 1, 1, 1, 2),
        ]
    else:
        query_t, pair_t, normed_t, gains = project_forward(
            meta, tokens_all, cosine, sine, pieces, Q, width, seqs, rows
        )
        mixed, mixed_t, logs = attend_forward(meta, query_t, pair_t, seqs)
        out_pieces = everywhere(chips_of(out_pack))
    first_sum, second = output_forward(meta, inputs, mixed, gains, out_pieces, Q)
    grad_spread = cores(tuple(after(piece, mixed) for piece in grad_spread))

    second_spread = cores(spread(second))
    chunks, outs, backs = [], [], []
    for n in range(0, 2 * half, 8):
        tokens_of = second_spread[n : n + 8] + grad_spread[n : n + 8]
        *parts, hidden_t, gate_t, up_t = ffn(tokens_of, ffn_w)
        chunks.append((tokens_of, (hidden_t, gate_t, up_t)))
        outs += parts[:2]
        backs += parts[2:]
    if len(outs) > 2:
        outs = (jnp.concatenate(outs[: len(outs) // 2]), jnp.concatenate(outs[len(outs) // 2 :]))
        backs = (jnp.concatenate(backs[: len(backs) // 2]), jnp.concatenate(backs[len(backs) // 2 :]))

    def joined(parts, other):
        shape = (half, own_rows, width)
        return added(parts[0].reshape(shape), other.reshape(shape))

    def sums_over(parts, tied, cost):
        found = None
        for tokens_of, made in chunks:
            part = ffn_sums(parts, after(made[0], *tied), made[1], made[2], tokens_of, units, cost)
            found = part if found is None else in_f32(found) + in_f32(part)
        return found.astype(BF)

    down_sum = sums_over((2,), (), 10**12)
    second_grad, blocks = joined(backs, after(step("c", backs[1]), down_sum))

    def sums_beside(second_grad, blocks, made):
        moved = blocks_to(blocks)
        gate_sum = None
        for (tokens_of, _), part in zip(chunks, made):
            part = ffn_sums((0, 1), *part, tokens_of, units, 10**12)
            gate_sum = part if gate_sum is None else in_f32(gate_sum) + in_f32(part)
        gate_sum, moved = lax.optimization_barrier((gate_sum.astype(BF), moved))
        return gate_sum, total(second_grad, moved)

    gate_sum, second_grad = window(sums_beside, second_grad, blocks, [made for _, made in chunks])
    grad_down = sum_z(down_sum)
    gate_sum, grad_down = lax.optimization_barrier((gate_sum, grad_down))
    grad_ffn = sum_z(gate_sum)

    def pieces_for(send, keep):
        if split:
            return send, keep
        value = keep.reshape(Z, Q, 2, 2, share, keep.shape[-1])

        def cut(c):
            return jnp.stack(
                [
                    lax.dynamic_slice(
                        value,
                        (0, (move.qi - j) % Q, (move.xi + i) % 2, c, 0, 0),
                        (Z, 1, 1, 1, share, keep.shape[-1]),
                    )[:, 0, 0, 0]
                    for j, i in near
                ]
            )

        return cut(1 - move.ci), cut(move.ci)

    first_grad, mixed_grad_t, out_send, out_keep = output_backward(
        meta, grad_out, first_sum, second_grad, gains, mixed_t, out_pieces, (Z, Q), split
    )
    out_send, out_keep = pieces_for(out_send, out_keep)
    out_send, out_other = lax.optimization_barrier(
        (step("c", out_send), step("c", after(outs[1], out_keep)))
    )
    out_rows, blocks = added(out_keep, out_send)

    def attention_beside(out_rows, blocks, meta, query_t, pair_t, mixed_grad_t, logs, cosine, sine, arrays):
        moved = blocks_to(blocks)
        query_back, pair_back = attend_backward(
            meta, query_t, pair_t, mixed_grad_t, logs, cosine, sine, seqs
        )
        found = [(array,) + piece[1:] for array, piece in zip(arrays, pieces)]
        query_grad, pair_grad = project_back(meta, query_back, pair_back, found, Q, width, seqs, Z)
        query_grad, moved = lax.optimization_barrier((query_grad, moved))
        return total(out_rows, moved).astype(BF), query_back, pair_back, query_grad, pair_grad

    out_rows, query_back, pair_back, query_grad, pair_grad = window(
        attention_beside, out_rows, blocks, meta, query_t, pair_t, mixed_grad_t, logs, cosine, sine,
        arrays_of(pieces),
    )
    send, keep = project_sums(meta, normed_t, query_back, pair_back, seqs, (Z, Q), split)
    send, keep = pieces_for(send, keep)
    grad_ffn, pair_grad = lax.optimization_barrier((grad_ffn, pair_grad))
    pair_grad = sum_z(pair_grad)
    rows_of, blocks = added(keep, step("c", send))
    rows_of = total(rows_of, blocks_to(blocks)).astype(BF)
    layer, blocks = joined((outs[0], None), after(out_other, rows_of))
    layer = total(first_sum + layer, blocks_to(blocks))
    sums = in_f32(sum_z(after(jnp.concatenate([rows_of, out_rows], axis=-1), pair_grad)))
    layer_out = layer.astype(BF)
    in_grad = input_grad(inputs, gains, first_grad, query_grad, pair_grad)
    grad_ffn, grad_down = in_f32(grad_ffn), in_f32(grad_down)
    grad_gate, grad_up = grad_ffn[:units], grad_ffn[units:]

    grad_key, grad_value = sums[:, :pair_width], sums[:, pair_width : 2 * pair_width]
    grad_query = sums[:, 2 * pair_width : 2 * pair_width + QUERY]
    output_sum = sums[:, 2 * pair_width + QUERY :]
    grad_output, grad_gain_ffn = output_sum[:, :width], output_sum[:, width]
    grad_gain_attn = (
        jnp.sum(grad_query * in_f32(w_query), axis=1)
        + jnp.sum(grad_key * in_f32(w_key), axis=1)
        + jnp.sum(grad_value * in_f32(w_value), axis=1)
    ) / in_f32(gain_attn)
    return (
        layer_out.reshape(seqs, rows, width),
        in_grad.reshape(seqs, rows, width),
        grad_query,
        grad_key,
        grad_value,
        grad_output,
        grad_gain_attn,
        grad_gain_ffn,
        grad_gate,
        grad_up,
        grad_down,
    )


def solution(mesh):
    rows = P(("seq", "dp"), None)
    vector = P(("seq", "dp"))
    act = P("dp", "seq", None)
    return jax.shard_map(
        per_device,
        mesh=mesh,
        in_specs=(act, P("dp", "seq"), act, rows, rows, rows, rows, vector, vector, rows, rows, rows),
        out_specs=(act, act, rows, rows, rows, rows, vector, vector, rows, rows, rows),
        check_vma=False,
    )
```

```python
import functools

import jax
import jax.numpy as jnp
from jax import lax
from jax.experimental import pallas as pl
from jax.experimental.pallas import tpu as pltpu
from jax.sharding import PartitionSpec as P

HEADS = 16
KV_HEADS = 8
HEAD = 96
GROUP = HEADS // KV_HEADS

EPS = 1e-05
THETA = 100000.0
NEG = -1e30
BF = jnp.bfloat16
F32 = jnp.float32


def inverse_rms(values):
    return lax.rsqrt(jnp.mean(values * values, axis=-1, keepdims=True) + EPS)


def angle_tables(places):
    offsets = jnp.arange(0, HEAD, 2, dtype=F32)
    angles = (THETA ** (-offsets / HEAD))[:, None] * places.astype(F32)[None, :]
    return (jnp.cos(angles), jnp.sin(angles))


def mm(left, right):
    return jnp.dot(left, right, preferred_element_type=F32)


def mm_t(left, right):
    return lax.dot_general(left, right, (((1,), (1,)), ((), ())), preferred_element_type=F32)


def t_mm(left, right):
    return lax.dot_general(left, right, (((0,), (0,)), ((), ())), preferred_element_type=F32)


def in_f32(value):
    return value.astype(F32)


def after(value, *others):
    return lax.optimization_barrier((value, *others))[0]


class Moves:
    def __init__(self):
        self.Z = lax.axis_size("seq")
        self.DP = lax.axis_size("dp")
        self.Q = self.DP // 4
        self.zi = lax.axis_index("seq")
        place = lax.axis_index("dp")
        self.qi = place // 4
        self.xi = (place // 2) % 2
        self.ci = place % 2

    def around(self, hop, value):
        return lax.ppermute(value, "seq", [(n, (n + hop) % self.Z) for n in range(self.Z)])

    def step(self, offset, value):
        if offset == "c":
            return lax.ppermute(value, "dp", [(n, n ^ 1) for n in range(self.DP)])
        j, i = offset
        return lax.ppermute(
            value, "dp", [(n, (n % 4) ^ (2 * i) | 4 * ((n // 4 + j) % self.Q)) for n in range(self.DP)]
        )


VMEM = pl.BlockSpec(memory_space=pltpu.VMEM)
ANY = pl.BlockSpec(memory_space=pl.ANY)
SMEM = pl.BlockSpec(memory_space=pltpu.SMEM)
SCALE = HEAD ** (-0.5)
HALF = HEAD // 2
QUERY = HEADS * HEAD
PAIR = 2 * KV_HEADS * HEAD


def kernel_call(body, out_shape, in_specs, out_specs, scratch, flops, moved, args):
    return pl.pallas_call(
        body,
        out_shape=out_shape,
        in_specs=in_specs,
        out_specs=out_specs,
        scratch_shapes=scratch,
        compiler_params=pltpu.CompilerParams(vmem_limit_bytes=60 << 20),
        cost_estimate=pl.CostEstimate(flops=flops, bytes_accessed=moved, transcendentals=0),
    )(*args)


def load_rows(meta, places, lines, refs, target, sems, columns):
    copies = []
    if len(refs) == 1:
        copies.append(pltpu.make_async_copy(refs[0].at[:, columns], target, sems.at[0]))
    else:
        zi, qi, xi, ci, count = meta[0], meta[1], meta[2], meta[3], target.shape[0] // (4 * lines * refs[0].shape[1])
        for ref, (j, i, l, first) in zip(refs, places):
            blocks, share, _ = ref.shape
            q = lax.rem(qi + (lines - j), lines)
            x = lax.rem(xi + i, 2)
            c = lax.rem(ci + l, 2)
            for k in range(blocks):
                z = lax.rem(zi + (count - first - k), count) if len(refs) == 10 else first + k
                row = pl.multiple_of((((z * lines + q) * 2 + x) * 2 + c) * share, share)
                copies.append(
                    pltpu.make_async_copy(
                        ref.at[k, :, columns], target.at[pl.ds(row, share), :], sems.at[len(copies)]
                    )
                )
    for copy in copies:
        copy.start()
    return copies


def arrays_of(pieces):
    return [piece[0] for piece in pieces]


def places_of(pieces):
    return tuple(piece[1:] for piece in pieces)


def copies_of(pieces):
    count = 1 if len(pieces) == 1 else sum(piece[0].shape[0] for piece in pieces)
    return pltpu.SemaphoreType.DMA((count,))


def store_rows(meta, split, block, first, send, keep, columns):
    if not split:
        keep[pl.ds(first, block.shape[0]), columns] = block.astype(keep.dtype)
        return
    lines, share = keep.shape[0] // 2, keep.shape[2]
    qi, xi, ci = meta[1], meta[2], meta[3]
    for n in range(block.shape[0] // (2 * share)):
        chip = first // (2 * share) + n
        z, q, x = chip // (2 * lines), chip // 2 % lines, chip % 2
        j = lax.rem(qi + (lines - q), lines)
        i = lax.rem(xi + x, 2)
        even = block[2 * n * share : (2 * n + 1) * share]
        odd = block[(2 * n + 1) * share : (2 * n + 2) * share]
        keep[2 * j + i, z, :, columns] = jnp.where(ci == 0, even, odd).astype(keep.dtype)
        send[2 * j + i, z, :, columns] = jnp.where(ci == 0, odd, even).astype(send.dtype)


def sums_shapes(split, parts, rows, width):
    if not split:
        return (jax.ShapeDtypeStruct((8, 128), BF), jax.ShapeDtypeStruct((rows, width), BF))
    shape = (parts[1] * 2, parts[0], rows // (parts[0] * parts[1] * 4), width)
    return (jax.ShapeDtypeStruct(shape, BF), jax.ShapeDtypeStruct(shape, BF))


def turned_store(ref, row, lanes, block, cosine, sine):
    upper, lower = block[:HALF], block[HALF:]
    ref[pl.ds(row, HALF), lanes] = (upper * cosine - lower * sine).astype(ref.dtype)
    ref[pl.ds(row + HALF, HALF), lanes] = (lower * cosine + upper * sine).astype(ref.dtype)


def head_scores(queries, keys, place, wide):
    scores = mm(keys, queries) * SCALE
    rows = scores.shape[1] // GROUP
    key_place = lax.broadcasted_iota(jnp.int32, scores.shape, 0)
    query_place = place * rows + lax.rem(lax.broadcasted_iota(jnp.int32, scores.shape, 1), rows)
    return jnp.where(key_place <= query_place, scores, NEG)


def group_of(ref, g, lanes):
    return jnp.concatenate(
        [ref[pl.ds(pl.multiple_of((g * GROUP + j) * HEAD, 16), HEAD), lanes] for j in range(GROUP)],
        axis=1,
    )


def flip(value):
    return value.astype(F32).T.astype(value.dtype)


def project_forward_body(seqs, wide, places, lines, meta, tokens, cosine, sine, *refs):
    count = len(places)
    pieces, refs = refs[:count], refs[count:]
    (
        query_t, pair_t, normed_t, gains,
        pair_v, query_v, gains_v, normed, own, pair_sems, query_sems, gain_sems,
    ) = refs
    place = meta[0]
    rows = own.shape[0] // seqs
    pair_width = KV_HEADS * HEAD
    gain_copies = load_rows(meta, places, lines, pieces, gains_v, gain_sems, pl.ds(PAIR, 128))
    pair_copies = load_rows(meta, places, lines, pieces, pair_v, pair_sems, pl.ds(0, PAIR))
    query_copies = load_rows(meta, places, lines, pieces, query_v, query_sems, pl.ds(PAIR + 128, QUERY))
    for copy in gain_copies:
        copy.wait()
    gains[...] = gains_v[...].astype(F32).T[:8]
    gain = gains[0:1]
    for s in range(seqs):
        for z in range(wide // rows):
            cut = slice(s * wide + z * rows, s * wide + (z + 1) * rows)
            values = tokens[z, s].astype(F32)
            block = (values * inverse_rms(values) * gain).astype(BF)
            normed[cut, :] = block
            normed_t[:, cut] = flip(block)
    for s in range(seqs):
        own[s * rows : (s + 1) * rows, :] = normed[
            pl.ds(pl.multiple_of(s * wide + place * rows, 128), rows), :
        ]
    for copy in pair_copies:
        copy.wait()
    heads = 8
    width = heads * HEAD
    for n in range(2 * pair_width // width):
        for s in range(seqs):
            lanes = slice(s * wide, (s + 1) * wide)
            block = mm(normed[lanes, :], pair_v[:, n * width : (n + 1) * width]).T
            if (n + 1) * width <= pair_width:
                for h in range(heads):
                    turned_store(
                        pair_t, n * width + h * HEAD, lanes, block[h * HEAD : (h + 1) * HEAD],
                        cosine[:, lanes], sine[:, lanes],
                    )
            else:
                pair_t[n * width : (n + 1) * width, lanes] = block.astype(BF)
    for copy in query_copies:
        copy.wait()
    for n in range(HEADS * HEAD // width):
        block = mm(own[...], query_v[:, n * width : (n + 1) * width]).T
        for s in range(seqs):
            lanes = slice(s * rows, (s + 1) * rows)
            here = pl.ds(pl.multiple_of(s * wide + place * rows, 128), rows)
            for h in range(heads):
                turned_store(
                    query_t, n * width + h * HEAD, lanes, block[h * HEAD : (h + 1) * HEAD, lanes],
                    cosine[:, here], sine[:, here],
                )


def attend_forward_body(seqs, wide, meta, query_t, pair_t, mixed, mixed_t, logs):
    place = meta[0]
    rows = query_t.shape[1] // seqs
    pair_width = KV_HEADS * HEAD

    def one(g, _):
        row = pl.multiple_of(g * HEAD, 16)
        for s in range(seqs):
            lanes = slice(s * wide, (s + 1) * wide)
            mine = slice(s * rows, (s + 1) * rows)
            scores = head_scores(
                group_of(query_t, g, mine), flip(pair_t[pl.ds(row, HEAD), lanes]), place, wide
            )
            top = jnp.max(scores, axis=0, keepdims=True)
            weights = jnp.exp(scores - top)
            total = jnp.sum(weights, axis=0, keepdims=True)
            probs = (weights * (1.0 / total)).astype(BF)
            out = mm(pair_t[pl.ds(row + pair_width, HEAD), lanes], probs).astype(BF)
            for j in range(GROUP):
                mixed_t[pl.ds(pl.multiple_of((g * GROUP + j) * HEAD, 16), HEAD), mine] = out[
                    :, j * rows : (j + 1) * rows
                ]
            logs[g, s] = top + jnp.log(total)
        return 0

    lax.fori_loop(0, KV_HEADS, one, 0)
    mixed[...] = flip(mixed_t[...])


def project_forward(meta, tokens, cosine, sine, pieces, lines, width, seqs, rows):
    wide = tokens.shape[0] * rows
    count, own = seqs * wide, seqs * rows
    sds = jax.ShapeDtypeStruct
    return kernel_call(
        functools.partial(project_forward_body, seqs, wide, places_of(pieces), lines),
        (sds((QUERY, own), BF), sds((PAIR, count), BF), sds((width, count), BF), sds((8, width), F32)),
        [SMEM, VMEM, VMEM, VMEM] + [ANY] * len(pieces),
        (VMEM,) * 4,
        [
            pltpu.VMEM((width, PAIR), BF), pltpu.VMEM((width, QUERY), BF), pltpu.VMEM((width, 128), BF),
            pltpu.VMEM((count, width), BF), pltpu.VMEM((own, width), BF),
            copies_of(pieces), copies_of(pieces), copies_of(pieces),
        ],
        2 * count * width * PAIR + 2 * own * width * QUERY,
        20 << 20,
        (meta, tokens, cosine, sine, *arrays_of(pieces)),
    )


def attend_forward(meta, query_t, pair_t, seqs):
    own = query_t.shape[1]
    wide = pair_t.shape[1] // seqs
    sds = jax.ShapeDtypeStruct
    return kernel_call(
        functools.partial(attend_forward_body, seqs, wide),
        (
            sds((own, QUERY), BF), sds((QUERY, own), BF),
            sds((KV_HEADS, seqs, 1, GROUP * own // seqs), F32),
        ),
        [SMEM, VMEM, VMEM],
        (VMEM,) * 3,
        [],
        4 * own * wide * QUERY,
        6 << 20,
        (meta, query_t, pair_t),
    )


def attend_backward_body(
    seqs, wide, meta, query_t, pair_t, grad_t, logs, cosine, sine, query_back, pair_back, pair_blocks
):
    place = meta[0]
    rows = query_t.shape[1] // seqs
    pair_width = KV_HEADS * HEAD

    def one(g, _):
        row = pl.multiple_of(g * HEAD, 16)
        for s in range(seqs):
            lanes = slice(s * wide, (s + 1) * wide)
            mine = slice(s * rows, (s + 1) * rows)
            here = pl.ds(pl.multiple_of(s * wide + place * rows, 128), rows)
            queries = group_of(query_t, g, mine)
            grads = group_of(grad_t, g, mine)
            keys_t = pair_t[pl.ds(row, HEAD), lanes]
            values_t = pair_t[pl.ds(row + pair_width, HEAD), lanes]
            probs = jnp.exp(head_scores(queries, flip(keys_t), place, wide) - logs[g, s])
            prob_grad = mm(flip(values_t), grads)
            centre = jnp.sum(probs * prob_grad, axis=0, keepdims=True)
            score_grad = (probs * (prob_grad - centre)).astype(BF)
            query_grad = mm(keys_t, score_grad) * SCALE
            for j in range(GROUP):
                turned_store(
                    query_back, pl.multiple_of((g * GROUP + j) * HEAD, 16), mine,
                    query_grad[:, j * rows : (j + 1) * rows], cosine[:, here], -sine[:, here],
                )
            turned_store(
                pair_back, row, lanes, mm_t(queries, score_grad) * SCALE,
                cosine[:, lanes], -sine[:, lanes],
            )
            pair_back[pl.ds(row + pair_width, HEAD), lanes] = mm_t(
                grads, probs.astype(BF)
            ).astype(BF)
            for z in range(wide // rows):
                from_z = slice(s * wide + z * rows, s * wide + (z + 1) * rows)
                for first in (row, row + pair_width):
                    pair_blocks[z, pl.ds(first, HEAD), mine] = pair_back[pl.ds(first, HEAD), from_z]
        return 0

    lax.fori_loop(0, KV_HEADS, one, 0)


def attend_backward(meta, query_t, pair_t, grad_t, logs, cosine, sine, seqs):
    wide = pair_t.shape[1] // seqs
    return kernel_call(
        functools.partial(attend_backward_body, seqs, wide),
        (
            jax.ShapeDtypeStruct(query_t.shape, BF),
            jax.ShapeDtypeStruct(pair_t.shape, BF),
            jax.ShapeDtypeStruct((pair_t.shape[1] // query_t.shape[1], PAIR, query_t.shape[1]), BF),
        ),
        [SMEM] + [VMEM] * 6,
        (VMEM,) * 3,
        [],
        10**12,
        12 << 20,
        (meta, query_t, pair_t, grad_t, logs, cosine, sine),
    )


def output_body(places, lines, meta, tokens, mixed, gain, *refs):
    pieces, (total, second, weights_v, sems) = refs[:-4], refs[-4:]
    for copy in load_rows(meta, places, lines, pieces, weights_v, sems, pl.ds(0, weights_v.shape[1])):
        copy.wait()
    value = tokens[...].astype(F32) + mm(mixed[...], weights_v[...])
    total[...] = value
    second[...] = (value * inverse_rms(value) * gain[1:2]).astype(BF)


def output_forward(meta, tokens, mixed, gain, pieces, lines):
    return kernel_call(
        functools.partial(output_body, places_of(pieces), lines),
        (jax.ShapeDtypeStruct(tokens.shape, F32), jax.ShapeDtypeStruct(tokens.shape, BF)),
        [SMEM, VMEM, VMEM, VMEM] + [ANY] * len(pieces),
        (VMEM, VMEM),
        [pltpu.VMEM((QUERY, tokens.shape[1]), BF), copies_of(pieces)],
        2 * tokens.size * QUERY,
        10 << 20,
        (meta, tokens, mixed, gain, *arrays_of(pieces)),
    )


def output_back_body(places, lines, split, meta, grad, total, second_grad, gain, mixed_t, *refs):
    pieces, (first_grad, mixed_grad_t, send, keep, weights_v, da, sems) = refs[:-7], refs[-7:]
    copies = load_rows(meta, places, lines, pieces, weights_v, sems, pl.ds(0, weights_v.shape[1]))
    value = total[...]
    inverse = inverse_rms(value)
    back = second_grad[...]
    scaled = back * gain[1:2]
    first = (
        grad[...].astype(F32)
        + inverse * scaled
        - value * inverse**3 * jnp.mean(scaled * value, axis=-1, keepdims=True)
    )
    first_grad[...] = first
    da[...] = first.astype(BF)
    width = value.shape[1]
    gain_part = jnp.broadcast_to(
        jnp.sum((back * value * inverse).T, axis=1, keepdims=True), (width, 128)
    )
    store_rows(meta, split, gain_part, 0, send, keep, pl.ds(width, 128))
    step = 384
    for n in range(width // step):
        cut = slice(n * step, (n + 1) * step)
        store_rows(meta, split, mm(mixed_t[cut, :], da[...]), n * step, send, keep, pl.ds(0, width))
    for copy in copies:
        copy.wait()
    for n in range(width // step):
        cut = slice(n * step, (n + 1) * step)
        mixed_grad_t[cut, :] = mm_t(weights_v[cut, :], da[...]).astype(BF)


def output_backward(meta, grad, total, second_grad, gain, mixed_t, pieces, parts, split):
    own, width = grad.shape
    return kernel_call(
        functools.partial(output_back_body, places_of(pieces), parts[1], split),
        (
            jax.ShapeDtypeStruct((own, width), F32),
            jax.ShapeDtypeStruct(mixed_t.shape, BF),
            *sums_shapes(split, parts, QUERY, width + 128),
        ),
        [SMEM] + [VMEM] * 5 + [ANY] * len(pieces),
        (VMEM,) * 4,
        [pltpu.VMEM((QUERY, width), BF), pltpu.VMEM((own, width), BF), copies_of(pieces)],
        4 * own * width * QUERY,
        22 << 20,
        (meta, grad, total, second_grad, gain, mixed_t, *arrays_of(pieces)),
    )


def ffn_body(count, *refs):
    second, grads, shards = refs[:count], refs[count : 2 * count], refs[2 * count]
    out_a, out_b, back_a, back_b, sums = refs[2 * count + 1 : 2 * count + 6]
    (
        second_v, grads_v, weights, hidden, gate_g, up_g, hidden_t, gate_t, up_t, sums_v, sems, row_sems, sum_sem,
    ) = refs[2 * count + 6 :]
    rows = second[0].shape[0]
    blocks, units = shards.shape[0], shards.shape[1] // 3
    weight_copies = [
        pltpu.make_async_copy(
            shards.at[b, pl.ds(p * units, units)], weights.at[p, pl.ds(b * units, units)], sems.at[p, b]
        )
        for p in range(3)
        for b in range(blocks)
    ]
    for copy in weight_copies:
        copy.start()
    for i in range(count):
        cut = pl.ds(i * rows, rows)
        pltpu.make_async_copy(second[i], second_v.at[cut], sems.at[3, i]).start()
        pltpu.make_async_copy(grads[i], grads_v.at[cut], sems.at[4, i]).start()
    for copy in weight_copies:
        copy.wait()
    per = 2
    step = per * rows

    def one(m, _):
        here = pl.ds(pl.multiple_of(m * step, step), step)
        for i in range(per):
            cut = pl.ds(pl.multiple_of((m * per + i) * rows, rows), rows)
            pltpu.make_async_copy(second_v.at[cut], second_v.at[cut], sems.at[3, m * per + i]).wait()
            pltpu.make_async_copy(grads_v.at[cut], grads_v.at[cut], sems.at[4, m * per + i]).wait()
        gate = mm_t(second_v[here, :], weights[0])
        up = mm_t(second_v[here, :], weights[1])
        hidden_grad = mm_t(grads_v[here, :], weights[2])
        sigma = jax.nn.sigmoid(gate)
        silu = gate * sigma
        mixed = silu * up
        hidden[here, :] = mixed.astype(BF)
        hidden_t[:, here] = mixed.T.astype(BF)
        gate_grad = hidden_grad * up * (sigma + silu * (1.0 - sigma))
        gate_g[here, :] = gate_grad.astype(BF)
        gate_t[:, here] = gate_grad.T.astype(BF)
        up_grad = hidden_grad * silu
        up_g[here, :] = up_grad.astype(BF)
        up_t[:, here] = up_grad.T.astype(BF)
        return 0

    lax.fori_loop(0, count // per, one, 0)

    width = second_v.shape[1]
    for n, (left, right) in enumerate(((gate_t, second_v), (up_t, second_v), (hidden_t, grads_v))):
        for c in range(width // step):
            cut = slice(c * step, (c + 1) * step)
            part = mm(left[...], right[:, cut]).astype(BF)
            for b in range(blocks):
                sums_v[b, n * units : (n + 1) * units, cut] = part[b * units : (b + 1) * units]
    sum_copy = pltpu.make_async_copy(sums_v, sums, sum_sem)
    sum_copy.start()

    half = count * rows // 2
    copies = []
    for n, (kind, first, target) in enumerate(
        (("b", half, back_b), ("b", 0, back_a), ("o", half, out_b), ("o", 0, out_a))
    ):
        place = second_v if kind == "b" else grads_v
        for k in range(half // step):
            here = slice(first + k * step, first + (k + 1) * step)
            if kind == "b":
                value = mm(gate_g[here, :], weights[0]) + mm(up_g[here, :], weights[1])
            else:
                value = mm(hidden[here, :], weights[2])
            place[here, :] = value.astype(BF)
            copies.append(
                pltpu.make_async_copy(
                    place.at[pl.ds(first + k * step, step)],
                    target.at[pl.ds(k * step, step)],
                    row_sems.at[n, k],
                )
            )
            copies[-1].start()
    sum_copy.wait()
    for copy in copies:
        copy.wait()


def ffn(tokens_of, weights):
    pieces = len(tokens_of) // 2
    rows, width = tokens_of[0].shape
    count, total = pieces * rows, weights.shape[0] * weights.shape[1] // 3
    sds = jax.ShapeDtypeStruct
    return kernel_call(
        functools.partial(ffn_body, pieces),
        (sds((count // 2, width), BF),) * 4 + (sds(weights.shape, BF),),
        [ANY] * (2 * pieces + 1),
        (ANY,) * 5,
        [
            pltpu.VMEM((count, width), BF), pltpu.VMEM((count, width), BF),
            pltpu.VMEM((3, total, width), BF),
            pltpu.VMEM((count, total), BF), pltpu.VMEM((count, total), BF), pltpu.VMEM((count, total), BF),
            pltpu.VMEM((total, count), BF), pltpu.VMEM((total, count), BF), pltpu.VMEM((total, count), BF),
            pltpu.VMEM(weights.shape, BF),
            pltpu.SemaphoreType.DMA((5, max(weights.shape[0], pieces))),
            pltpu.SemaphoreType.DMA((4, max(count // 2 // (2 * rows), 1))),
            pltpu.SemaphoreType.DMA,
        ],
        18 * count * total * width,
        34 << 20,
        (*tokens_of, weights),
    )


def project_sums_body(seqs, split, meta, normed_t, query_back, pair_back, send, keep):
    place = meta[0]
    wide = normed_t.shape[1] // seqs
    rows = query_back.shape[1] // seqs
    step = 384
    for n in range(normed_t.shape[0] // step):
        cut = slice(n * step, (n + 1) * step)
        own = jnp.concatenate(
            [normed_t[cut, pl.ds(pl.multiple_of(s * wide + place * rows, 128), rows)] for s in range(seqs)],
            axis=1,
        )
        store_rows(
            meta, split, mm_t(own, query_back[...]), n * step, send, keep, pl.ds(PAIR, QUERY)
        )
        store_rows(
            meta, split, mm_t(normed_t[cut, :], pair_back[...]), n * step, send, keep, pl.ds(0, PAIR)
        )


def project_sums(meta, normed_t, query_back, pair_back, seqs, parts, split):
    width = normed_t.shape[0]
    return kernel_call(
        functools.partial(project_sums_body, seqs, split),
        sums_shapes(split, parts, width, PAIR + QUERY),
        [SMEM, VMEM, VMEM, VMEM],
        (VMEM,) * 2,
        [],
        1,
        26 << 20,
        (meta, normed_t, query_back, pair_back),
    )


def input_grad_body(places, lines, meta, tokens, gain, first_grad, query_back, pair_back, *refs):
    pieces, (out, pair_v, query_v, pair_sems, query_sems) = refs[: len(places)], refs[len(places) :]
    query_copies = load_rows(meta, places, lines, pieces, query_v, query_sems, pl.ds(PAIR + 128, QUERY))
    pair_copies = load_rows(meta, places, lines, pieces, pair_v, pair_sems, pl.ds(0, PAIR))
    for copy in query_copies:
        copy.wait()
    back = mm(query_v[...], query_back[...])
    for copy in pair_copies:
        copy.wait()
    back = (back + mm(pair_v[...], pair_back[...])).T
    value = tokens[...].astype(F32)
    inverse = inverse_rms(value)
    scaled = back * gain[0:1]
    out[...] = (
        first_grad[...]
        + inverse * scaled
        - value * inverse**3 * jnp.mean(scaled * value, axis=-1, keepdims=True)
    ).astype(BF)


def input_grad(meta, tokens, gain, first_grad, query_back, pair_back, pieces, lines):
    width = tokens.shape[1]
    return kernel_call(
        functools.partial(input_grad_body, places_of(pieces), lines),
        jax.ShapeDtypeStruct(tokens.shape, BF),
        [SMEM] + [VMEM] * 5 + [ANY] * len(pieces),
        VMEM,
        [
            pltpu.VMEM((width, PAIR), BF), pltpu.VMEM((width, QUERY), BF), copies_of(pieces), copies_of(pieces),
        ],
        2 * width * (query_back.size + pair_back.size),
        14 << 20,
        (meta, tokens, gain, first_grad, query_back, pair_back, *arrays_of(pieces)),
    )


def per_device(
    tokens,
    positions,
    out_grad,
    w_query,
    w_key,
    w_value,
    w_output,
    gain_attn,
    gain_ffn,
    w_gate,
    w_up,
    w_down,
):
    move = Moves()
    Z, Q, step = move.Z, move.Q, move.step
    seqs, rows, width = tokens.shape
    wide = rows * Z
    own_rows = seqs * rows
    pair_width = KV_HEADS * HEAD
    share, units = w_query.shape[0], w_gate.shape[0]
    split = share % 16 == 0
    meta = jnp.stack([move.zi, move.qi, move.xi, move.ci]).astype(jnp.int32)
    near = [(j, i) for j in range(Q) for i in range(2)]
    rounds = (Z, Q) == (4, 2)
    grad_out = out_grad.reshape(own_rows, width)
    inputs = tokens.reshape(own_rows, width)

    always = lax.optimization_barrier(jnp.ones((), jnp.bool_))

    def window(body, *operands):
        shapes = jax.eval_shape(body, *operands)
        return lax.cond(
            always,
            body,
            lambda *_: jax.tree.map(lambda s: jnp.zeros(s.shape, s.dtype), shapes),
            *operands,
        )

    def over_z(value):
        return lax.all_gather(value, "seq", axis=0, tiled=False)

    def sum_z(value):
        return lax.psum_scatter(value, "seq", scatter_dimension=0, tiled=False)

    columns = -(-own_rows // share)
    spots = jnp.pad(positions.reshape(own_rows), (0, columns * share - own_rows)).reshape(share, columns)
    gains_in = jnp.concatenate(
        [gain_attn[:, None], gain_ffn[:, None], (spots // 256).astype(BF), (spots % 256).astype(BF)], axis=1
    )
    gains_in = jnp.pad(gains_in, ((0, 0), (0, 126 - 2 * columns)))
    pack0 = jnp.concatenate([w_key, w_value, gains_in, w_query], axis=1)
    ffn_in = jnp.concatenate([w_gate, w_up, w_down], axis=0)
    half = len(near)

    def spread(value):
        return tuple(step((j, i), value) if j or i else value for j, i in near)

    def cores(pieces):
        return tuple(pieces) + tuple(step("c", piece) for piece in pieces)

    def to_send(own, other):
        return [(in_f32(own[n]) + in_f32(other[n])).astype(BF) for n in range(1, half)]

    def halves(parts):
        return [part.reshape(half, own_rows, width) for part in parts]

    def blocks_to(blocks, *held):
        return [after(step((-j % Q, i), block), *held) for block, (j, i) in zip(blocks, near[1:])]

    def total(first, parts):
        for part in parts:
            first = first + in_f32(part)
        return first

    def chips_of(rows):
        return [(step((j, i), rows) if j or i else rows, j, i, 0) for j, i in near]

    def everywhere(chips):
        found = []
        for array, j, i, z in chips:
            found += [(array, j, i, 0, z), (step("c", array), j, i, 1, z)]
        if split:
            return found
        rows = found[0][0]
        whole = jnp.zeros((Z, Q, 2, 2) + rows.shape[1:], BF)
        for array, j, i, l, z in found:
            for k in range(array.shape[0]):
                at = (z + k, (move.qi - j) % Q, (move.xi + i) % 2, (move.ci + l) % 2, 0, 0)
                whole = lax.dynamic_update_slice(whole, array[k][None, None, None, None], at)
        return [(whole.reshape(-1, rows.shape[-1]), 0, 0, 0, 0)]

    if rounds:
        def round0(pack0, grad_out):
            return (
                move.around(1, pack0), move.around(-1, pack0), step((0, 1), grad_out), step((1, 0), grad_out)
            )

        up, down, grad_x, grad_q = window(round0, pack0, grad_out)
        carried, ffn_in, up, down = lax.optimization_barrier((tokens, ffn_in, up, down))
        tokens_all = over_z(carried)
        ffn_w = over_z(ffn_in)

        def round1(pack0, up, down, grad_x, grad_q):
            middle = own_rows // 2
            far = move.around(1, up)
            corner = step((0, 1), grad_q[:middle]), step((1, 0), grad_x[middle:])
            return jnp.stack([pack0, up, far, down]), jnp.concatenate(corner)

        pack, grad_xq = window(round1, pack0, up, down, grad_x, grad_q)
        grad_spread = (grad_out, grad_x, grad_q, grad_xq)

        def round2(pack, output0):
            return (
                step((0, 1), pack), step((1, 0), pack), step("c", pack),
                move.around(1, output0), move.around(-1, output0),
            )

        at_x, at_q, pack_c, output1, output3 = window(round2, pack, w_output)

        def round3(at_x, at_q, output0, output1, output3):
            corner = step((0, 1), at_q[:2]), step((1, 0), at_x[2:])
            cores_of = step("c", at_x), step("c", at_q)
            output2 = move.around(1, output1)
            return corner + cores_of + (jnp.stack([output0, output1, output2, output3]),)

        corner_a, corner_b, at_xc, at_qc, out_pack = window(
            round3, at_x, at_q, w_output, output1, output3
        )
        pieces = [
            (pack, 0, 0, 0, 0), (pack_c, 0, 0, 1, 0), (at_x, 0, 1, 0, 0), (at_xc, 0, 1, 1, 0),
            (at_q, 1, 0, 0, 0), (at_qc, 1, 0, 1, 0),
            (corner_a, 1, 1, 0, 0), (step("c", corner_a), 1, 1, 1, 0),
            (corner_b, 1, 1, 0, 2), (step("c", corner_b), 1, 1, 1, 2),
        ]
    else:
        tokens_all = over_z(tokens)
        pack = over_z(pack0)
        grad_spread = spread(grad_out)
        ffn_w = over_z(ffn_in)
        out_pack = over_z(w_output)
        pieces = everywhere(chips_of(pack))

    spots = in_f32(pack[:, :, 2 * pair_width + 2 : 2 * pair_width + 2 + 2 * columns])
    spots = (spots[..., :columns] * 256 + spots[..., columns:]).reshape(Z, -1)[:, :own_rows]
    if rounds:
        order = (move.zi - jnp.arange(Z)) % Z
        spots = jnp.sum(jnp.where((order[:, None] == jnp.arange(Z)[None])[..., None], spots[None], 0), axis=1)
    cosine, sine = angle_tables(
        spots.reshape(Z, seqs, rows).transpose(1, 0, 2).reshape(seqs * wide)
    )

    if rounds:

        def round4(meta, cosine, sine, out_pack, tokens_all, arrays):
            moved = step((0, 1), out_pack), step((1, 0), out_pack)
            found = [(array,) + piece[1:] for array, piece in zip(arrays, pieces)]
            return moved + tuple(
                project_forward(meta, tokens_all, cosine, sine, found, Q, width, seqs, rows)
            )

        out_x, out_q, query_t, pair_t, normed_t, gains = window(
            round4, meta, cosine, sine, out_pack, tokens_all, arrays_of(pieces)
        )

        def round5(meta, query_t, pair_t, out_pack, out_x, out_q):
            corner = step((0, 1), out_q[:2]), step((1, 0), out_x[2:])
            cores_of = step("c", out_pack), step("c", out_x), step("c", out_q)
            return corner + cores_of + tuple(attend_forward(meta, query_t, pair_t, seqs))

        corner_a, corner_b, out_packc, out_xc, out_qc, mixed, mixed_t, logs = window(
            round5, meta, query_t, pair_t, out_pack, out_x, out_q
        )
        out_pieces = [
            (out_pack, 0, 0, 0, 0), (out_packc, 0, 0, 1, 0), (out_x, 0, 1, 0, 0), (out_xc, 0, 1, 1, 0),
            (out_q, 1, 0, 0, 0), (out_qc, 1, 0, 1, 0),
            (corner_a, 1, 1, 0, 0), (step("c", corner_a), 1, 1, 1, 0),
            (corner_b, 1, 1, 0, 2), (step("c", corner_b), 1, 1, 1, 2),
        ]
    else:
        query_t, pair_t, normed_t, gains = project_forward(
            meta, tokens_all, cosine, sine, pieces, Q, width, seqs, rows
        )
        mixed, mixed_t, logs = attend_forward(meta, query_t, pair_t, seqs)
        out_pieces = everywhere(chips_of(out_pack))
    first_sum, second = output_forward(meta, inputs, mixed, gains, out_pieces, Q)
    grad_spread = cores(tuple(after(piece, mixed) for piece in grad_spread))

    second_spread = cores(spread(second))
    outs, backs, ffn_sum = [], [], None
    for n in range(0, 2 * half, 8):
        *parts, sums = ffn(second_spread[n : n + 8] + grad_spread[n : n + 8], ffn_w)
        outs += parts[:2]
        backs += parts[2:]
        ffn_sum = sums if ffn_sum is None else in_f32(ffn_sum) + in_f32(sums)
    if len(outs) > 2:
        outs = (jnp.concatenate(outs[: len(outs) // 2]), jnp.concatenate(outs[len(outs) // 2 :]))
        backs = (jnp.concatenate(backs[: len(backs) // 2]), jnp.concatenate(backs[len(backs) // 2 :]))
    grad_ffn = sum_z(ffn_sum.astype(BF))
    back, other = halves((backs[0], step("c", backs[1])))

    def second_round(first, second, blocks, out):
        moved, out = lax.optimization_barrier((blocks_to(blocks), step("c", out)))
        return total(in_f32(first) + in_f32(second), moved), out

    second_grad, out_other = window(second_round, back[0], other[0], to_send(back, other), outs[1])

    def pieces_for(send, keep):
        if split:
            return send, keep
        value = keep.reshape(Z, Q, 2, 2, share, keep.shape[-1])

        def cut(c):
            return jnp.stack(
                [
                    lax.dynamic_slice(
                        value,
                        (0, (move.qi - j) % Q, (move.xi + i) % 2, c, 0, 0),
                        (Z, 1, 1, 1, share, keep.shape[-1]),
                    )[:, 0, 0, 0]
                    for j, i in near
                ]
            )

        return cut(1 - move.ci), cut(move.ci)

    first_grad, mixed_grad_t, out_send, out_keep = output_backward(
        meta, grad_out, first_sum, second_grad, gains, mixed_t, out_pieces, (Z, Q), split
    )
    out_send, out_keep = pieces_for(out_send, out_keep)
    out_send = step("c", out_send)
    blocks = to_send(out_keep, out_send)

    def attention_beside(first, second, blocks, meta, query_t, pair_t, mixed_grad_t, logs, cosine, sine, normed_t):
        moved = blocks_to(blocks)
        query_back, pair_back, pair_blocks = attend_backward(
            meta, query_t, pair_t, mixed_grad_t, logs, cosine, sine, seqs
        )
        send, keep = project_sums(meta, normed_t, query_back, pair_back, seqs, (Z, Q), split)
        keep, moved = lax.optimization_barrier((keep, moved))
        out_rows = total(in_f32(first) + in_f32(second), moved).astype(BF)
        return out_rows, query_back, pair_blocks, send, keep

    out_rows, query_back, pair_blocks, send, keep = window(
        attention_beside, out_keep[0], out_send[0], blocks, meta, query_t, pair_t, mixed_grad_t, logs,
        cosine, sine, normed_t,
    )
    grad_ffn, pair_blocks = lax.optimization_barrier((grad_ffn, pair_blocks))
    pair_own = sum_z(pair_blocks)
    send, keep = pieces_for(send, keep)
    send = step("c", send)
    rows_of = total(in_f32(keep[0]) + in_f32(send[0]), blocks_to(to_send(keep, send))).astype(BF)
    out, out_other = halves((outs[0], out_other))
    blocks = [after(block, rows_of) for block in to_send(out, out_other)]
    rows_of, pair_own = lax.optimization_barrier((jnp.concatenate([rows_of, out_rows], axis=-1), pair_own))
    sums = in_f32(sum_z(rows_of))
    in_grad = input_grad(meta, inputs, gains, first_grad, query_back, pair_own, pieces, Q)
    layer = total(first_sum + in_f32(out[0]) + in_f32(out_other[0]), blocks_to(blocks, in_grad))
    layer_out = layer.astype(BF)
    grad_ffn = in_f32(grad_ffn)
    grad_gate, grad_up, grad_down = grad_ffn[:units], grad_ffn[units : 2 * units], grad_ffn[2 * units :]

    grad_key, grad_value = sums[:, :pair_width], sums[:, pair_width : 2 * pair_width]
    grad_query = sums[:, 2 * pair_width : 2 * pair_width + QUERY]
    output_sum = sums[:, 2 * pair_width + QUERY :]
    grad_output, grad_gain_ffn = output_sum[:, :width], output_sum[:, width]
    grad_gain_attn = (
        jnp.sum(grad_query * in_f32(w_query), axis=1)
        + jnp.sum(grad_key * in_f32(w_key), axis=1)
        + jnp.sum(grad_value * in_f32(w_value), axis=1)
    ) / in_f32(gain_attn)
    return (
        layer_out.reshape(seqs, rows, width),
        in_grad.reshape(seqs, rows, width),
        grad_query,
        grad_key,
        grad_value,
        grad_output,
        grad_gain_attn,
        grad_gain_ffn,
        grad_gate,
        grad_up,
        grad_down,
    )


def solution(mesh):
    rows = P(("seq", "dp"), None)
    vector = P(("seq", "dp"))
    act = P("dp", "seq", None)
    return jax.shard_map(
        per_device,
        mesh=mesh,
        in_specs=(act, P("dp", "seq"), act, rows, rows, rows, rows, vector, vector, rows, rows, rows),
        out_specs=(act, act, rows, rows, rows, rows, vector, vector, rows, rows, rows),
        check_vma=False,
    )
```

```python
import functools

import jax
import jax.numpy as jnp
from jax import lax
from jax.experimental import pallas as pl
from jax.experimental.pallas import tpu as pltpu
from jax.sharding import PartitionSpec as P

HEADS = 16
KV_HEADS = 8
HEAD = 96
GROUP = HEADS // KV_HEADS

EPS = 1e-05
THETA = 100000.0
NEG = -1e30
BF = jnp.bfloat16
F32 = jnp.float32


def inverse_rms(values):
    return lax.rsqrt(jnp.mean(values * values, axis=-1, keepdims=True) + EPS)


def angle_tables(places):
    offsets = jnp.arange(0, HEAD, 2, dtype=F32)
    angles = (THETA ** (-offsets / HEAD))[:, None] * places.astype(F32)[None, :]
    return (jnp.cos(angles), jnp.sin(angles))


def mm(left, right):
    return jnp.dot(left, right, preferred_element_type=F32)


def mm_t(left, right):
    return lax.dot_general(left, right, (((1,), (1,)), ((), ())), preferred_element_type=F32)


def t_mm(left, right):
    return lax.dot_general(left, right, (((0,), (0,)), ((), ())), preferred_element_type=F32)


def in_f32(value):
    return value.astype(F32)


def after(value, *others):
    return lax.optimization_barrier((value, *others))[0]


class Moves:
    def __init__(self):
        self.Z = lax.axis_size("seq")
        self.DP = lax.axis_size("dp")
        self.Q = self.DP // 4
        self.zi = lax.axis_index("seq")
        place = lax.axis_index("dp")
        self.qi = place // 4
        self.xi = (place // 2) % 2
        self.ci = place % 2

    def around(self, hop, value):
        return lax.ppermute(value, "seq", [(n, (n + hop) % self.Z) for n in range(self.Z)])

    def step(self, offset, value):
        if offset == "c":
            return lax.ppermute(value, "dp", [(n, n ^ 1) for n in range(self.DP)])
        j, i = offset
        return lax.ppermute(
            value, "dp", [(n, (n % 4) ^ (2 * i) | 4 * ((n // 4 + j) % self.Q)) for n in range(self.DP)]
        )


VMEM = pl.BlockSpec(memory_space=pltpu.VMEM)
ANY = pl.BlockSpec(memory_space=pl.ANY)
SMEM = pl.BlockSpec(memory_space=pltpu.SMEM)
SCALE = HEAD ** (-0.5)
HALF = HEAD // 2
QUERY = HEADS * HEAD
PAIR = 2 * KV_HEADS * HEAD


def kernel_call(body, out_shape, in_specs, out_specs, scratch, flops, moved, args):
    return pl.pallas_call(
        body,
        out_shape=out_shape,
        in_specs=in_specs,
        out_specs=out_specs,
        scratch_shapes=scratch,
        compiler_params=pltpu.CompilerParams(vmem_limit_bytes=60 << 20),
        cost_estimate=pl.CostEstimate(flops=flops, bytes_accessed=moved, transcendentals=0),
    )(*args)


def load_rows(meta, places, lines, refs, target, sems, columns):
    copies = []
    if len(refs) == 1:
        copies.append(pltpu.make_async_copy(refs[0].at[:, columns], target, sems.at[0]))
    else:
        zi, qi, xi, ci, count = meta[0], meta[1], meta[2], meta[3], target.shape[0] // (4 * lines * refs[0].shape[1])
        for ref, (j, i, l, first) in zip(refs, places):
            blocks, share, _ = ref.shape
            q = lax.rem(qi + (lines - j), lines)
            x = lax.rem(xi + i, 2)
            c = lax.rem(ci + l, 2)
            for k in range(blocks):
                z = lax.rem(zi + (count - first - k), count) if len(refs) == 10 else first + k
                row = pl.multiple_of((((z * lines + q) * 2 + x) * 2 + c) * share, share)
                copies.append(
                    pltpu.make_async_copy(
                        ref.at[k, :, columns], target.at[pl.ds(row, share), :], sems.at[len(copies)]
                    )
                )
    for copy in copies:
        copy.start()
    return copies


def arrays_of(pieces):
    return [piece[0] for piece in pieces]


def places_of(pieces):
    return tuple(piece[1:] for piece in pieces)


def copies_of(pieces):
    count = 1 if len(pieces) == 1 else sum(piece[0].shape[0] for piece in pieces)
    return pltpu.SemaphoreType.DMA((count,))


def store_rows(meta, split, block, first, send, keep, columns):
    if not split:
        keep[pl.ds(first, block.shape[0]), columns] = block.astype(keep.dtype)
        return
    lines, share = keep.shape[0] // 2, keep.shape[2]
    qi, xi, ci = meta[1], meta[2], meta[3]
    for n in range(block.shape[0] // (2 * share)):
        chip = first // (2 * share) + n
        z, q, x = chip // (2 * lines), chip // 2 % lines, chip % 2
        j = lax.rem(qi + (lines - q), lines)
        i = lax.rem(xi + x, 2)
        even = block[2 * n * share : (2 * n + 1) * share]
        odd = block[(2 * n + 1) * share : (2 * n + 2) * share]
        keep[2 * j + i, z, :, columns] = jnp.where(ci == 0, even, odd).astype(keep.dtype)
        send[2 * j + i, z, :, columns] = jnp.where(ci == 0, odd, even).astype(send.dtype)


def sums_shapes(split, parts, rows, width):
    if not split:
        return (jax.ShapeDtypeStruct((8, 128), BF), jax.ShapeDtypeStruct((rows, width), BF))
    shape = (parts[1] * 2, parts[0], rows // (parts[0] * parts[1] * 4), width)
    return (jax.ShapeDtypeStruct(shape, BF), jax.ShapeDtypeStruct(shape, BF))


def turned_store(ref, row, lanes, block, cosine, sine):
    upper, lower = block[:HALF], block[HALF:]
    ref[pl.ds(row, HALF), lanes] = (upper * cosine - lower * sine).astype(ref.dtype)
    ref[pl.ds(row + HALF, HALF), lanes] = (lower * cosine + upper * sine).astype(ref.dtype)


def head_scores(queries, keys, place, wide):
    scores = mm(keys, queries) * SCALE
    rows = scores.shape[1] // GROUP
    key_place = lax.broadcasted_iota(jnp.int32, scores.shape, 0)
    query_place = place * rows + lax.rem(lax.broadcasted_iota(jnp.int32, scores.shape, 1), rows)
    return jnp.where(key_place <= query_place, scores, NEG)


def group_of(ref, g, lanes):
    return jnp.concatenate(
        [ref[pl.ds(pl.multiple_of((g * GROUP + j) * HEAD, 16), HEAD), lanes] for j in range(GROUP)],
        axis=1,
    )


def flip(value):
    return value.astype(F32).T.astype(value.dtype)


def project_forward_body(seqs, wide, places, lines, meta, tokens, cosine, sine, *refs):
    count = len(places)
    pieces, refs = refs[:count], refs[count:]
    (
        query_t, pair_t, normed_t, gains,
        pair_v, query_v, gains_v, normed, own, pair_sems, query_sems, gain_sems,
    ) = refs
    place = meta[0]
    rows = own.shape[0] // seqs
    pair_width = KV_HEADS * HEAD
    gain_copies = load_rows(meta, places, lines, pieces, gains_v, gain_sems, pl.ds(PAIR, 128))
    pair_copies = load_rows(meta, places, lines, pieces, pair_v, pair_sems, pl.ds(0, PAIR))
    query_copies = load_rows(meta, places, lines, pieces, query_v, query_sems, pl.ds(PAIR + 128, QUERY))
    for copy in gain_copies:
        copy.wait()
    gains[...] = gains_v[...].astype(F32).T[:8]
    gain = gains[0:1]
    for s in range(seqs):
        for z in range(wide // rows):
            cut = slice(s * wide + z * rows, s * wide + (z + 1) * rows)
            values = tokens[z, s].astype(F32)
            block = (values * inverse_rms(values) * gain).astype(BF)
            normed[cut, :] = block
            normed_t[:, cut] = flip(block)
    for s in range(seqs):
        own[s * rows : (s + 1) * rows, :] = normed[
            pl.ds(pl.multiple_of(s * wide + place * rows, 128), rows), :
        ]
    for copy in pair_copies:
        copy.wait()
    heads = 8
    width = heads * HEAD
    for n in range(2 * pair_width // width):
        for s in range(seqs):
            lanes = slice(s * wide, (s + 1) * wide)
            block = mm(normed[lanes, :], pair_v[:, n * width : (n + 1) * width]).T
            if (n + 1) * width <= pair_width:
                for h in range(heads):
                    turned_store(
                        pair_t, n * width + h * HEAD, lanes, block[h * HEAD : (h + 1) * HEAD],
                        cosine[:, lanes], sine[:, lanes],
                    )
            else:
                pair_t[n * width : (n + 1) * width, lanes] = block.astype(BF)
    for copy in query_copies:
        copy.wait()
    for n in range(HEADS * HEAD // width):
        block = mm(own[...], query_v[:, n * width : (n + 1) * width]).T
        for s in range(seqs):
            lanes = slice(s * rows, (s + 1) * rows)
            here = pl.ds(pl.multiple_of(s * wide + place * rows, 128), rows)
            for h in range(heads):
                turned_store(
                    query_t, n * width + h * HEAD, lanes, block[h * HEAD : (h + 1) * HEAD, lanes],
                    cosine[:, here], sine[:, here],
                )


def attend_forward_body(seqs, wide, meta, query_t, pair_t, mixed, mixed_t, logs):
    place = meta[0]
    rows = query_t.shape[1] // seqs
    pair_width = KV_HEADS * HEAD

    def one(g, _):
        row = pl.multiple_of(g * HEAD, 16)
        for s in range(seqs):
            lanes = slice(s * wide, (s + 1) * wide)
            mine = slice(s * rows, (s + 1) * rows)
            scores = head_scores(
                group_of(query_t, g, mine), flip(pair_t[pl.ds(row, HEAD), lanes]), place, wide
            )
            top = jnp.max(scores, axis=0, keepdims=True)
            weights = jnp.exp(scores - top)
            total = jnp.sum(weights, axis=0, keepdims=True)
            probs = (weights * (1.0 / total)).astype(BF)
            out = mm(pair_t[pl.ds(row + pair_width, HEAD), lanes], probs).astype(BF)
            for j in range(GROUP):
                mixed_t[pl.ds(pl.multiple_of((g * GROUP + j) * HEAD, 16), HEAD), mine] = out[
                    :, j * rows : (j + 1) * rows
                ]
            logs[g, s] = top + jnp.log(total)
        return 0

    lax.fori_loop(0, KV_HEADS, one, 0)
    mixed[...] = flip(mixed_t[...])


def project_forward(meta, tokens, cosine, sine, pieces, lines, width, seqs, rows):
    wide = tokens.shape[0] * rows
    count, own = seqs * wide, seqs * rows
    sds = jax.ShapeDtypeStruct
    return kernel_call(
        functools.partial(project_forward_body, seqs, wide, places_of(pieces), lines),
        (sds((QUERY, own), BF), sds((PAIR, count), BF), sds((width, count), BF), sds((8, width), F32)),
        [SMEM, VMEM, VMEM, VMEM] + [ANY] * len(pieces),
        (VMEM,) * 4,
        [
            pltpu.VMEM((width, PAIR), BF), pltpu.VMEM((width, QUERY), BF), pltpu.VMEM((width, 128), BF),
            pltpu.VMEM((count, width), BF), pltpu.VMEM((own, width), BF),
            copies_of(pieces), copies_of(pieces), copies_of(pieces),
        ],
        2 * count * width * PAIR + 2 * own * width * QUERY,
        20 << 20,
        (meta, tokens, cosine, sine, *arrays_of(pieces)),
    )


def attend_forward(meta, query_t, pair_t, seqs):
    own = query_t.shape[1]
    wide = pair_t.shape[1] // seqs
    sds = jax.ShapeDtypeStruct
    return kernel_call(
        functools.partial(attend_forward_body, seqs, wide),
        (
            sds((own, QUERY), BF), sds((QUERY, own), BF),
            sds((KV_HEADS, seqs, 1, GROUP * own // seqs), F32),
        ),
        [SMEM, VMEM, VMEM],
        (VMEM,) * 3,
        [],
        4 * own * wide * QUERY,
        6 << 20,
        (meta, query_t, pair_t),
    )


def attend_backward_body(
    seqs, wide, meta, query_t, pair_t, grad_t, logs, cosine, sine, query_back, pair_back, pair_blocks
):
    place = meta[0]
    rows = query_t.shape[1] // seqs
    pair_width = KV_HEADS * HEAD

    def one(g, _):
        row = pl.multiple_of(g * HEAD, 16)
        for s in range(seqs):
            lanes = slice(s * wide, (s + 1) * wide)
            mine = slice(s * rows, (s + 1) * rows)
            here = pl.ds(pl.multiple_of(s * wide + place * rows, 128), rows)
            queries = group_of(query_t, g, mine)
            grads = group_of(grad_t, g, mine)
            keys_t = pair_t[pl.ds(row, HEAD), lanes]
            values_t = pair_t[pl.ds(row + pair_width, HEAD), lanes]
            probs = jnp.exp(head_scores(queries, flip(keys_t), place, wide) - logs[g, s])
            prob_grad = mm(flip(values_t), grads)
            centre = jnp.sum(probs * prob_grad, axis=0, keepdims=True)
            score_grad = (probs * (prob_grad - centre)).astype(BF)
            query_grad = mm(keys_t, score_grad) * SCALE
            for j in range(GROUP):
                turned_store(
                    query_back, pl.multiple_of((g * GROUP + j) * HEAD, 16), mine,
                    query_grad[:, j * rows : (j + 1) * rows], cosine[:, here], -sine[:, here],
                )
            turned_store(
                pair_back, row, lanes, mm_t(queries, score_grad) * SCALE,
                cosine[:, lanes], -sine[:, lanes],
            )
            pair_back[pl.ds(row + pair_width, HEAD), lanes] = mm_t(
                grads, probs.astype(BF)
            ).astype(BF)
            for z in range(wide // rows):
                from_z = slice(s * wide + z * rows, s * wide + (z + 1) * rows)
                for first in (row, row + pair_width):
                    pair_blocks[z, pl.ds(first, HEAD), mine] = pair_back[pl.ds(first, HEAD), from_z]
        return 0

    lax.fori_loop(0, KV_HEADS, one, 0)


def attend_backward(meta, query_t, pair_t, grad_t, logs, cosine, sine, seqs):
    wide = pair_t.shape[1] // seqs
    return kernel_call(
        functools.partial(attend_backward_body, seqs, wide),
        (
            jax.ShapeDtypeStruct(query_t.shape, BF),
            jax.ShapeDtypeStruct(pair_t.shape, BF),
            jax.ShapeDtypeStruct((pair_t.shape[1] // query_t.shape[1], PAIR, query_t.shape[1]), BF),
        ),
        [SMEM] + [VMEM] * 6,
        (VMEM,) * 3,
        [],
        10**12,
        12 << 20,
        (meta, query_t, pair_t, grad_t, logs, cosine, sine),
    )


def output_body(places, lines, meta, tokens, mixed, gain, *refs):
    pieces, (total, second, weights_v, sems) = refs[:-4], refs[-4:]
    for copy in load_rows(meta, places, lines, pieces, weights_v, sems, pl.ds(0, weights_v.shape[1])):
        copy.wait()
    value = tokens[...].astype(F32) + mm(mixed[...], weights_v[...])
    total[...] = value
    second[...] = (value * inverse_rms(value) * gain[1:2]).astype(BF)


def output_forward(meta, tokens, mixed, gain, pieces, lines):
    return kernel_call(
        functools.partial(output_body, places_of(pieces), lines),
        (jax.ShapeDtypeStruct(tokens.shape, F32), jax.ShapeDtypeStruct(tokens.shape, BF)),
        [SMEM, VMEM, VMEM, VMEM] + [ANY] * len(pieces),
        (VMEM, VMEM),
        [pltpu.VMEM((QUERY, tokens.shape[1]), BF), copies_of(pieces)],
        2 * tokens.size * QUERY,
        10 << 20,
        (meta, tokens, mixed, gain, *arrays_of(pieces)),
    )


def output_back_body(split, grad, total, second_grad, gain, mixed_t, meta, first_grad, da, send, keep):
    value = total[...]
    inverse = inverse_rms(value)
    back = second_grad[...]
    scaled = back * gain[1:2]
    first = (
        grad[...].astype(F32)
        + inverse * scaled
        - value * inverse**3 * jnp.mean(scaled * value, axis=-1, keepdims=True)
    )
    first_grad[...] = first
    da[...] = first.astype(BF)
    width = value.shape[1]
    gain_part = jnp.broadcast_to(
        jnp.sum((back * value * inverse).T, axis=1, keepdims=True), (width, 128)
    )
    store_rows(meta, split, gain_part, 0, send, keep, pl.ds(width, 128))
    step = 384
    for n in range(width // step):
        cut = slice(n * step, (n + 1) * step)
        store_rows(meta, split, mm(mixed_t[cut, :], da[...]), n * step, send, keep, pl.ds(0, width))


def output_backward(grad, total, second_grad, gain, mixed_t, meta, parts, split):
    own, width = grad.shape
    return kernel_call(
        functools.partial(output_back_body, split),
        (
            jax.ShapeDtypeStruct((own, width), F32),
            jax.ShapeDtypeStruct((own, width), BF),
            *sums_shapes(split, parts, QUERY, width + 128),
        ),
        [VMEM] * 5 + [SMEM],
        (VMEM,) * 4,
        [],
        2 * own * width * QUERY,
        14 << 20,
        (grad, total, second_grad, gain, mixed_t, meta),
    )


def mixed_back_body(places, lines, meta, da, *refs):
    pieces, (mixed_grad_t, weights_v, sems) = refs[:-3], refs[-3:]
    for copy in load_rows(meta, places, lines, pieces, weights_v, sems, pl.ds(0, weights_v.shape[1])):
        copy.wait()
    step = 384
    for n in range(weights_v.shape[0] // step):
        cut = slice(n * step, (n + 1) * step)
        mixed_grad_t[cut, :] = mm_t(weights_v[cut, :], da[...]).astype(BF)


def mixed_backward(meta, da, pieces, lines):
    own, width = da.shape
    return kernel_call(
        functools.partial(mixed_back_body, places_of(pieces), lines),
        jax.ShapeDtypeStruct((QUERY, own), BF),
        [SMEM, VMEM] + [ANY] * len(pieces),
        VMEM,
        [pltpu.VMEM((QUERY, width), BF), copies_of(pieces)],
        10**12,
        8 << 20,
        (meta, da, *arrays_of(pieces)),
    )


def ffn_body(count, *refs):
    second, grads, shards = refs[:count], refs[count : 2 * count], refs[2 * count]
    out_a, out_b, back_a, back_b, sums = refs[2 * count + 1 : 2 * count + 6]
    (
        second_v, grads_v, weights, hidden, gate_g, up_g, hidden_t, gate_t, up_t, sums_v, sems, row_sems, sum_sem,
    ) = refs[2 * count + 6 :]
    rows = second[0].shape[0]
    blocks, units = shards.shape[0], shards.shape[1] // 3
    weight_copies = [
        pltpu.make_async_copy(
            shards.at[b, pl.ds(p * units, units)], weights.at[p, pl.ds(b * units, units)], sems.at[p, b]
        )
        for p in range(3)
        for b in range(blocks)
    ]
    for copy in weight_copies:
        copy.start()
    for i in range(count):
        cut = pl.ds(i * rows, rows)
        pltpu.make_async_copy(second[i], second_v.at[cut], sems.at[3, i]).start()
        pltpu.make_async_copy(grads[i], grads_v.at[cut], sems.at[4, i]).start()
    for copy in weight_copies:
        copy.wait()
    per = 2
    step = per * rows

    def one(m, _):
        here = pl.ds(pl.multiple_of(m * step, step), step)
        for i in range(per):
            cut = pl.ds(pl.multiple_of((m * per + i) * rows, rows), rows)
            pltpu.make_async_copy(second_v.at[cut], second_v.at[cut], sems.at[3, m * per + i]).wait()
            pltpu.make_async_copy(grads_v.at[cut], grads_v.at[cut], sems.at[4, m * per + i]).wait()
        gate = mm_t(second_v[here, :], weights[0])
        up = mm_t(second_v[here, :], weights[1])
        hidden_grad = mm_t(grads_v[here, :], weights[2])
        sigma = jax.nn.sigmoid(gate)
        silu = gate * sigma
        mixed = silu * up
        hidden[here, :] = mixed.astype(BF)
        hidden_t[:, here] = mixed.T.astype(BF)
        gate_grad = hidden_grad * up * (sigma + silu * (1.0 - sigma))
        gate_g[here, :] = gate_grad.astype(BF)
        gate_t[:, here] = gate_grad.T.astype(BF)
        up_grad = hidden_grad * silu
        up_g[here, :] = up_grad.astype(BF)
        up_t[:, here] = up_grad.T.astype(BF)
        return 0

    lax.fori_loop(0, count // per, one, 0)

    width = second_v.shape[1]
    for n, (left, right) in enumerate(((gate_t, second_v), (up_t, second_v), (hidden_t, grads_v))):
        for c in range(width // step):
            cut = slice(c * step, (c + 1) * step)
            part = mm(left[...], right[:, cut]).astype(BF)
            for b in range(blocks):
                sums_v[b, n * units : (n + 1) * units, cut] = part[b * units : (b + 1) * units]
    sum_copy = pltpu.make_async_copy(sums_v, sums, sum_sem)
    sum_copy.start()

    half = count * rows // 2
    copies = []
    for n, (kind, first, target) in enumerate(
        (("b", half, back_b), ("b", 0, back_a), ("o", half, out_b), ("o", 0, out_a))
    ):
        place = second_v if kind == "b" else grads_v
        for k in range(half // step):
            here = slice(first + k * step, first + (k + 1) * step)
            if kind == "b":
                value = mm(gate_g[here, :], weights[0]) + mm(up_g[here, :], weights[1])
            else:
                value = mm(hidden[here, :], weights[2])
            place[here, :] = value.astype(BF)
            copies.append(
                pltpu.make_async_copy(
                    place.at[pl.ds(first + k * step, step)],
                    target.at[pl.ds(k * step, step)],
                    row_sems.at[n, k],
                )
            )
            copies[-1].start()
    sum_copy.wait()
    for copy in copies:
        copy.wait()


def ffn(tokens_of, weights):
    pieces = len(tokens_of) // 2
    rows, width = tokens_of[0].shape
    count, total = pieces * rows, weights.shape[0] * weights.shape[1] // 3
    sds = jax.ShapeDtypeStruct
    return kernel_call(
        functools.partial(ffn_body, pieces),
        (sds((count // 2, width), BF),) * 4 + (sds(weights.shape, BF),),
        [ANY] * (2 * pieces + 1),
        (ANY,) * 5,
        [
            pltpu.VMEM((count, width), BF), pltpu.VMEM((count, width), BF),
            pltpu.VMEM((3, total, width), BF),
            pltpu.VMEM((count, total), BF), pltpu.VMEM((count, total), BF), pltpu.VMEM((count, total), BF),
            pltpu.VMEM((total, count), BF), pltpu.VMEM((total, count), BF), pltpu.VMEM((total, count), BF),
            pltpu.VMEM(weights.shape, BF),
            pltpu.SemaphoreType.DMA((5, max(weights.shape[0], pieces))),
            pltpu.SemaphoreType.DMA((4, max(count // 2 // (2 * rows), 1))),
            pltpu.SemaphoreType.DMA,
        ],
        18 * count * total * width,
        34 << 20,
        (*tokens_of, weights),
    )


def project_sums_body(seqs, split, meta, normed_t, query_back, pair_back, send, keep):
    place = meta[0]
    wide = normed_t.shape[1] // seqs
    rows = query_back.shape[1] // seqs
    step = 384
    for n in range(normed_t.shape[0] // step):
        cut = slice(n * step, (n + 1) * step)
        own = jnp.concatenate(
            [normed_t[cut, pl.ds(pl.multiple_of(s * wide + place * rows, 128), rows)] for s in range(seqs)],
            axis=1,
        )
        store_rows(
            meta, split, mm_t(own, query_back[...]), n * step, send, keep, pl.ds(PAIR, QUERY)
        )
        store_rows(
            meta, split, mm_t(normed_t[cut, :], pair_back[...]), n * step, send, keep, pl.ds(0, PAIR)
        )


def project_sums(meta, normed_t, query_back, pair_back, seqs, parts, split):
    width = normed_t.shape[0]
    return kernel_call(
        functools.partial(project_sums_body, seqs, split),
        sums_shapes(split, parts, width, PAIR + QUERY),
        [SMEM, VMEM, VMEM, VMEM],
        (VMEM,) * 2,
        [],
        1,
        26 << 20,
        (meta, normed_t, query_back, pair_back),
    )


def input_grad_body(places, lines, meta, tokens, gain, first_grad, query_back, pair_back, *refs):
    pieces, (out, pair_v, query_v, pair_sems, query_sems) = refs[: len(places)], refs[len(places) :]
    query_copies = load_rows(meta, places, lines, pieces, query_v, query_sems, pl.ds(PAIR + 128, QUERY))
    pair_copies = load_rows(meta, places, lines, pieces, pair_v, pair_sems, pl.ds(0, PAIR))
    for copy in query_copies:
        copy.wait()
    back = mm(query_v[...], query_back[...])
    for copy in pair_copies:
        copy.wait()
    back = (back + mm(pair_v[...], pair_back[...])).T
    value = tokens[...].astype(F32)
    inverse = inverse_rms(value)
    scaled = back * gain[0:1]
    out[...] = (
        first_grad[...]
        + inverse * scaled
        - value * inverse**3 * jnp.mean(scaled * value, axis=-1, keepdims=True)
    ).astype(BF)


def input_grad(meta, tokens, gain, first_grad, query_back, pair_back, pieces, lines):
    width = tokens.shape[1]
    return kernel_call(
        functools.partial(input_grad_body, places_of(pieces), lines),
        jax.ShapeDtypeStruct(tokens.shape, BF),
        [SMEM] + [VMEM] * 5 + [ANY] * len(pieces),
        VMEM,
        [
            pltpu.VMEM((width, PAIR), BF), pltpu.VMEM((width, QUERY), BF), copies_of(pieces), copies_of(pieces),
        ],
        2 * width * (query_back.size + pair_back.size),
        14 << 20,
        (meta, tokens, gain, first_grad, query_back, pair_back, *arrays_of(pieces)),
    )


def per_device(
    tokens,
    positions,
    out_grad,
    w_query,
    w_key,
    w_value,
    w_output,
    gain_attn,
    gain_ffn,
    w_gate,
    w_up,
    w_down,
):
    move = Moves()
    Z, Q, step = move.Z, move.Q, move.step
    seqs, rows, width = tokens.shape
    wide = rows * Z
    own_rows = seqs * rows
    pair_width = KV_HEADS * HEAD
    share, units = w_query.shape[0], w_gate.shape[0]
    split = share % 16 == 0
    meta = jnp.stack([move.zi, move.qi, move.xi, move.ci]).astype(jnp.int32)
    near = [(j, i) for j in range(Q) for i in range(2)]
    rounds = (Z, Q) == (4, 2)
    grad_out = out_grad.reshape(own_rows, width)
    inputs = tokens.reshape(own_rows, width)

    always = lax.optimization_barrier(jnp.ones((), jnp.bool_))

    def window(body, *operands):
        shapes = jax.eval_shape(body, *operands)
        return lax.cond(
            always,
            body,
            lambda *_: jax.tree.map(lambda s: jnp.zeros(s.shape, s.dtype), shapes),
            *operands,
        )

    def over_z(value):
        return lax.all_gather(value, "seq", axis=0, tiled=False)

    def sum_z(value):
        return lax.psum_scatter(value, "seq", scatter_dimension=0, tiled=False)

    columns = -(-own_rows // share)
    spots = jnp.pad(positions.reshape(own_rows), (0, columns * share - own_rows)).reshape(share, columns)
    gains_in = jnp.concatenate(
        [gain_attn[:, None], gain_ffn[:, None], (spots // 256).astype(BF), (spots % 256).astype(BF)], axis=1
    )
    gains_in = jnp.pad(gains_in, ((0, 0), (0, 126 - 2 * columns)))
    pack0 = jnp.concatenate([w_key, w_value, gains_in, w_query], axis=1)
    ffn_in = jnp.concatenate([w_gate, w_up, w_down], axis=0)
    half = len(near)

    def spread(value):
        return tuple(step((j, i), value) if j or i else value for j, i in near)

    def cores(pieces):
        return tuple(pieces) + tuple(step("c", piece) for piece in pieces)

    def to_send(own, other):
        return [(in_f32(own[n]) + in_f32(other[n])).astype(BF) for n in range(1, half)]

    def halves(parts):
        return [part.reshape(half, own_rows, width) for part in parts]

    def blocks_to(blocks, *held):
        return [after(step((-j % Q, i), block), *held) for block, (j, i) in zip(blocks, near[1:])]

    def total(first, parts):
        for part in parts:
            first = first + in_f32(part)
        return first

    def chips_of(rows):
        return [(step((j, i), rows) if j or i else rows, j, i, 0) for j, i in near]

    def everywhere(chips):
        found = []
        for array, j, i, z in chips:
            found += [(array, j, i, 0, z), (step("c", array), j, i, 1, z)]
        if split:
            return found
        rows = found[0][0]
        whole = jnp.zeros((Z, Q, 2, 2) + rows.shape[1:], BF)
        for array, j, i, l, z in found:
            for k in range(array.shape[0]):
                at = (z + k, (move.qi - j) % Q, (move.xi + i) % 2, (move.ci + l) % 2, 0, 0)
                whole = lax.dynamic_update_slice(whole, array[k][None, None, None, None], at)
        return [(whole.reshape(-1, rows.shape[-1]), 0, 0, 0, 0)]

    if rounds:
        def round0(pack0, grad_out):
            return (
                move.around(1, pack0), move.around(-1, pack0), step((0, 1), grad_out), step((1, 0), grad_out)
            )

        up, down, grad_x, grad_q = window(round0, pack0, grad_out)
        carried, ffn_in, up, down = lax.optimization_barrier((tokens, ffn_in, up, down))
        tokens_all = over_z(carried)
        ffn_w = over_z(ffn_in)

        def round1(pack0, up, down, grad_x, grad_q):
            middle = own_rows // 2
            far = move.around(1, up)
            corner = step((0, 1), grad_q[:middle]), step((1, 0), grad_x[middle:])
            return jnp.stack([pack0, up, far, down]), jnp.concatenate(corner)

        pack, grad_xq = window(round1, pack0, up, down, grad_x, grad_q)
        grad_spread = (grad_out, grad_x, grad_q, grad_xq)

        def round2(pack, output0):
            return (
                step((0, 1), pack), step((1, 0), pack), step("c", pack),
                move.around(1, output0), move.around(-1, output0),
            )

        at_x, at_q, pack_c, output1, output3 = window(round2, pack, w_output)

        def round3(at_x, at_q, output0, output1, output3):
            corner = step((0, 1), at_q[:2]), step((1, 0), at_x[2:])
            cores_of = step("c", at_x), step("c", at_q)
            output2 = move.around(1, output1)
            return corner + cores_of + (jnp.stack([output0, output1, output2, output3]),)

        corner_a, corner_b, at_xc, at_qc, out_pack = window(
            round3, at_x, at_q, w_output, output1, output3
        )
        pieces = [
            (pack, 0, 0, 0, 0), (pack_c, 0, 0, 1, 0), (at_x, 0, 1, 0, 0), (at_xc, 0, 1, 1, 0),
            (at_q, 1, 0, 0, 0), (at_qc, 1, 0, 1, 0),
            (corner_a, 1, 1, 0, 0), (step("c", corner_a), 1, 1, 1, 0),
            (corner_b, 1, 1, 0, 2), (step("c", corner_b), 1, 1, 1, 2),
        ]
    else:
        tokens_all = over_z(tokens)
        pack = over_z(pack0)
        grad_spread = spread(grad_out)
        ffn_w = over_z(ffn_in)
        out_pack = over_z(w_output)
        pieces = everywhere(chips_of(pack))

    spots = in_f32(pack[:, :, 2 * pair_width + 2 : 2 * pair_width + 2 + 2 * columns])
    spots = (spots[..., :columns] * 256 + spots[..., columns:]).reshape(Z, -1)[:, :own_rows]
    if rounds:
        order = (move.zi - jnp.arange(Z)) % Z
        spots = jnp.sum(jnp.where((order[:, None] == jnp.arange(Z)[None])[..., None], spots[None], 0), axis=1)
    cosine, sine = angle_tables(
        spots.reshape(Z, seqs, rows).transpose(1, 0, 2).reshape(seqs * wide)
    )

    if rounds:

        def round4(meta, cosine, sine, out_pack, tokens_all, arrays):
            moved = step((0, 1), out_pack), step((1, 0), out_pack)
            found = [(array,) + piece[1:] for array, piece in zip(arrays, pieces)]
            return moved + tuple(
                project_forward(meta, tokens_all, cosine, sine, found, Q, width, seqs, rows)
            )

        out_x, out_q, query_t, pair_t, normed_t, gains = window(
            round4, meta, cosine, sine, out_pack, tokens_all, arrays_of(pieces)
        )

        def round5(meta, query_t, pair_t, out_pack, out_x, out_q):
            corner = step((0, 1), out_q[:2]), step((1, 0), out_x[2:])
            cores_of = step("c", out_pack), step("c", out_x), step("c", out_q)
            return corner + cores_of + tuple(attend_forward(meta, query_t, pair_t, seqs))

        corner_a, corner_b, out_packc, out_xc, out_qc, mixed, mixed_t, logs = window(
            round5, meta, query_t, pair_t, out_pack, out_x, out_q
        )
        out_pieces = [
            (out_pack, 0, 0, 0, 0), (out_packc, 0, 0, 1, 0), (out_x, 0, 1, 0, 0), (out_xc, 0, 1, 1, 0),
            (out_q, 1, 0, 0, 0), (out_qc, 1, 0, 1, 0),
            (corner_a, 1, 1, 0, 0), (step("c", corner_a), 1, 1, 1, 0),
            (corner_b, 1, 1, 0, 2), (step("c", corner_b), 1, 1, 1, 2),
        ]
    else:
        query_t, pair_t, normed_t, gains = project_forward(
            meta, tokens_all, cosine, sine, pieces, Q, width, seqs, rows
        )
        mixed, mixed_t, logs = attend_forward(meta, query_t, pair_t, seqs)
        out_pieces = everywhere(chips_of(out_pack))
    first_sum, second = output_forward(meta, inputs, mixed, gains, out_pieces, Q)
    grad_spread = cores(tuple(after(piece, mixed) for piece in grad_spread))

    second_spread = cores(spread(second))
    outs, backs, ffn_sum = [], [], None
    for n in range(0, 2 * half, 8):
        *parts, sums = ffn(second_spread[n : n + 8] + grad_spread[n : n + 8], ffn_w)
        outs += parts[:2]
        backs += parts[2:]
        ffn_sum = sums if ffn_sum is None else in_f32(ffn_sum) + in_f32(sums)
    if len(outs) > 2:
        outs = (jnp.concatenate(outs[: len(outs) // 2]), jnp.concatenate(outs[len(outs) // 2 :]))
        backs = (jnp.concatenate(backs[: len(backs) // 2]), jnp.concatenate(backs[len(backs) // 2 :]))
    grad_ffn = sum_z(ffn_sum.astype(BF))
    back, other = halves((backs[0], step("c", backs[1])))

    def second_round(first, second, blocks, out):
        moved, out = lax.optimization_barrier((blocks_to(blocks), step("c", out)))
        return total(in_f32(first) + in_f32(second), moved), out

    second_grad, out_other = window(second_round, back[0], other[0], to_send(back, other), outs[1])

    def pieces_for(send, keep):
        if split:
            return send, keep
        value = keep.reshape(Z, Q, 2, 2, share, keep.shape[-1])

        def cut(c):
            return jnp.stack(
                [
                    lax.dynamic_slice(
                        value,
                        (0, (move.qi - j) % Q, (move.xi + i) % 2, c, 0, 0),
                        (Z, 1, 1, 1, share, keep.shape[-1]),
                    )[:, 0, 0, 0]
                    for j, i in near
                ]
            )

        return cut(1 - move.ci), cut(move.ci)

    first_grad, rounded, out_send, out_keep = output_backward(
        grad_out, first_sum, second_grad, gains, mixed_t, meta, (Z, Q), split
    )
    out_send, out_keep = pieces_for(out_send, out_keep)
    moving = step("c", out_send)
    mixed_grad_t = mixed_backward(meta, rounded, out_pieces, Q)
    out_send, mixed_grad_t = lax.optimization_barrier((moving, mixed_grad_t))
    blocks = to_send(out_keep, out_send)

    def attention_beside(first, second, blocks, meta, query_t, pair_t, mixed_grad_t, logs, cosine, sine, normed_t):
        moved = blocks_to(blocks)
        query_back, pair_back, pair_blocks = attend_backward(
            meta, query_t, pair_t, mixed_grad_t, logs, cosine, sine, seqs
        )
        send, keep = project_sums(meta, normed_t, query_back, pair_back, seqs, (Z, Q), split)
        keep, moved = lax.optimization_barrier((keep, moved))
        out_rows = total(in_f32(first) + in_f32(second), moved).astype(BF)
        return out_rows, query_back, pair_blocks, send, keep

    out_rows, query_back, pair_blocks, send, keep = window(
        attention_beside, out_keep[0], out_send[0], blocks, meta, query_t, pair_t, mixed_grad_t, logs,
        cosine, sine, normed_t,
    )
    grad_ffn, pair_blocks = lax.optimization_barrier((grad_ffn, pair_blocks))
    pair_own = sum_z(pair_blocks)
    send, keep = pieces_for(send, keep)
    send = step("c", send)
    rows_of = total(in_f32(keep[0]) + in_f32(send[0]), blocks_to(to_send(keep, send))).astype(BF)
    out, out_other = halves((outs[0], out_other))
    blocks = [after(block, rows_of) for block in to_send(out, out_other)]
    rows_of, pair_own = lax.optimization_barrier((jnp.concatenate([rows_of, out_rows], axis=-1), pair_own))
    sums = in_f32(sum_z(rows_of))
    in_grad = input_grad(meta, inputs, gains, first_grad, query_back, pair_own, pieces, Q)
    layer = total(first_sum + in_f32(out[0]) + in_f32(out_other[0]), blocks_to(blocks, in_grad))
    layer_out = layer.astype(BF)
    grad_ffn = in_f32(grad_ffn)
    grad_gate, grad_up, grad_down = grad_ffn[:units], grad_ffn[units : 2 * units], grad_ffn[2 * units :]

    grad_key, grad_value = sums[:, :pair_width], sums[:, pair_width : 2 * pair_width]
    grad_query = sums[:, 2 * pair_width : 2 * pair_width + QUERY]
    output_sum = sums[:, 2 * pair_width + QUERY :]
    grad_output, grad_gain_ffn = output_sum[:, :width], output_sum[:, width]
    grad_gain_attn = (
        jnp.sum(grad_query * in_f32(w_query), axis=1)
        + jnp.sum(grad_key * in_f32(w_key), axis=1)
        + jnp.sum(grad_value * in_f32(w_value), axis=1)
    ) / in_f32(gain_attn)
    return (
        layer_out.reshape(seqs, rows, width),
        in_grad.reshape(seqs, rows, width),
        grad_query,
        grad_key,
        grad_value,
        grad_output,
        grad_gain_attn,
        grad_gain_ffn,
        grad_gate,
        grad_up,
        grad_down,
    )


def solution(mesh):
    rows = P(("seq", "dp"), None)
    vector = P(("seq", "dp"))
    act = P("dp", "seq", None)
    return jax.shard_map(
        per_device,
        mesh=mesh,
        in_specs=(act, P("dp", "seq"), act, rows, rows, rows, rows, vector, vector, rows, rows, rows),
        out_specs=(act, act, rows, rows, rows, rows, vector, vector, rows, rows, rows),
        check_vma=False,
    )
```

```python
import functools

import jax
import jax.numpy as jnp
from jax import lax
from jax.experimental import pallas as pl
from jax.experimental.pallas import tpu as pltpu
from jax.sharding import PartitionSpec as P

HEADS = 16
KV_HEADS = 8
HEAD = 96
GROUP = HEADS // KV_HEADS

EPS = 1e-05
THETA = 100000.0
NEG = -1e30
BF = jnp.bfloat16
F32 = jnp.float32


def inverse_rms(values):
    return lax.rsqrt(jnp.mean(values * values, axis=-1, keepdims=True) + EPS)


def angle_tables(places):
    offsets = jnp.arange(0, HEAD, 2, dtype=F32)
    angles = (THETA ** (-offsets / HEAD))[:, None] * places.astype(F32)[None, :]
    return (jnp.cos(angles), jnp.sin(angles))


def mm(left, right):
    return jnp.dot(left, right, preferred_element_type=F32)


def mm_t(left, right):
    return lax.dot_general(left, right, (((1,), (1,)), ((), ())), preferred_element_type=F32)


def t_mm(left, right):
    return lax.dot_general(left, right, (((0,), (0,)), ((), ())), preferred_element_type=F32)


def in_f32(value):
    return value.astype(F32)


def after(value, *others):
    return lax.optimization_barrier((value, *others))[0]


class Moves:
    def __init__(self):
        self.Z = lax.axis_size("seq")
        self.DP = lax.axis_size("dp")
        self.Q = self.DP // 4
        self.zi = lax.axis_index("seq")
        place = lax.axis_index("dp")
        self.qi = place // 4
        self.xi = (place // 2) % 2
        self.ci = place % 2

    def around(self, hop, value):
        return lax.ppermute(value, "seq", [(n, (n + hop) % self.Z) for n in range(self.Z)])

    def step(self, offset, value):
        if offset == "c":
            return lax.ppermute(value, "dp", [(n, n ^ 1) for n in range(self.DP)])
        j, i = offset
        return lax.ppermute(
            value, "dp", [(n, (n % 4) ^ (2 * i) | 4 * ((n // 4 + j) % self.Q)) for n in range(self.DP)]
        )


VMEM = pl.BlockSpec(memory_space=pltpu.VMEM)
ANY = pl.BlockSpec(memory_space=pl.ANY)
SMEM = pl.BlockSpec(memory_space=pltpu.SMEM)
SCALE = HEAD ** (-0.5)
HALF = HEAD // 2
QUERY = HEADS * HEAD
PAIR = 2 * KV_HEADS * HEAD


def kernel_call(body, out_shape, in_specs, out_specs, scratch, flops, moved, args):
    return pl.pallas_call(
        body,
        out_shape=out_shape,
        in_specs=in_specs,
        out_specs=out_specs,
        scratch_shapes=scratch,
        compiler_params=pltpu.CompilerParams(vmem_limit_bytes=60 << 20),
        cost_estimate=pl.CostEstimate(flops=flops, bytes_accessed=moved, transcendentals=0),
    )(*args)


def load_rows(meta, places, lines, refs, target, sems, columns):
    copies = []
    if len(refs) == 1:
        copies.append(pltpu.make_async_copy(refs[0].at[:, columns], target, sems.at[0]))
    else:
        zi, qi, xi, ci, count = meta[0], meta[1], meta[2], meta[3], target.shape[0] // (4 * lines * refs[0].shape[1])
        for ref, (j, i, l, first) in zip(refs, places):
            blocks, share, _ = ref.shape
            q = lax.rem(qi + (lines - j), lines)
            x = lax.rem(xi + i, 2)
            c = lax.rem(ci + l, 2)
            for k in range(blocks):
                z = lax.rem(zi + (count - first - k), count) if len(refs) == 10 else first + k
                row = pl.multiple_of((((z * lines + q) * 2 + x) * 2 + c) * share, share)
                copies.append(
                    pltpu.make_async_copy(
                        ref.at[k, :, columns], target.at[pl.ds(row, share), :], sems.at[len(copies)]
                    )
                )
    for copy in copies:
        copy.start()
    return copies


def arrays_of(pieces):
    return [piece[0] for piece in pieces]


def places_of(pieces):
    return tuple(piece[1:] for piece in pieces)


def copies_of(pieces):
    count = 1 if len(pieces) == 1 else sum(piece[0].shape[0] for piece in pieces)
    return pltpu.SemaphoreType.DMA((count,))


def store_rows(meta, split, block, first, send, keep, columns):
    if not split:
        keep[pl.ds(first, block.shape[0]), columns] = block.astype(keep.dtype)
        return
    lines, share = keep.shape[0] // 2, keep.shape[2]
    qi, xi, ci = meta[1], meta[2], meta[3]
    for n in range(block.shape[0] // (2 * share)):
        chip = first // (2 * share) + n
        z, q, x = chip // (2 * lines), chip // 2 % lines, chip % 2
        j = lax.rem(qi + (lines - q), lines)
        i = lax.rem(xi + x, 2)
        even = block[2 * n * share : (2 * n + 1) * share]
        odd = block[(2 * n + 1) * share : (2 * n + 2) * share]
        keep[2 * j + i, z, :, columns] = jnp.where(ci == 0, even, odd).astype(keep.dtype)
        send[2 * j + i, z, :, columns] = jnp.where(ci == 0, odd, even).astype(send.dtype)


def sums_shapes(split, parts, rows, width):
    if not split:
        return (jax.ShapeDtypeStruct((8, 128), BF), jax.ShapeDtypeStruct((rows, width), BF))
    shape = (parts[1] * 2, parts[0], rows // (parts[0] * parts[1] * 4), width)
    return (jax.ShapeDtypeStruct(shape, BF), jax.ShapeDtypeStruct(shape, BF))


def turned_store(ref, row, lanes, block, cosine, sine):
    upper, lower = block[:HALF], block[HALF:]
    ref[pl.ds(row, HALF), lanes] = (upper * cosine - lower * sine).astype(ref.dtype)
    ref[pl.ds(row + HALF, HALF), lanes] = (lower * cosine + upper * sine).astype(ref.dtype)


def head_scores(queries, keys, place, wide):
    scores = mm(keys, queries) * SCALE
    rows = scores.shape[1] // GROUP
    key_place = lax.broadcasted_iota(jnp.int32, scores.shape, 0)
    query_place = place * rows + lax.rem(lax.broadcasted_iota(jnp.int32, scores.shape, 1), rows)
    return jnp.where(key_place <= query_place, scores, NEG)


def group_of(ref, g, lanes):
    return jnp.concatenate(
        [ref[pl.ds(pl.multiple_of((g * GROUP + j) * HEAD, 16), HEAD), lanes] for j in range(GROUP)],
        axis=1,
    )


def flip(value):
    return value.astype(F32).T.astype(value.dtype)


def project_forward_body(seqs, wide, places, lines, meta, tokens, cosine, sine, *refs):
    count = len(places)
    pieces, refs = refs[:count], refs[count:]
    (
        query_t, pair_t, normed_t, gains,
        pair_v, query_v, gains_v, normed, own, pair_sems, query_sems, gain_sems,
    ) = refs
    place = meta[0]
    rows = own.shape[0] // seqs
    pair_width = KV_HEADS * HEAD
    gain_copies = load_rows(meta, places, lines, pieces, gains_v, gain_sems, pl.ds(PAIR, 128))
    pair_copies = load_rows(meta, places, lines, pieces, pair_v, pair_sems, pl.ds(0, PAIR))
    query_copies = load_rows(meta, places, lines, pieces, query_v, query_sems, pl.ds(PAIR + 128, QUERY))
    for copy in gain_copies:
        copy.wait()
    gains[...] = gains_v[...].astype(F32).T[:8]
    gain = gains[0:1]
    for s in range(seqs):
        for z in range(wide // rows):
            cut = slice(s * wide + z * rows, s * wide + (z + 1) * rows)
            values = tokens[z, s].astype(F32)
            block = (values * inverse_rms(values) * gain).astype(BF)
            normed[cut, :] = block
            normed_t[:, cut] = flip(block)
    for s in range(seqs):
        own[s * rows : (s + 1) * rows, :] = normed[
            pl.ds(pl.multiple_of(s * wide + place * rows, 128), rows), :
        ]
    for copy in pair_copies:
        copy.wait()
    heads = 8
    width = heads * HEAD
    for n in range(2 * pair_width // width):
        for s in range(seqs):
            lanes = slice(s * wide, (s + 1) * wide)
            block = mm(normed[lanes, :], pair_v[:, n * width : (n + 1) * width]).T
            if (n + 1) * width <= pair_width:
                for h in range(heads):
                    turned_store(
                        pair_t, n * width + h * HEAD, lanes, block[h * HEAD : (h + 1) * HEAD],
                        cosine[:, lanes], sine[:, lanes],
                    )
            else:
                pair_t[n * width : (n + 1) * width, lanes] = block.astype(BF)
    for copy in query_copies:
        copy.wait()
    for n in range(HEADS * HEAD // width):
        block = mm(own[...], query_v[:, n * width : (n + 1) * width]).T
        for s in range(seqs):
            lanes = slice(s * rows, (s + 1) * rows)
            here = pl.ds(pl.multiple_of(s * wide + place * rows, 128), rows)
            for h in range(heads):
                turned_store(
                    query_t, n * width + h * HEAD, lanes, block[h * HEAD : (h + 1) * HEAD, lanes],
                    cosine[:, here], sine[:, here],
                )


def attend_forward_body(seqs, wide, meta, query_t, pair_t, mixed, mixed_t, logs):
    place = meta[0]
    rows = query_t.shape[1] // seqs
    pair_width = KV_HEADS * HEAD

    def one(g, _):
        row = pl.multiple_of(g * HEAD, 16)
        for s in range(seqs):
            lanes = slice(s * wide, (s + 1) * wide)
            mine = slice(s * rows, (s + 1) * rows)
            scores = head_scores(
                group_of(query_t, g, mine), flip(pair_t[pl.ds(row, HEAD), lanes]), place, wide
            )
            top = jnp.max(scores, axis=0, keepdims=True)
            weights = jnp.exp(scores - top)
            total = jnp.sum(weights, axis=0, keepdims=True)
            probs = (weights * (1.0 / total)).astype(BF)
            out = mm(pair_t[pl.ds(row + pair_width, HEAD), lanes], probs).astype(BF)
            for j in range(GROUP):
                mixed_t[pl.ds(pl.multiple_of((g * GROUP + j) * HEAD, 16), HEAD), mine] = out[
                    :, j * rows : (j + 1) * rows
                ]
            logs[g, s] = top + jnp.log(total)
        return 0

    lax.fori_loop(0, KV_HEADS, one, 0)
    mixed[...] = flip(mixed_t[...])


def project_forward(meta, tokens, cosine, sine, pieces, lines, width, seqs, rows):
    wide = tokens.shape[0] * rows
    count, own = seqs * wide, seqs * rows
    sds = jax.ShapeDtypeStruct
    return kernel_call(
        functools.partial(project_forward_body, seqs, wide, places_of(pieces), lines),
        (sds((QUERY, own), BF), sds((PAIR, count), BF), sds((width, count), BF), sds((8, width), F32)),
        [SMEM, VMEM, VMEM, VMEM] + [ANY] * len(pieces),
        (VMEM,) * 4,
        [
            pltpu.VMEM((width, PAIR), BF), pltpu.VMEM((width, QUERY), BF), pltpu.VMEM((width, 128), BF),
            pltpu.VMEM((count, width), BF), pltpu.VMEM((own, width), BF),
            copies_of(pieces), copies_of(pieces), copies_of(pieces),
        ],
        2 * count * width * PAIR + 2 * own * width * QUERY,
        20 << 20,
        (meta, tokens, cosine, sine, *arrays_of(pieces)),
    )


def attend_forward(meta, query_t, pair_t, seqs):
    own = query_t.shape[1]
    wide = pair_t.shape[1] // seqs
    sds = jax.ShapeDtypeStruct
    return kernel_call(
        functools.partial(attend_forward_body, seqs, wide),
        (
            sds((own, QUERY), BF), sds((QUERY, own), BF),
            sds((KV_HEADS, seqs, 1, GROUP * own // seqs), F32),
        ),
        [SMEM, VMEM, VMEM],
        (VMEM,) * 3,
        [],
        4 * own * wide * QUERY,
        6 << 20,
        (meta, query_t, pair_t),
    )


def attend_backward_body(
    seqs, wide, meta, query_t, pair_t, grad_t, logs, cosine, sine, query_back, pair_back, pair_blocks
):
    place = meta[0]
    rows = query_t.shape[1] // seqs
    pair_width = KV_HEADS * HEAD

    def one(g, _):
        row = pl.multiple_of(g * HEAD, 16)
        for s in range(seqs):
            lanes = slice(s * wide, (s + 1) * wide)
            mine = slice(s * rows, (s + 1) * rows)
            here = pl.ds(pl.multiple_of(s * wide + place * rows, 128), rows)
            queries = group_of(query_t, g, mine)
            grads = group_of(grad_t, g, mine)
            keys_t = pair_t[pl.ds(row, HEAD), lanes]
            values_t = pair_t[pl.ds(row + pair_width, HEAD), lanes]
            probs = jnp.exp(head_scores(queries, flip(keys_t), place, wide) - logs[g, s])
            prob_grad = mm(flip(values_t), grads)
            centre = jnp.sum(probs * prob_grad, axis=0, keepdims=True)
            score_grad = (probs * (prob_grad - centre)).astype(BF)
            query_grad = mm(keys_t, score_grad) * SCALE
            for j in range(GROUP):
                turned_store(
                    query_back, pl.multiple_of((g * GROUP + j) * HEAD, 16), mine,
                    query_grad[:, j * rows : (j + 1) * rows], cosine[:, here], -sine[:, here],
                )
            turned_store(
                pair_back, row, lanes, mm_t(queries, score_grad) * SCALE,
                cosine[:, lanes], -sine[:, lanes],
            )
            pair_back[pl.ds(row + pair_width, HEAD), lanes] = mm_t(
                grads, probs.astype(BF)
            ).astype(BF)
            for z in range(wide // rows):
                from_z = slice(s * wide + z * rows, s * wide + (z + 1) * rows)
                for first in (row, row + pair_width):
                    pair_blocks[z, pl.ds(first, HEAD), mine] = pair_back[pl.ds(first, HEAD), from_z]
        return 0

    lax.fori_loop(0, KV_HEADS, one, 0)


def attend_backward(meta, query_t, pair_t, grad_t, logs, cosine, sine, seqs):
    wide = pair_t.shape[1] // seqs
    return kernel_call(
        functools.partial(attend_backward_body, seqs, wide),
        (
            jax.ShapeDtypeStruct(query_t.shape, BF),
            jax.ShapeDtypeStruct(pair_t.shape, BF),
            jax.ShapeDtypeStruct((pair_t.shape[1] // query_t.shape[1], PAIR, query_t.shape[1]), BF),
        ),
        [SMEM] + [VMEM] * 6,
        (VMEM,) * 3,
        [],
        10**12,
        12 << 20,
        (meta, query_t, pair_t, grad_t, logs, cosine, sine),
    )


def output_body(places, lines, meta, tokens, mixed, gain, *refs):
    pieces, (total, second, weights_v, sems) = refs[:-4], refs[-4:]
    for copy in load_rows(meta, places, lines, pieces, weights_v, sems, pl.ds(0, weights_v.shape[1])):
        copy.wait()
    value = tokens[...].astype(F32) + mm(mixed[...], weights_v[...])
    total[...] = value
    second[...] = (value * inverse_rms(value) * gain[1:2]).astype(BF)


def output_forward(meta, tokens, mixed, gain, pieces, lines):
    return kernel_call(
        functools.partial(output_body, places_of(pieces), lines),
        (jax.ShapeDtypeStruct(tokens.shape, F32), jax.ShapeDtypeStruct(tokens.shape, BF)),
        [SMEM, VMEM, VMEM, VMEM] + [ANY] * len(pieces),
        (VMEM, VMEM),
        [pltpu.VMEM((QUERY, tokens.shape[1]), BF), copies_of(pieces)],
        2 * tokens.size * QUERY,
        10 << 20,
        (meta, tokens, mixed, gain, *arrays_of(pieces)),
    )


def output_back_body(split, grad, total, second_grad, gain, mixed_t, meta, first_grad, da, send, keep):
    value = total[...]
    inverse = inverse_rms(value)
    back = second_grad[...]
    scaled = back * gain[1:2]
    first = (
        grad[...].astype(F32)
        + inverse * scaled
        - value * inverse**3 * jnp.mean(scaled * value, axis=-1, keepdims=True)
    )
    first_grad[...] = first
    da[...] = first.astype(BF)
    width = value.shape[1]
    gain_part = jnp.broadcast_to(
        jnp.sum((back * value * inverse).T, axis=1, keepdims=True), (width, 128)
    )
    store_rows(meta, split, gain_part, 0, send, keep, pl.ds(width, 128))
    step = 384
    for n in range(width // step):
        cut = slice(n * step, (n + 1) * step)
        store_rows(meta, split, mm(mixed_t[cut, :], da[...]), n * step, send, keep, pl.ds(0, width))


def output_backward(grad, total, second_grad, gain, mixed_t, meta, parts, split):
    own, width = grad.shape
    return kernel_call(
        functools.partial(output_back_body, split),
        (
            jax.ShapeDtypeStruct((own, width), F32),
            jax.ShapeDtypeStruct((own, width), BF),
            *sums_shapes(split, parts, QUERY, width + 128),
        ),
        [VMEM] * 5 + [SMEM],
        (VMEM,) * 4,
        [],
        2 * own * width * QUERY,
        14 << 20,
        (grad, total, second_grad, gain, mixed_t, meta),
    )


def mixed_back_body(places, lines, meta, da, *refs):
    pieces, (mixed_grad_t, weights_v, sems) = refs[:-3], refs[-3:]
    for copy in load_rows(meta, places, lines, pieces, weights_v, sems, pl.ds(0, weights_v.shape[1])):
        copy.wait()
    step = 384
    for n in range(weights_v.shape[0] // step):
        cut = slice(n * step, (n + 1) * step)
        mixed_grad_t[cut, :] = mm_t(weights_v[cut, :], da[...]).astype(BF)


def mixed_backward(meta, da, pieces, lines):
    own, width = da.shape
    return kernel_call(
        functools.partial(mixed_back_body, places_of(pieces), lines),
        jax.ShapeDtypeStruct((QUERY, own), BF),
        [SMEM, VMEM] + [ANY] * len(pieces),
        VMEM,
        [pltpu.VMEM((QUERY, width), BF), copies_of(pieces)],
        10**12,
        8 << 20,
        (meta, da, *arrays_of(pieces)),
    )


def ffn_body(count, *refs):
    second, grads, shards = refs[:count], refs[count : 2 * count], refs[2 * count]
    out_a, out_b, *backs, sums = refs[2 * count + 1 : 3 * count + 4]
    (
        second_v, grads_v, weights, hidden, gate_g, up_g, hidden_t, gate_t, up_t, sums_v, sems, row_sems, sum_sem,
    ) = refs[3 * count + 4 :]
    rows = second[0].shape[0]
    blocks, units = shards.shape[0], shards.shape[1] // 3
    weight_copies = [
        pltpu.make_async_copy(
            shards.at[b, pl.ds(p * units, units)], weights.at[p, pl.ds(b * units, units)], sems.at[p, b]
        )
        for p in range(3)
        for b in range(blocks)
    ]
    for copy in weight_copies:
        copy.start()
    for i in range(count):
        cut = pl.ds(i * rows, rows)
        pltpu.make_async_copy(second[i], second_v.at[cut], sems.at[3, i]).start()
        pltpu.make_async_copy(grads[i], grads_v.at[cut], sems.at[4, i]).start()
    for copy in weight_copies:
        copy.wait()
    per = 2
    step = per * rows

    def one(m, _):
        here = pl.ds(pl.multiple_of(m * step, step), step)
        for i in range(per):
            cut = pl.ds(pl.multiple_of((m * per + i) * rows, rows), rows)
            pltpu.make_async_copy(second_v.at[cut], second_v.at[cut], sems.at[3, m * per + i]).wait()
            pltpu.make_async_copy(grads_v.at[cut], grads_v.at[cut], sems.at[4, m * per + i]).wait()
        gate = mm_t(second_v[here, :], weights[0])
        up = mm_t(second_v[here, :], weights[1])
        hidden_grad = mm_t(grads_v[here, :], weights[2])
        sigma = jax.nn.sigmoid(gate)
        silu = gate * sigma
        mixed = silu * up
        hidden[here, :] = mixed.astype(BF)
        hidden_t[:, here] = mixed.T.astype(BF)
        gate_grad = hidden_grad * up * (sigma + silu * (1.0 - sigma))
        gate_g[here, :] = gate_grad.astype(BF)
        gate_t[:, here] = gate_grad.T.astype(BF)
        up_grad = hidden_grad * silu
        up_g[here, :] = up_grad.astype(BF)
        up_t[:, here] = up_grad.T.astype(BF)
        return 0

    lax.fori_loop(0, count // per, one, 0)

    width = second_v.shape[1]
    for n, (left, right) in enumerate(((gate_t, second_v), (up_t, second_v), (hidden_t, grads_v))):
        for c in range(width // step):
            cut = slice(c * step, (c + 1) * step)
            part = mm(left[...], right[:, cut]).astype(BF)
            for b in range(blocks):
                sums_v[b, n * units : (n + 1) * units, cut] = part[b * units : (b + 1) * units]
    sum_copy = pltpu.make_async_copy(sums_v, sums, sum_sem)
    sum_copy.start()

    half = count * rows // 2
    copies = []
    for n, (kind, first) in enumerate((("b", half), ("b", 0), ("o", half), ("o", 0))):
        place = second_v if kind == "b" else grads_v
        for k in range(half // step):
            here = slice(first + k * step, first + (k + 1) * step)
            if kind == "b":
                value = mm(gate_g[here, :], weights[0]) + mm(up_g[here, :], weights[1])
            else:
                value = mm(hidden[here, :], weights[2])
            place[here, :] = value.astype(BF)
            for i in range(per):
                row = first + k * step + i * rows
                if kind == "b":
                    target = backs[row // rows]
                else:
                    target = (out_b if first else out_a).at[pl.ds(row - first, rows)]
                copies.append(
                    pltpu.make_async_copy(
                        place.at[pl.ds(row, rows)], target, row_sems.at[n, k * per + i]
                    )
                )
                copies[-1].start()
    sum_copy.wait()
    for copy in copies:
        copy.wait()


def ffn(tokens_of, weights):
    pieces = len(tokens_of) // 2
    rows, width = tokens_of[0].shape
    count, total = pieces * rows, weights.shape[0] * weights.shape[1] // 3
    sds = jax.ShapeDtypeStruct
    return kernel_call(
        functools.partial(ffn_body, pieces),
        (sds((count // 2, width), BF),) * 2 + (sds((rows, width), BF),) * pieces + (sds(weights.shape, BF),),
        [ANY] * (2 * pieces + 1),
        (ANY,) * (pieces + 3),
        [
            pltpu.VMEM((count, width), BF), pltpu.VMEM((count, width), BF),
            pltpu.VMEM((3, total, width), BF),
            pltpu.VMEM((count, total), BF), pltpu.VMEM((count, total), BF), pltpu.VMEM((count, total), BF),
            pltpu.VMEM((total, count), BF), pltpu.VMEM((total, count), BF), pltpu.VMEM((total, count), BF),
            pltpu.VMEM(weights.shape, BF),
            pltpu.SemaphoreType.DMA((5, max(weights.shape[0], pieces))),
            pltpu.SemaphoreType.DMA((4, pieces // 2)),
            pltpu.SemaphoreType.DMA,
        ],
        18 * count * total * width,
        34 << 20,
        (*tokens_of, weights),
    )


def project_sums_body(
    seqs, split, meta, normed_t, query_back, pair_back, pair_send, pair_keep, query_send, query_keep
):
    place = meta[0]
    wide = normed_t.shape[1] // seqs
    rows = query_back.shape[1] // seqs
    step = 384
    for n in range(normed_t.shape[0] // step):
        cut = slice(n * step, (n + 1) * step)
        own = jnp.concatenate(
            [normed_t[cut, pl.ds(pl.multiple_of(s * wide + place * rows, 128), rows)] for s in range(seqs)],
            axis=1,
        )
        store_rows(
            meta, split, mm_t(own, query_back[...]), n * step, query_send, query_keep, pl.ds(0, QUERY)
        )
        store_rows(
            meta, split, mm_t(normed_t[cut, :], pair_back[...]), n * step, pair_send, pair_keep, pl.ds(0, PAIR)
        )


def project_sums(meta, normed_t, query_back, pair_back, seqs, parts, split):
    width = normed_t.shape[0]
    return kernel_call(
        functools.partial(project_sums_body, seqs, split),
        (*sums_shapes(split, parts, width, PAIR), *sums_shapes(split, parts, width, QUERY)),
        [SMEM, VMEM, VMEM, VMEM],
        (VMEM,) * 4,
        [],
        1,
        26 << 20,
        (meta, normed_t, query_back, pair_back),
    )


def input_grad_body(places, lines, meta, tokens, gain, first_grad, query_back, pair_back, *refs):
    pieces, (out, pair_v, query_v, pair_sems, query_sems) = refs[: len(places)], refs[len(places) :]
    query_copies = load_rows(meta, places, lines, pieces, query_v, query_sems, pl.ds(PAIR + 128, QUERY))
    pair_copies = load_rows(meta, places, lines, pieces, pair_v, pair_sems, pl.ds(0, PAIR))
    for copy in query_copies:
        copy.wait()
    back = mm(query_v[...], query_back[...])
    for copy in pair_copies:
        copy.wait()
    back = (back + mm(pair_v[...], pair_back[...])).T
    value = tokens[...].astype(F32)
    inverse = inverse_rms(value)
    scaled = back * gain[0:1]
    out[...] = (
        first_grad[...]
        + inverse * scaled
        - value * inverse**3 * jnp.mean(scaled * value, axis=-1, keepdims=True)
    ).astype(BF)


def input_grad(meta, tokens, gain, first_grad, query_back, pair_back, pieces, lines):
    width = tokens.shape[1]
    return kernel_call(
        functools.partial(input_grad_body, places_of(pieces), lines),
        jax.ShapeDtypeStruct(tokens.shape, BF),
        [SMEM] + [VMEM] * 5 + [ANY] * len(pieces),
        VMEM,
        [
            pltpu.VMEM((width, PAIR), BF), pltpu.VMEM((width, QUERY), BF), copies_of(pieces), copies_of(pieces),
        ],
        2 * width * (query_back.size + pair_back.size),
        14 << 20,
        (meta, tokens, gain, first_grad, query_back, pair_back, *arrays_of(pieces)),
    )


def per_device(
    tokens,
    positions,
    out_grad,
    w_query,
    w_key,
    w_value,
    w_output,
    gain_attn,
    gain_ffn,
    w_gate,
    w_up,
    w_down,
):
    move = Moves()
    Z, Q, step = move.Z, move.Q, move.step
    seqs, rows, width = tokens.shape
    wide = rows * Z
    own_rows = seqs * rows
    pair_width = KV_HEADS * HEAD
    share, units = w_query.shape[0], w_gate.shape[0]
    split = share % 16 == 0
    meta = jnp.stack([move.zi, move.qi, move.xi, move.ci]).astype(jnp.int32)
    near = [(j, i) for j in range(Q) for i in range(2)]
    rounds = (Z, Q) == (4, 2)
    grad_out = out_grad.reshape(own_rows, width)
    inputs = tokens.reshape(own_rows, width)

    always = lax.optimization_barrier(jnp.ones((), jnp.bool_))

    def window(body, *operands):
        shapes = jax.eval_shape(body, *operands)
        return lax.cond(
            always,
            body,
            lambda *_: jax.tree.map(lambda s: jnp.zeros(s.shape, s.dtype), shapes),
            *operands,
        )

    def over_z(value):
        return lax.all_gather(value, "seq", axis=0, tiled=False)

    def sum_z(value):
        return lax.psum_scatter(value, "seq", scatter_dimension=0, tiled=False)

    columns = -(-own_rows // share)
    spots = jnp.pad(positions.reshape(own_rows), (0, columns * share - own_rows)).reshape(share, columns)
    gains_in = jnp.concatenate(
        [gain_attn[:, None], gain_ffn[:, None], (spots // 256).astype(BF), (spots % 256).astype(BF)], axis=1
    )
    gains_in = jnp.pad(gains_in, ((0, 0), (0, 126 - 2 * columns)))
    pack0 = jnp.concatenate([w_key, w_value, gains_in, w_query], axis=1)
    ffn_in = jnp.concatenate([w_gate, w_up, w_down], axis=0)
    half = len(near)

    def spread(value):
        return tuple(step((j, i), value) if j or i else value for j, i in near)

    def cores(pieces):
        return tuple(pieces) + tuple(step("c", piece) for piece in pieces)

    def to_send(own, other):
        return [(in_f32(own[n]) + in_f32(other[n])).astype(BF) for n in range(1, half)]

    def halves(parts):
        return [part.reshape(half, own_rows, width) for part in parts]

    def blocks_to(blocks, *held):
        return [after(step((-j % Q, i), block), *held) for block, (j, i) in zip(blocks, near[1:])]

    def total(first, parts):
        for part in parts:
            first = first + in_f32(part)
        return first

    def chips_of(rows):
        return [(step((j, i), rows) if j or i else rows, j, i, 0) for j, i in near]

    def everywhere(chips):
        found = []
        for array, j, i, z in chips:
            found += [(array, j, i, 0, z), (step("c", array), j, i, 1, z)]
        if split:
            return found
        rows = found[0][0]
        whole = jnp.zeros((Z, Q, 2, 2) + rows.shape[1:], BF)
        for array, j, i, l, z in found:
            for k in range(array.shape[0]):
                at = (z + k, (move.qi - j) % Q, (move.xi + i) % 2, (move.ci + l) % 2, 0, 0)
                whole = lax.dynamic_update_slice(whole, array[k][None, None, None, None], at)
        return [(whole.reshape(-1, rows.shape[-1]), 0, 0, 0, 0)]

    if rounds:
        def round0(pack0, grad_out):
            return (
                move.around(1, pack0), move.around(-1, pack0), step((0, 1), grad_out), step((1, 0), grad_out)
            )

        up, down, grad_x, grad_q = window(round0, pack0, grad_out)
        carried, ffn_in, up, down = lax.optimization_barrier((tokens, ffn_in, up, down))
        tokens_all = over_z(carried)
        ffn_w = over_z(ffn_in)

        def round1(pack0, up, down, grad_x, grad_q):
            middle = own_rows // 2
            far = move.around(1, up)
            corner = step((0, 1), grad_q[:middle]), step((1, 0), grad_x[middle:])
            return jnp.stack([pack0, up, far, down]), jnp.concatenate(corner)

        pack, grad_xq = window(round1, pack0, up, down, grad_x, grad_q)
        grad_spread = (grad_out, grad_x, grad_q, grad_xq)

        def round2(pack, output0):
            return (
                step((0, 1), pack), step((1, 0), pack), step("c", pack),
                move.around(1, output0), move.around(-1, output0),
            )

        at_x, at_q, pack_c, output1, output3 = window(round2, pack, w_output)

        def round3(at_x, at_q, output0, output1, output3):
            corner = step((0, 1), at_q[:2]), step((1, 0), at_x[2:])
            cores_of = step("c", at_x), step("c", at_q)
            output2 = move.around(1, output1)
            return corner + cores_of + (jnp.stack([output0, output1, output2, output3]),)

        corner_a, corner_b, at_xc, at_qc, out_pack = window(
            round3, at_x, at_q, w_output, output1, output3
        )
        pieces = [
            (pack, 0, 0, 0, 0), (pack_c, 0, 0, 1, 0), (at_x, 0, 1, 0, 0), (at_xc, 0, 1, 1, 0),
            (at_q, 1, 0, 0, 0), (at_qc, 1, 0, 1, 0),
            (corner_a, 1, 1, 0, 0), (step("c", corner_a), 1, 1, 1, 0),
            (corner_b, 1, 1, 0, 2), (step("c", corner_b), 1, 1, 1, 2),
        ]
    else:
        tokens_all = over_z(tokens)
        pack = over_z(pack0)
        grad_spread = spread(grad_out)
        ffn_w = over_z(ffn_in)
        out_pack = over_z(w_output)
        pieces = everywhere(chips_of(pack))

    spots = in_f32(pack[:, :, 2 * pair_width + 2 : 2 * pair_width + 2 + 2 * columns])
    spots = (spots[..., :columns] * 256 + spots[..., columns:]).reshape(Z, -1)[:, :own_rows]
    if rounds:
        order = (move.zi - jnp.arange(Z)) % Z
        spots = jnp.sum(jnp.where((order[:, None] == jnp.arange(Z)[None])[..., None], spots[None], 0), axis=1)
    cosine, sine = angle_tables(
        spots.reshape(Z, seqs, rows).transpose(1, 0, 2).reshape(seqs * wide)
    )

    if rounds:

        def round4(meta, cosine, sine, out_pack, tokens_all, arrays):
            moved = step((0, 1), out_pack), step((1, 0), out_pack)
            found = [(array,) + piece[1:] for array, piece in zip(arrays, pieces)]
            return moved + tuple(
                project_forward(meta, tokens_all, cosine, sine, found, Q, width, seqs, rows)
            )

        out_x, out_q, query_t, pair_t, normed_t, gains = window(
            round4, meta, cosine, sine, out_pack, tokens_all, arrays_of(pieces)
        )

        def round5(meta, query_t, pair_t, out_pack, out_x, out_q):
            corner = step((0, 1), out_q[:2]), step((1, 0), out_x[2:])
            cores_of = step("c", out_pack), step("c", out_x), step("c", out_q)
            return corner + cores_of + tuple(attend_forward(meta, query_t, pair_t, seqs))

        corner_a, corner_b, out_packc, out_xc, out_qc, mixed, mixed_t, logs = window(
            round5, meta, query_t, pair_t, out_pack, out_x, out_q
        )
        out_pieces = [
            (out_pack, 0, 0, 0, 0), (out_packc, 0, 0, 1, 0), (out_x, 0, 1, 0, 0), (out_xc, 0, 1, 1, 0),
            (out_q, 1, 0, 0, 0), (out_qc, 1, 0, 1, 0),
            (corner_a, 1, 1, 0, 0), (step("c", corner_a), 1, 1, 1, 0),
            (corner_b, 1, 1, 0, 2), (step("c", corner_b), 1, 1, 1, 2),
        ]
    else:
        query_t, pair_t, normed_t, gains = project_forward(
            meta, tokens_all, cosine, sine, pieces, Q, width, seqs, rows
        )
        mixed, mixed_t, logs = attend_forward(meta, query_t, pair_t, seqs)
        out_pieces = everywhere(chips_of(out_pack))
    first_sum, second = output_forward(meta, inputs, mixed, gains, out_pieces, Q)
    grad_spread = cores(tuple(after(piece, mixed) for piece in grad_spread))

    second_spread = cores(spread(second))
    outs, backs, ffn_sum = [], [], None
    for n in range(0, 2 * half, 8):
        out_a, out_b, *parts, sums = ffn(second_spread[n : n + 8] + grad_spread[n : n + 8], ffn_w)
        outs += [out_a, out_b]
        backs += parts
        ffn_sum = sums if ffn_sum is None else in_f32(ffn_sum) + in_f32(sums)
    if len(outs) > 2:
        outs = (jnp.concatenate(outs[: len(outs) // 2]), jnp.concatenate(outs[len(outs) // 2 :]))
    grad_ffn = sum_z(ffn_sum.astype(BF))
    back, other = backs[:half], [step("c", part) for part in backs[half:]]
    second_grad = total(in_f32(back[0]) + in_f32(other[0]), blocks_to(to_send(back, other)))

    def pieces_for(send, keep):
        if split:
            return send, keep
        value = keep.reshape(Z, Q, 2, 2, share, keep.shape[-1])

        def cut(c):
            return jnp.stack(
                [
                    lax.dynamic_slice(
                        value,
                        (0, (move.qi - j) % Q, (move.xi + i) % 2, c, 0, 0),
                        (Z, 1, 1, 1, share, keep.shape[-1]),
                    )[:, 0, 0, 0]
                    for j, i in near
                ]
            )

        return cut(1 - move.ci), cut(move.ci)

    first_grad, rounded, out_send, out_keep = output_backward(
        grad_out, first_sum, second_grad, gains, mixed_t, meta, (Z, Q), split
    )
    out_send, out_keep = pieces_for(out_send, out_keep)
    moving = step("c", out_send)
    mixed_grad_t = mixed_backward(meta, rounded, out_pieces, Q)
    out_send, mixed_grad_t = lax.optimization_barrier((moving, mixed_grad_t))
    blocks = to_send(out_keep, out_send)

    def attention_beside(first, second, blocks, meta, query_t, pair_t, mixed_grad_t, logs, cosine, sine, normed_t, out):
        moved, out = blocks_to(blocks), step("c", out)
        query_back, pair_back, pair_blocks = attend_backward(
            meta, query_t, pair_t, mixed_grad_t, logs, cosine, sine, seqs
        )
        sums = project_sums(meta, normed_t, query_back, pair_back, seqs, (Z, Q), split)
        sums, moved, out = lax.optimization_barrier((tuple(sums), moved, out))
        out_rows = total(in_f32(first) + in_f32(second), moved).astype(BF)
        return out_rows, query_back, pair_blocks, sums, out

    out_rows, query_back, pair_blocks, sums, out_other = window(
        attention_beside, out_keep[0], out_send[0], blocks, meta, query_t, pair_t, mixed_grad_t, logs,
        cosine, sine, normed_t, outs[1],
    )
    grad_ffn, pair_blocks = lax.optimization_barrier((grad_ffn, pair_blocks))
    pair_own = sum_z(pair_blocks)
    pair_send, pair_keep = pieces_for(*sums[:2])
    query_send, query_keep = pieces_for(*sums[2:])
    pair_send, query_send = step("c", pair_send), step("c", query_send)
    pair_blocks_out = blocks_to(to_send(pair_keep, pair_send))
    query_blocks_out = blocks_to(to_send(query_keep, query_send))
    pair_rows = total(in_f32(pair_keep[0]) + in_f32(pair_send[0]), pair_blocks_out).astype(BF)
    query_rows = total(in_f32(query_keep[0]) + in_f32(query_send[0]), query_blocks_out).astype(BF)
    rows_of = jnp.concatenate([pair_rows, query_rows], axis=-1)
    out, out_other = halves((outs[0], out_other))
    blocks = [after(block, rows_of) for block in to_send(out, out_other)]
    rows_of, pair_own = lax.optimization_barrier((jnp.concatenate([rows_of, out_rows], axis=-1), pair_own))
    sums = in_f32(sum_z(rows_of))
    in_grad = input_grad(meta, inputs, gains, first_grad, query_back, pair_own, pieces, Q)
    layer = total(first_sum + in_f32(out[0]) + in_f32(out_other[0]), blocks_to(blocks, in_grad))
    layer_out = layer.astype(BF)
    grad_ffn = in_f32(grad_ffn)
    grad_gate, grad_up, grad_down = grad_ffn[:units], grad_ffn[units : 2 * units], grad_ffn[2 * units :]

    grad_key, grad_value = sums[:, :pair_width], sums[:, pair_width : 2 * pair_width]
    grad_query = sums[:, 2 * pair_width : 2 * pair_width + QUERY]
    output_sum = sums[:, 2 * pair_width + QUERY :]
    grad_output, grad_gain_ffn = output_sum[:, :width], output_sum[:, width]
    grad_gain_attn = (
        jnp.sum(grad_query * in_f32(w_query), axis=1)
        + jnp.sum(grad_key * in_f32(w_key), axis=1)
        + jnp.sum(grad_value * in_f32(w_value), axis=1)
    ) / in_f32(gain_attn)
    return (
        layer_out.reshape(seqs, rows, width),
        in_grad.reshape(seqs, rows, width),
        grad_query,
        grad_key,
        grad_value,
        grad_output,
        grad_gain_attn,
        grad_gain_ffn,
        grad_gate,
        grad_up,
        grad_down,
    )


def solution(mesh):
    rows = P(("seq", "dp"), None)
    vector = P(("seq", "dp"))
    act = P("dp", "seq", None)
    return jax.shard_map(
        per_device,
        mesh=mesh,
        in_specs=(act, P("dp", "seq"), act, rows, rows, rows, rows, vector, vector, rows, rows, rows),
        out_specs=(act, act, rows, rows, rows, rows, vector, vector, rows, rows, rows),
        check_vma=False,
    )
```

```python
import functools

import jax
import jax.numpy as jnp
from jax import lax
from jax.experimental import pallas as pl
from jax.experimental.pallas import tpu as pltpu
from jax.sharding import PartitionSpec as P

HEADS = 16
KV_HEADS = 8
HEAD = 96
GROUP = HEADS // KV_HEADS

EPS = 1e-05
THETA = 100000.0
NEG = -1e30
BF = jnp.bfloat16
F32 = jnp.float32


def inverse_rms(values):
    return lax.rsqrt(jnp.mean(values * values, axis=-1, keepdims=True) + EPS)


def angle_tables(places):
    offsets = jnp.arange(0, HEAD, 2, dtype=F32)
    angles = (THETA ** (-offsets / HEAD))[:, None] * places.astype(F32)[None, :]
    return (jnp.cos(angles), jnp.sin(angles))


def mm(left, right):
    return jnp.dot(left, right, preferred_element_type=F32)


def mm_t(left, right):
    return lax.dot_general(left, right, (((1,), (1,)), ((), ())), preferred_element_type=F32)


def t_mm(left, right):
    return lax.dot_general(left, right, (((0,), (0,)), ((), ())), preferred_element_type=F32)


def in_f32(value):
    return value.astype(F32)


def after(value, *others):
    return lax.optimization_barrier((value, *others))[0]


class Moves:
    def __init__(self):
        self.Z = lax.axis_size("seq")
        self.DP = lax.axis_size("dp")
        self.Q = self.DP // 4
        self.zi = lax.axis_index("seq")
        place = lax.axis_index("dp")
        self.qi = place // 4
        self.xi = (place // 2) % 2
        self.ci = place % 2

    def around(self, hop, value):
        return lax.ppermute(value, "seq", [(n, (n + hop) % self.Z) for n in range(self.Z)])

    def step(self, offset, value):
        if offset == "c":
            return lax.ppermute(value, "dp", [(n, n ^ 1) for n in range(self.DP)])
        j, i = offset
        return lax.ppermute(
            value, "dp", [(n, (n % 4) ^ (2 * i) | 4 * ((n // 4 + j) % self.Q)) for n in range(self.DP)]
        )


VMEM = pl.BlockSpec(memory_space=pltpu.VMEM)
ANY = pl.BlockSpec(memory_space=pl.ANY)
SMEM = pl.BlockSpec(memory_space=pltpu.SMEM)
SCALE = HEAD ** (-0.5)
HALF = HEAD // 2
QUERY = HEADS * HEAD
PAIR = 2 * KV_HEADS * HEAD


def kernel_call(body, out_shape, in_specs, out_specs, scratch, flops, moved, args):
    return pl.pallas_call(
        body,
        out_shape=out_shape,
        in_specs=in_specs,
        out_specs=out_specs,
        scratch_shapes=scratch,
        compiler_params=pltpu.CompilerParams(vmem_limit_bytes=60 << 20),
        cost_estimate=pl.CostEstimate(flops=flops, bytes_accessed=moved, transcendentals=0),
    )(*args)


def load_rows(meta, places, lines, refs, target, sems, columns):
    copies = []
    if len(refs) == 1:
        copies.append(pltpu.make_async_copy(refs[0].at[:, columns], target, sems.at[0]))
    else:
        zi, qi, xi, ci, count = meta[0], meta[1], meta[2], meta[3], target.shape[0] // (4 * lines * refs[0].shape[1])
        for ref, (j, i, l, first) in zip(refs, places):
            blocks, share, _ = ref.shape
            q = lax.rem(qi + (lines - j), lines)
            x = lax.rem(xi + i, 2)
            c = lax.rem(ci + l, 2)
            for k in range(blocks):
                z = lax.rem(zi + (count - first - k), count) if len(refs) == 10 else first + k
                row = pl.multiple_of((((z * lines + q) * 2 + x) * 2 + c) * share, share)
                copies.append(
                    pltpu.make_async_copy(
                        ref.at[k, :, columns], target.at[pl.ds(row, share), :], sems.at[len(copies)]
                    )
                )
    for copy in copies:
        copy.start()
    return copies


def arrays_of(pieces):
    return [piece[0] for piece in pieces]


def places_of(pieces):
    return tuple(piece[1:] for piece in pieces)


def copies_of(pieces):
    count = 1 if len(pieces) == 1 else sum(piece[0].shape[0] for piece in pieces)
    return pltpu.SemaphoreType.DMA((count,))


def store_rows(meta, split, block, first, send, keep, columns):
    if not split:
        keep[pl.ds(first, block.shape[0]), columns] = block.astype(keep.dtype)
        return
    lines, share = keep.shape[0] // 2, keep.shape[2]
    qi, xi, ci = meta[1], meta[2], meta[3]
    for n in range(block.shape[0] // (2 * share)):
        chip = first // (2 * share) + n
        z, q, x = chip // (2 * lines), chip // 2 % lines, chip % 2
        j = lax.rem(qi + (lines - q), lines)
        i = lax.rem(xi + x, 2)
        even = block[2 * n * share : (2 * n + 1) * share]
        odd = block[(2 * n + 1) * share : (2 * n + 2) * share]
        keep[2 * j + i, z, :, columns] = jnp.where(ci == 0, even, odd).astype(keep.dtype)
        send[2 * j + i, z, :, columns] = jnp.where(ci == 0, odd, even).astype(send.dtype)


def sums_shapes(split, parts, rows, width):
    if not split:
        return (jax.ShapeDtypeStruct((8, 128), BF), jax.ShapeDtypeStruct((rows, width), BF))
    shape = (parts[1] * 2, parts[0], rows // (parts[0] * parts[1] * 4), width)
    return (jax.ShapeDtypeStruct(shape, BF), jax.ShapeDtypeStruct(shape, BF))


def turned_store(ref, row, lanes, block, cosine, sine):
    upper, lower = block[:HALF], block[HALF:]
    ref[pl.ds(row, HALF), lanes] = (upper * cosine - lower * sine).astype(ref.dtype)
    ref[pl.ds(row + HALF, HALF), lanes] = (lower * cosine + upper * sine).astype(ref.dtype)


def head_scores(queries, keys, place, wide):
    scores = mm(keys, queries) * SCALE
    rows = scores.shape[1] // GROUP
    key_place = lax.broadcasted_iota(jnp.int32, scores.shape, 0)
    query_place = place * rows + lax.rem(lax.broadcasted_iota(jnp.int32, scores.shape, 1), rows)
    return jnp.where(key_place <= query_place, scores, NEG)


def group_of(ref, g, lanes):
    return jnp.concatenate(
        [ref[pl.ds(pl.multiple_of((g * GROUP + j) * HEAD, 16), HEAD), lanes] for j in range(GROUP)],
        axis=1,
    )


def flip(value):
    return value.astype(F32).T.astype(value.dtype)


def project_forward_body(seqs, wide, places, lines, meta, tokens, cosine, sine, *refs):
    count = len(places)
    pieces, refs = refs[:count], refs[count:]
    (
        query_t, pair_t, normed_t, gains,
        pair_v, query_v, gains_v, normed, own, pair_sems, query_sems, gain_sems,
    ) = refs
    place = meta[0]
    rows = own.shape[0] // seqs
    pair_width = KV_HEADS * HEAD
    gain_copies = load_rows(meta, places, lines, pieces, gains_v, gain_sems, pl.ds(PAIR, 128))
    pair_copies = load_rows(meta, places, lines, pieces, pair_v, pair_sems, pl.ds(0, PAIR))
    query_copies = load_rows(meta, places, lines, pieces, query_v, query_sems, pl.ds(PAIR + 128, QUERY))
    for copy in gain_copies:
        copy.wait()
    gains[...] = gains_v[...].astype(F32).T[:8]
    gain = gains[0:1]
    for s in range(seqs):
        for z in range(wide // rows):
            cut = slice(s * wide + z * rows, s * wide + (z + 1) * rows)
            values = tokens[z, s].astype(F32)
            block = (values * inverse_rms(values) * gain).astype(BF)
            normed[cut, :] = block
            normed_t[:, cut] = flip(block)
    for s in range(seqs):
        own[s * rows : (s + 1) * rows, :] = normed[
            pl.ds(pl.multiple_of(s * wide + place * rows, 128), rows), :
        ]
    for copy in pair_copies:
        copy.wait()
    heads = 8
    width = heads * HEAD
    for n in range(2 * pair_width // width):
        for s in range(seqs):
            lanes = slice(s * wide, (s + 1) * wide)
            block = mm(normed[lanes, :], pair_v[:, n * width : (n + 1) * width]).T
            if (n + 1) * width <= pair_width:
                for h in range(heads):
                    turned_store(
                        pair_t, n * width + h * HEAD, lanes, block[h * HEAD : (h + 1) * HEAD],
                        cosine[:, lanes], sine[:, lanes],
                    )
            else:
                pair_t[n * width : (n + 1) * width, lanes] = block.astype(BF)
    for copy in query_copies:
        copy.wait()
    for n in range(HEADS * HEAD // width):
        block = mm(own[...], query_v[:, n * width : (n + 1) * width]).T
        for s in range(seqs):
            lanes = slice(s * rows, (s + 1) * rows)
            here = pl.ds(pl.multiple_of(s * wide + place * rows, 128), rows)
            for h in range(heads):
                turned_store(
                    query_t, n * width + h * HEAD, lanes, block[h * HEAD : (h + 1) * HEAD, lanes],
                    cosine[:, here], sine[:, here],
                )


def attend_forward_body(seqs, wide, meta, query_t, pair_t, mixed, mixed_t, logs):
    place = meta[0]
    rows = query_t.shape[1] // seqs
    pair_width = KV_HEADS * HEAD

    def one(g, _):
        row = pl.multiple_of(g * HEAD, 16)
        for s in range(seqs):
            lanes = slice(s * wide, (s + 1) * wide)
            mine = slice(s * rows, (s + 1) * rows)
            scores = head_scores(
                group_of(query_t, g, mine), flip(pair_t[pl.ds(row, HEAD), lanes]), place, wide
            )
            top = jnp.max(scores, axis=0, keepdims=True)
            weights = jnp.exp(scores - top)
            total = jnp.sum(weights, axis=0, keepdims=True)
            probs = (weights * (1.0 / total)).astype(BF)
            out = mm(pair_t[pl.ds(row + pair_width, HEAD), lanes], probs).astype(BF)
            for j in range(GROUP):
                mixed_t[pl.ds(pl.multiple_of((g * GROUP + j) * HEAD, 16), HEAD), mine] = out[
                    :, j * rows : (j + 1) * rows
                ]
            logs[g, s] = top + jnp.log(total)
        return 0

    lax.fori_loop(0, KV_HEADS, one, 0)
    mixed[...] = flip(mixed_t[...])


def project_forward(meta, tokens, cosine, sine, pieces, lines, width, seqs, rows):
    wide = tokens.shape[0] * rows
    count, own = seqs * wide, seqs * rows
    sds = jax.ShapeDtypeStruct
    return kernel_call(
        functools.partial(project_forward_body, seqs, wide, places_of(pieces), lines),
        (sds((QUERY, own), BF), sds((PAIR, count), BF), sds((width, count), BF), sds((8, width), F32)),
        [SMEM, VMEM, VMEM, VMEM] + [ANY] * len(pieces),
        (VMEM,) * 4,
        [
            pltpu.VMEM((width, PAIR), BF), pltpu.VMEM((width, QUERY), BF), pltpu.VMEM((width, 128), BF),
            pltpu.VMEM((count, width), BF), pltpu.VMEM((own, width), BF),
            copies_of(pieces), copies_of(pieces), copies_of(pieces),
        ],
        2 * count * width * PAIR + 2 * own * width * QUERY,
        20 << 20,
        (meta, tokens, cosine, sine, *arrays_of(pieces)),
    )


def attend_forward(meta, query_t, pair_t, seqs):
    own = query_t.shape[1]
    wide = pair_t.shape[1] // seqs
    sds = jax.ShapeDtypeStruct
    return kernel_call(
        functools.partial(attend_forward_body, seqs, wide),
        (
            sds((own, QUERY), BF), sds((QUERY, own), BF),
            sds((KV_HEADS, seqs, 1, GROUP * own // seqs), F32),
        ),
        [SMEM, VMEM, VMEM],
        (VMEM,) * 3,
        [],
        4 * own * wide * QUERY,
        6 << 20,
        (meta, query_t, pair_t),
    )


def attend_backward_body(
    seqs, wide, meta, query_t, pair_t, grad_t, logs, cosine, sine, query_back, pair_back, pair_blocks
):
    place = meta[0]
    rows = query_t.shape[1] // seqs
    pair_width = KV_HEADS * HEAD

    def one(g, _):
        row = pl.multiple_of(g * HEAD, 16)
        for s in range(seqs):
            lanes = slice(s * wide, (s + 1) * wide)
            mine = slice(s * rows, (s + 1) * rows)
            here = pl.ds(pl.multiple_of(s * wide + place * rows, 128), rows)
            queries = group_of(query_t, g, mine)
            grads = group_of(grad_t, g, mine)
            keys_t = pair_t[pl.ds(row, HEAD), lanes]
            values_t = pair_t[pl.ds(row + pair_width, HEAD), lanes]
            probs = jnp.exp(head_scores(queries, flip(keys_t), place, wide) - logs[g, s])
            prob_grad = mm(flip(values_t), grads)
            centre = jnp.sum(probs * prob_grad, axis=0, keepdims=True)
            score_grad = (probs * (prob_grad - centre)).astype(BF)
            query_grad = mm(keys_t, score_grad) * SCALE
            for j in range(GROUP):
                turned_store(
                    query_back, pl.multiple_of((g * GROUP + j) * HEAD, 16), mine,
                    query_grad[:, j * rows : (j + 1) * rows], cosine[:, here], -sine[:, here],
                )
            turned_store(
                pair_back, row, lanes, mm_t(queries, score_grad) * SCALE,
                cosine[:, lanes], -sine[:, lanes],
            )
            pair_back[pl.ds(row + pair_width, HEAD), lanes] = mm_t(
                grads, probs.astype(BF)
            ).astype(BF)
            for z in range(wide // rows):
                from_z = slice(s * wide + z * rows, s * wide + (z + 1) * rows)
                for first in (row, row + pair_width):
                    pair_blocks[z, pl.ds(first, HEAD), mine] = pair_back[pl.ds(first, HEAD), from_z]
        return 0

    lax.fori_loop(0, KV_HEADS, one, 0)


def attend_backward(meta, query_t, pair_t, grad_t, logs, cosine, sine, seqs):
    wide = pair_t.shape[1] // seqs
    return kernel_call(
        functools.partial(attend_backward_body, seqs, wide),
        (
            jax.ShapeDtypeStruct(query_t.shape, BF),
            jax.ShapeDtypeStruct(pair_t.shape, BF),
            jax.ShapeDtypeStruct((pair_t.shape[1] // query_t.shape[1], PAIR, query_t.shape[1]), BF),
        ),
        [SMEM] + [VMEM] * 6,
        (VMEM,) * 3,
        [],
        10**12,
        12 << 20,
        (meta, query_t, pair_t, grad_t, logs, cosine, sine),
    )


def output_body(places, lines, meta, tokens, mixed, gain, *refs):
    pieces, (total, second, weights_v, sems) = refs[:-4], refs[-4:]
    for copy in load_rows(meta, places, lines, pieces, weights_v, sems, pl.ds(0, weights_v.shape[1])):
        copy.wait()
    value = tokens[...].astype(F32) + mm(mixed[...], weights_v[...])
    total[...] = value
    second[...] = (value * inverse_rms(value) * gain[1:2]).astype(BF)


def output_forward(meta, tokens, mixed, gain, pieces, lines):
    return kernel_call(
        functools.partial(output_body, places_of(pieces), lines),
        (jax.ShapeDtypeStruct(tokens.shape, F32), jax.ShapeDtypeStruct(tokens.shape, BF)),
        [SMEM, VMEM, VMEM, VMEM] + [ANY] * len(pieces),
        (VMEM, VMEM),
        [pltpu.VMEM((QUERY, tokens.shape[1]), BF), copies_of(pieces)],
        2 * tokens.size * QUERY,
        10 << 20,
        (meta, tokens, mixed, gain, *arrays_of(pieces)),
    )


def output_back_body(split, grad, total, second_grad, gain, mixed_t, meta, first_grad, da, send, keep):
    value = total[...]
    inverse = inverse_rms(value)
    back = second_grad[...]
    scaled = back * gain[1:2]
    first = (
        grad[...].astype(F32)
        + inverse * scaled
        - value * inverse**3 * jnp.mean(scaled * value, axis=-1, keepdims=True)
    )
    first_grad[...] = first
    da[...] = first.astype(BF)
    width = value.shape[1]
    gain_part = jnp.broadcast_to(
        jnp.sum((back * value * inverse).T, axis=1, keepdims=True), (width, 128)
    )
    store_rows(meta, split, gain_part, 0, send, keep, pl.ds(width, 128))
    step = 384
    for n in range(width // step):
        cut = slice(n * step, (n + 1) * step)
        store_rows(meta, split, mm(mixed_t[cut, :], da[...]), n * step, send, keep, pl.ds(0, width))


def output_backward(grad, total, second_grad, gain, mixed_t, meta, parts, split):
    own, width = grad.shape
    return kernel_call(
        functools.partial(output_back_body, split),
        (
            jax.ShapeDtypeStruct((own, width), F32),
            jax.ShapeDtypeStruct((own, width), BF),
            *sums_shapes(split, parts, QUERY, width + 128),
        ),
        [VMEM] * 5 + [SMEM],
        (VMEM,) * 4,
        [],
        2 * own * width * QUERY,
        14 << 20,
        (grad, total, second_grad, gain, mixed_t, meta),
    )


def mixed_back_body(places, lines, meta, da, *refs):
    pieces, (mixed_grad_t, weights_v, sems) = refs[:-3], refs[-3:]
    for copy in load_rows(meta, places, lines, pieces, weights_v, sems, pl.ds(0, weights_v.shape[1])):
        copy.wait()
    step = 384
    for n in range(weights_v.shape[0] // step):
        cut = slice(n * step, (n + 1) * step)
        mixed_grad_t[cut, :] = mm_t(weights_v[cut, :], da[...]).astype(BF)


def mixed_backward(meta, da, pieces, lines):
    own, width = da.shape
    return kernel_call(
        functools.partial(mixed_back_body, places_of(pieces), lines),
        jax.ShapeDtypeStruct((QUERY, own), BF),
        [SMEM, VMEM] + [ANY] * len(pieces),
        VMEM,
        [pltpu.VMEM((QUERY, width), BF), copies_of(pieces)],
        10**12,
        8 << 20,
        (meta, da, *arrays_of(pieces)),
    )


def ffn_body(count, *refs):
    second, grads, shards = refs[:count], refs[count : 2 * count], refs[2 * count]
    out_a, out_b, *backs, sums = refs[2 * count + 1 : 3 * count + 4]
    (
        second_v, grads_v, weights, hidden, gate_g, up_g, hidden_t, gate_t, up_t, sums_v, sems, row_sems, sum_sem,
    ) = refs[3 * count + 4 :]
    rows = second[0].shape[0]
    blocks, units = shards.shape[0], shards.shape[1] // 3
    weight_copies = [
        pltpu.make_async_copy(
            shards.at[b, pl.ds(p * units, units)], weights.at[p, pl.ds(b * units, units)], sems.at[p, b]
        )
        for p in range(3)
        for b in range(blocks)
    ]
    for copy in weight_copies:
        copy.start()
    for i in range(count):
        cut = pl.ds(i * rows, rows)
        pltpu.make_async_copy(second[i], second_v.at[cut], sems.at[3, i]).start()
        pltpu.make_async_copy(grads[i], grads_v.at[cut], sems.at[4, i]).start()
    for copy in weight_copies:
        copy.wait()
    per = 2
    step = per * rows

    def one(m, _):
        here = pl.ds(pl.multiple_of(m * step, step), step)
        for i in range(per):
            cut = pl.ds(pl.multiple_of((m * per + i) * rows, rows), rows)
            pltpu.make_async_copy(second_v.at[cut], second_v.at[cut], sems.at[3, m * per + i]).wait()
            pltpu.make_async_copy(grads_v.at[cut], grads_v.at[cut], sems.at[4, m * per + i]).wait()
        gate = mm_t(second_v[here, :], weights[0])
        up = mm_t(second_v[here, :], weights[1])
        hidden_grad = mm_t(grads_v[here, :], weights[2])
        sigma = jax.nn.sigmoid(gate)
        silu = gate * sigma
        mixed = silu * up
        hidden[here, :] = mixed.astype(BF)
        hidden_t[:, here] = mixed.T.astype(BF)
        gate_grad = hidden_grad * up * (sigma + silu * (1.0 - sigma))
        gate_g[here, :] = gate_grad.astype(BF)
        gate_t[:, here] = gate_grad.T.astype(BF)
        up_grad = hidden_grad * silu
        up_g[here, :] = up_grad.astype(BF)
        up_t[:, here] = up_grad.T.astype(BF)
        return 0

    lax.fori_loop(0, count // per, one, 0)

    width = second_v.shape[1]
    for n, (left, right) in enumerate(((gate_t, second_v), (up_t, second_v), (hidden_t, grads_v))):
        for c in range(width // step):
            cut = slice(c * step, (c + 1) * step)
            part = mm(left[...], right[:, cut]).astype(BF)
            for b in range(blocks):
                sums_v[b, n * units : (n + 1) * units, cut] = part[b * units : (b + 1) * units]
    sum_copy = pltpu.make_async_copy(sums_v, sums, sum_sem)
    sum_copy.start()

    half = count * rows // 2
    copies = []
    for n, (kind, first) in enumerate((("b", half), ("b", 0), ("o", half), ("o", 0))):
        place = second_v if kind == "b" else grads_v
        for k in range(half // step):
            here = slice(first + k * step, first + (k + 1) * step)
            if kind == "b":
                value = mm(gate_g[here, :], weights[0]) + mm(up_g[here, :], weights[1])
            else:
                value = mm(hidden[here, :], weights[2])
            place[here, :] = value.astype(BF)
            for i in range(per):
                row = first + k * step + i * rows
                if kind == "b":
                    target = backs[row // rows]
                else:
                    target = (out_b if first else out_a).at[pl.ds(row - first, rows)]
                copies.append(
                    pltpu.make_async_copy(
                        place.at[pl.ds(row, rows)], target, row_sems.at[n, k * per + i]
                    )
                )
                copies[-1].start()
    sum_copy.wait()
    for copy in copies:
        copy.wait()


def ffn(tokens_of, weights):
    pieces = len(tokens_of) // 2
    rows, width = tokens_of[0].shape
    count, total = pieces * rows, weights.shape[0] * weights.shape[1] // 3
    sds = jax.ShapeDtypeStruct
    return kernel_call(
        functools.partial(ffn_body, pieces),
        (sds((count // 2, width), BF),) * 2 + (sds((rows, width), BF),) * pieces + (sds(weights.shape, BF),),
        [ANY] * (2 * pieces + 1),
        (ANY,) * (pieces + 3),
        [
            pltpu.VMEM((count, width), BF), pltpu.VMEM((count, width), BF),
            pltpu.VMEM((3, total, width), BF),
            pltpu.VMEM((count, total), BF), pltpu.VMEM((count, total), BF), pltpu.VMEM((count, total), BF),
            pltpu.VMEM((total, count), BF), pltpu.VMEM((total, count), BF), pltpu.VMEM((total, count), BF),
            pltpu.VMEM(weights.shape, BF),
            pltpu.SemaphoreType.DMA((5, max(weights.shape[0], pieces))),
            pltpu.SemaphoreType.DMA((4, pieces // 2)),
            pltpu.SemaphoreType.DMA,
        ],
        18 * count * total * width,
        34 << 20,
        (*tokens_of, weights),
    )


def project_sums_body(
    seqs, split, meta, normed_t, query_back, pair_back, pair_send, pair_keep, query_send, query_keep
):
    place = meta[0]
    wide = normed_t.shape[1] // seqs
    rows = query_back.shape[1] // seqs
    step = 384
    for n in range(normed_t.shape[0] // step):
        cut = slice(n * step, (n + 1) * step)
        own = jnp.concatenate(
            [normed_t[cut, pl.ds(pl.multiple_of(s * wide + place * rows, 128), rows)] for s in range(seqs)],
            axis=1,
        )
        store_rows(
            meta, split, mm_t(own, query_back[...]), n * step, query_send, query_keep, pl.ds(0, QUERY)
        )
        store_rows(
            meta, split, mm_t(normed_t[cut, :], pair_back[...]), n * step, pair_send, pair_keep, pl.ds(0, PAIR)
        )


def project_sums(meta, normed_t, query_back, pair_back, seqs, parts, split):
    width = normed_t.shape[0]
    return kernel_call(
        functools.partial(project_sums_body, seqs, split),
        (*sums_shapes(split, parts, width, PAIR), *sums_shapes(split, parts, width, QUERY)),
        [SMEM, VMEM, VMEM, VMEM],
        (VMEM,) * 4,
        [],
        1,
        26 << 20,
        (meta, normed_t, query_back, pair_back),
    )


def input_grad_body(places, lines, meta, tokens, gain, first_grad, query_back, pair_back, *refs):
    pieces, (out, pair_v, query_v, pair_sems, query_sems) = refs[: len(places)], refs[len(places) :]
    query_copies = load_rows(meta, places, lines, pieces, query_v, query_sems, pl.ds(PAIR + 128, QUERY))
    pair_copies = load_rows(meta, places, lines, pieces, pair_v, pair_sems, pl.ds(0, PAIR))
    for copy in query_copies:
        copy.wait()
    back = mm(query_v[...], query_back[...])
    for copy in pair_copies:
        copy.wait()
    back = (back + mm(pair_v[...], pair_back[...])).T
    value = tokens[...].astype(F32)
    inverse = inverse_rms(value)
    scaled = back * gain[0:1]
    out[...] = (
        first_grad[...]
        + inverse * scaled
        - value * inverse**3 * jnp.mean(scaled * value, axis=-1, keepdims=True)
    ).astype(BF)


def input_grad(meta, tokens, gain, first_grad, query_back, pair_back, pieces, lines):
    width = tokens.shape[1]
    return kernel_call(
        functools.partial(input_grad_body, places_of(pieces), lines),
        jax.ShapeDtypeStruct(tokens.shape, BF),
        [SMEM] + [VMEM] * 5 + [ANY] * len(pieces),
        VMEM,
        [
            pltpu.VMEM((width, PAIR), BF), pltpu.VMEM((width, QUERY), BF), copies_of(pieces), copies_of(pieces),
        ],
        2 * width * (query_back.size + pair_back.size),
        14 << 20,
        (meta, tokens, gain, first_grad, query_back, pair_back, *arrays_of(pieces)),
    )


def per_device(
    tokens,
    positions,
    out_grad,
    w_query,
    w_key,
    w_value,
    w_output,
    gain_attn,
    gain_ffn,
    w_gate,
    w_up,
    w_down,
):
    move = Moves()
    Z, Q, step = move.Z, move.Q, move.step
    seqs, rows, width = tokens.shape
    wide = rows * Z
    own_rows = seqs * rows
    pair_width = KV_HEADS * HEAD
    share, units = w_query.shape[0], w_gate.shape[0]
    split = share % 16 == 0
    meta = jnp.stack([move.zi, move.qi, move.xi, move.ci]).astype(jnp.int32)
    near = [(j, i) for j in range(Q) for i in range(2)]
    rounds = (Z, Q) == (4, 2)
    grad_out = out_grad.reshape(own_rows, width)
    inputs = tokens.reshape(own_rows, width)

    always = lax.optimization_barrier(jnp.ones((), jnp.bool_))

    def window(body, *operands):
        shapes = jax.eval_shape(body, *operands)
        return lax.cond(
            always,
            body,
            lambda *_: jax.tree.map(lambda s: jnp.zeros(s.shape, s.dtype), shapes),
            *operands,
        )

    def over_z(value):
        return lax.all_gather(value, "seq", axis=0, tiled=False)

    def sum_z(value):
        return lax.psum_scatter(value, "seq", scatter_dimension=0, tiled=False)

    columns = -(-own_rows // share)
    spots = jnp.pad(positions.reshape(own_rows), (0, columns * share - own_rows)).reshape(share, columns)
    gains_in = jnp.concatenate(
        [gain_attn[:, None], gain_ffn[:, None], (spots // 256).astype(BF), (spots % 256).astype(BF)], axis=1
    )
    gains_in = jnp.pad(gains_in, ((0, 0), (0, 126 - 2 * columns)))
    pack0 = jnp.concatenate([w_key, w_value, gains_in, w_query], axis=1)
    ffn_in = jnp.concatenate([w_gate, w_up, w_down], axis=0)
    half = len(near)

    def spread(value):
        return tuple(step((j, i), value) if j or i else value for j, i in near)

    def cores(pieces):
        return tuple(pieces) + tuple(step("c", piece) for piece in pieces)

    def to_send(own, other):
        return [(in_f32(own[n]) + in_f32(other[n])).astype(BF) for n in range(1, half)]

    def halves(parts):
        return [part.reshape(half, own_rows, width) for part in parts]

    def blocks_to(blocks, *held):
        return [after(step((-j % Q, i), block), *held) for block, (j, i) in zip(blocks, near[1:])]

    def total(first, parts):
        for part in parts:
            first = first + in_f32(part)
        return first

    def chips_of(rows):
        return [(step((j, i), rows) if j or i else rows, j, i, 0) for j, i in near]

    def everywhere(chips):
        found = []
        for array, j, i, z in chips:
            found += [(array, j, i, 0, z), (step("c", array), j, i, 1, z)]
        if split:
            return found
        rows = found[0][0]
        whole = jnp.zeros((Z, Q, 2, 2) + rows.shape[1:], BF)
        for array, j, i, l, z in found:
            for k in range(array.shape[0]):
                at = (z + k, (move.qi - j) % Q, (move.xi + i) % 2, (move.ci + l) % 2, 0, 0)
                whole = lax.dynamic_update_slice(whole, array[k][None, None, None, None], at)
        return [(whole.reshape(-1, rows.shape[-1]), 0, 0, 0, 0)]

    if rounds:
        def round0(pack0, grad_out):
            return (
                move.around(1, pack0), move.around(-1, pack0), step((0, 1), grad_out), step((1, 0), grad_out)
            )

        up, down, grad_x, grad_q = window(round0, pack0, grad_out)
        carried, ffn_in, up, down = lax.optimization_barrier((tokens, ffn_in, up, down))
        tokens_all = over_z(carried)
        ffn_w = over_z(ffn_in)

        def round1(pack0, up, down, grad_x, grad_q):
            middle = own_rows // 2
            far = move.around(1, up)
            corner = step((0, 1), grad_q[:middle]), step((1, 0), grad_x[middle:])
            return jnp.stack([pack0, up, far, down]), jnp.concatenate(corner)

        pack, grad_xq = window(round1, pack0, up, down, grad_x, grad_q)
        grad_spread = (grad_out, grad_x, grad_q, grad_xq)

        def round2(pack, output0):
            return (
                step((0, 1), pack), step((1, 0), pack), step("c", pack),
                move.around(1, output0), move.around(-1, output0),
            )

        at_x, at_q, pack_c, output1, output3 = window(round2, pack, w_output)

        def round3(at_x, at_q, output0, output1, output3):
            corner = step((0, 1), at_q[:2]), step((1, 0), at_x[2:])
            cores_of = step("c", at_x), step("c", at_q)
            output2 = move.around(1, output1)
            return corner + cores_of + (jnp.stack([output0, output1, output2, output3]),)

        corner_a, corner_b, at_xc, at_qc, out_pack = window(
            round3, at_x, at_q, w_output, output1, output3
        )
        pieces = [
            (pack, 0, 0, 0, 0), (pack_c, 0, 0, 1, 0), (at_x, 0, 1, 0, 0), (at_xc, 0, 1, 1, 0),
            (at_q, 1, 0, 0, 0), (at_qc, 1, 0, 1, 0),
            (corner_a, 1, 1, 0, 0), (step("c", corner_a), 1, 1, 1, 0),
            (corner_b, 1, 1, 0, 2), (step("c", corner_b), 1, 1, 1, 2),
        ]
    else:
        tokens_all = over_z(tokens)
        pack = over_z(pack0)
        grad_spread = spread(grad_out)
        ffn_w = over_z(ffn_in)
        out_pack = over_z(w_output)
        pieces = everywhere(chips_of(pack))

    spots = in_f32(pack[:, :, 2 * pair_width + 2 : 2 * pair_width + 2 + 2 * columns])
    spots = (spots[..., :columns] * 256 + spots[..., columns:]).reshape(Z, -1)[:, :own_rows]
    if rounds:
        order = (move.zi - jnp.arange(Z)) % Z
        spots = jnp.sum(jnp.where((order[:, None] == jnp.arange(Z)[None])[..., None], spots[None], 0), axis=1)
    cosine, sine = angle_tables(
        spots.reshape(Z, seqs, rows).transpose(1, 0, 2).reshape(seqs * wide)
    )

    if rounds:

        def round4(meta, cosine, sine, out_pack, tokens_all, arrays):
            moved = step((0, 1), out_pack), step((1, 0), out_pack), step("c", out_pack)
            found = [(array,) + piece[1:] for array, piece in zip(arrays, pieces)]
            return moved + tuple(
                project_forward(meta, tokens_all, cosine, sine, found, Q, width, seqs, rows)
            )

        out_x, out_q, out_packc, query_t, pair_t, normed_t, gains = window(
            round4, meta, cosine, sine, out_pack, tokens_all, arrays_of(pieces)
        )

        def round5(meta, query_t, pair_t, out_x, out_q):
            corner = step((0, 1), out_q[:2]), step((1, 0), out_x[2:])
            cores_of = step("c", out_x), step("c", out_q)
            return corner + cores_of + tuple(attend_forward(meta, query_t, pair_t, seqs))

        corner_a, corner_b, out_xc, out_qc, mixed, mixed_t, logs = window(
            round5, meta, query_t, pair_t, out_x, out_q
        )
        out_pieces = [
            (out_pack, 0, 0, 0, 0), (out_packc, 0, 0, 1, 0), (out_x, 0, 1, 0, 0), (out_xc, 0, 1, 1, 0),
            (out_q, 1, 0, 0, 0), (out_qc, 1, 0, 1, 0),
            (corner_a, 1, 1, 0, 0), (step("c", corner_a), 1, 1, 1, 0),
            (corner_b, 1, 1, 0, 2), (step("c", corner_b), 1, 1, 1, 2),
        ]
    else:
        query_t, pair_t, normed_t, gains = project_forward(
            meta, tokens_all, cosine, sine, pieces, Q, width, seqs, rows
        )
        mixed, mixed_t, logs = attend_forward(meta, query_t, pair_t, seqs)
        out_pieces = everywhere(chips_of(out_pack))
    first_sum, second = output_forward(meta, inputs, mixed, gains, out_pieces, Q)
    grad_spread = cores(tuple(after(piece, mixed) for piece in grad_spread))

    second_spread = cores(spread(second))
    outs, backs, ffn_sum = [], [], None
    for n in range(0, 2 * half, 8):
        out_a, out_b, *parts, sums = ffn(second_spread[n : n + 8] + grad_spread[n : n + 8], ffn_w)
        outs += [out_a, out_b]
        backs += parts
        ffn_sum = sums if ffn_sum is None else in_f32(ffn_sum) + in_f32(sums)
    if len(outs) > 2:
        outs = (jnp.concatenate(outs[: len(outs) // 2]), jnp.concatenate(outs[len(outs) // 2 :]))
    grad_ffn = sum_z(ffn_sum.astype(BF))
    back, other = backs[:half], [step("c", part) for part in backs[half:]]
    second_grad = total(in_f32(back[0]) + in_f32(other[0]), blocks_to(to_send(back, other)))

    def pieces_for(send, keep):
        if split:
            return send, keep
        value = keep.reshape(Z, Q, 2, 2, share, keep.shape[-1])

        def cut(c):
            return jnp.stack(
                [
                    lax.dynamic_slice(
                        value,
                        (0, (move.qi - j) % Q, (move.xi + i) % 2, c, 0, 0),
                        (Z, 1, 1, 1, share, keep.shape[-1]),
                    )[:, 0, 0, 0]
                    for j, i in near
                ]
            )

        return cut(1 - move.ci), cut(move.ci)

    first_grad, rounded, out_send, out_keep = output_backward(
        grad_out, first_sum, second_grad, gains, mixed_t, meta, (Z, Q), split
    )
    out_send, out_keep = pieces_for(out_send, out_keep)
    moving = step("c", out_send)
    mixed_grad_t = mixed_backward(meta, rounded, out_pieces, Q)
    out_send, mixed_grad_t = lax.optimization_barrier((moving, mixed_grad_t))
    blocks = to_send(out_keep, out_send)

    def attention_beside(first, second, blocks, meta, query_t, pair_t, mixed_grad_t, logs, cosine, sine, normed_t, out):
        moved, out = blocks_to(blocks), step("c", out)
        query_back, pair_back, pair_blocks = attend_backward(
            meta, query_t, pair_t, mixed_grad_t, logs, cosine, sine, seqs
        )
        sums = project_sums(meta, normed_t, query_back, pair_back, seqs, (Z, Q), split)
        sums, moved, out = lax.optimization_barrier((tuple(sums), moved, out))
        out_rows = total(in_f32(first) + in_f32(second), moved).astype(BF)
        return out_rows, query_back, pair_blocks, sums, out

    out_rows, query_back, pair_blocks, sums, out_other = window(
        attention_beside, out_keep[0], out_send[0], blocks, meta, query_t, pair_t, mixed_grad_t, logs,
        cosine, sine, normed_t, outs[1],
    )
    grad_ffn, pair_blocks = lax.optimization_barrier((grad_ffn, pair_blocks))
    pair_own = sum_z(pair_blocks)
    pair_send, pair_keep = pieces_for(*sums[:2])
    query_send, query_keep = pieces_for(*sums[2:])
    pair_send, query_send = step("c", pair_send), step("c", query_send)
    pair_blocks_out = blocks_to(to_send(pair_keep, pair_send))
    query_blocks_out = blocks_to(to_send(query_keep, query_send))
    pair_rows = total(in_f32(pair_keep[0]) + in_f32(pair_send[0]), pair_blocks_out).astype(BF)
    query_rows = total(in_f32(query_keep[0]) + in_f32(query_send[0]), query_blocks_out).astype(BF)
    rows_of = jnp.concatenate([pair_rows, query_rows], axis=-1)
    out, out_other = halves((outs[0], out_other))
    blocks = [after(block, rows_of) for block in to_send(out, out_other)]
    rows_of, pair_own = lax.optimization_barrier((jnp.concatenate([rows_of, out_rows], axis=-1), pair_own))
    sums = in_f32(sum_z(rows_of))
    in_grad = input_grad(meta, inputs, gains, first_grad, query_back, pair_own, pieces, Q)
    layer = total(first_sum + in_f32(out[0]) + in_f32(out_other[0]), blocks_to(blocks, in_grad))
    layer_out = layer.astype(BF)
    grad_ffn = in_f32(grad_ffn)
    grad_gate, grad_up, grad_down = grad_ffn[:units], grad_ffn[units : 2 * units], grad_ffn[2 * units :]

    grad_key, grad_value = sums[:, :pair_width], sums[:, pair_width : 2 * pair_width]
    grad_query = sums[:, 2 * pair_width : 2 * pair_width + QUERY]
    output_sum = sums[:, 2 * pair_width + QUERY :]
    grad_output, grad_gain_ffn = output_sum[:, :width], output_sum[:, width]
    grad_gain_attn = (
        jnp.sum(grad_query * in_f32(w_query), axis=1)
        + jnp.sum(grad_key * in_f32(w_key), axis=1)
        + jnp.sum(grad_value * in_f32(w_value), axis=1)
    ) / in_f32(gain_attn)
    return (
        layer_out.reshape(seqs, rows, width),
        in_grad.reshape(seqs, rows, width),
        grad_query,
        grad_key,
        grad_value,
        grad_output,
        grad_gain_attn,
        grad_gain_ffn,
        grad_gate,
        grad_up,
        grad_down,
    )


def solution(mesh):
    rows = P(("seq", "dp"), None)
    vector = P(("seq", "dp"))
    act = P("dp", "seq", None)
    return jax.shard_map(
        per_device,
        mesh=mesh,
        in_specs=(act, P("dp", "seq"), act, rows, rows, rows, rows, vector, vector, rows, rows, rows),
        out_specs=(act, act, rows, rows, rows, rows, vector, vector, rows, rows, rows),
        check_vma=False,
    )
```
